32 devices in a mesh: cell: 16 (over z, y, core), inst: 2 (over x).
Axes of the slice: x: 2, y: 2, z: 4, core: 2. Of those that a mesh axis runs over, the one named last changes fastest.
Arguments:
- initial: float32 [80, 32768], P('inst', 'cell'), may hold values from -6 to 6
- source: float32 [80, 32768], P('inst', 'cell'), may hold values from -6 to 6
- neighbors: int32 [4, 32768], P(None, 'cell'), may hold values from -256 to 256, as said below
- face_weights: float32 [4, 32768], P(None, 'cell'), may hold values from 0.25 to 1
- damping: float32 [32768], P('cell'), may hold values from 0.5 to 2
Outputs:
- solution: float32 [80, 32768], P('inst', 'cell')
The draws below stay inside these ranges and needn't reach their ends.
Inputs may be any that keep to these rules, and one draw needn't show every extreme that they name: `neighbors`: entries 0 and 2 of a cell's offsets are at or below zero, entries 1 and 3 at or above zero; a cell plus each of its offsets is a cell of the grid; in every draw some offsets are exactly -256 and exactly 256.
All inputs are finite; a program needn't handle non-finite values.
Results may differ from the reference program's by a relative error of at most 0.0001.
Values sent between devices are 32-bit elements; how exact they have to be, the bound alone decides.
No kernel may reach another device: no remote copies, remote signals or barrier semaphores. Data moves between devices by JAX's collectives and lax.ppermute only.
A program may use at most 64 MiB of HBM per device.

```python
import math
import jax
import jax.numpy as jnp
from jax import lax

NI = 16
NC = 4
COMP = 5
NEIGH = 4
SWEEPS_FINE = 2
SWEEPS_COARSE = 3
PLANE = 256
NCELLS = 32768


def draw_neighbors(key, part):
    number = jnp.arange(NCELLS, dtype=jnp.int32)
    key_near, key_far = jax.random.split(jax.random.fold_in(key, 17))
    near = jax.random.randint(key_near, (2, NCELLS), 1, 9, dtype=jnp.int32)
    far = PLANE - jax.random.randint(key_far, (2, NCELLS), 0, max(PLANE // 2, 1), dtype=jnp.int32)
    far = jnp.where((number % 4 == 0)[None, :], PLANE, far)
    offsets = jnp.stack([-near[0], near[1], -far[0], far[1]])
    target = jnp.clip(number[None, :] + offsets, 0, NCELLS - 1)
    return (target - number[None, :]).astype(jnp.int32)


def level_of(key, dims, shards, smallest, top_value):
    loudness, own = 1.0, jax.random.fold_in(key, 6)
    for dim, parts in shards:
        steps = jnp.exp(jax.random.uniform(jax.random.fold_in(own, dim), (parts,), jnp.float32, smallest / len(shards), top_value / len(shards)))
        loudness = loudness * jnp.repeat(steps, dims[dim] // parts).reshape([-1 if axis == dim else 1 for axis in range(len(dims))])
    return loudness


def noise(stream_key, shape, scale, most, cuts=(), kind=jnp.bfloat16):
    level = level_of(stream_key, shape, cuts, -0.22, 0.18) if cuts else 1.0
    entries = jax.random.normal(stream_key, shape, jnp.float32) * scale * level
    return jnp.minimum(jnp.maximum(entries, -most), most).astype(kind)


def setup_inputs(seed: int = 0) -> dict:
    splits = jax.random.split(jax.random.key(seed), 6)
    return {
        "initial": noise(splits[0], (NI * COMP, NCELLS), 1.0, 6.0, ((0, 2), (1, 16)), jnp.float32),
        "source": noise(splits[1], (NI * COMP, NCELLS), 1.0, 6.0, ((0, 2), (1, 16)), jnp.float32),
        "neighbors": draw_neighbors(jax.random.fold_in(splits[5], 71), 0),
        "face_weights": jnp.clip(jnp.exp(math.log(1.0) - 1.3862944 * jax.random.uniform(splits[3], (NEIGH, NCELLS), jnp.float32) ** level_of(splits[3], (NEIGH, NCELLS), ((1, 16),), -0.2, 0.2)), 0.25, 1.0),
        "damping": jnp.clip(jnp.exp(math.log(2.0) - 1.3862944 * jax.random.uniform(splits[4], (NCELLS,), jnp.float32) ** level_of(splits[4], (NCELLS,), ((0, 16),), -0.2, 0.2)), 0.5, 2.0),
    }


FREQ = 0.15
RELAX = 0.6


def spectral_matrix(points):
    steps = jnp.arange(points, dtype=jnp.float32)
    offset = steps[:, None] - steps[None, :]
    parity = 1.0 - 2.0 * jnp.mod(offset, 2.0)
    angle = jnp.where(offset == 0, 0.5, jnp.pi * offset / points)
    return jnp.where(offset == 0, 0.0, 0.5 * parity / jnp.tan(angle))


def restrict_matrix():
    coarse_t = jnp.arange(NC, dtype=jnp.float32) / NC
    fine_t = jnp.arange(NI, dtype=jnp.float32) / NI
    return (1.0 + 2.0 * jnp.cos(2.0 * jnp.pi * (coarse_t[:, None] - fine_t[None, :]))) / NI


def prolong_matrix():
    coarse_t = jnp.arange(NC, dtype=jnp.float32) / NC
    fine_t = jnp.arange(NI, dtype=jnp.float32) / NI
    return (1.0 + 2.0 * jnp.cos(2.0 * jnp.pi * (fine_t[:, None] - coarse_t[None, :]))) / NC


def neighbour_terms(values, neighbors, face_weights):
    number = jnp.arange(values.shape[1], dtype=jnp.int32)
    summed = jnp.zeros(values.shape, jnp.float32)
    for slot in range(NEIGH):
        target = (number + neighbors[slot].astype(jnp.int32)).astype(jnp.int32)
        summed = summed + face_weights[slot] * jnp.take(values, target, axis=1)
    return summed


def operate(values, matrix, neighbors, face_weights, diagonal):
    points = matrix.shape[0]
    shaped = values.reshape(points, COMP, values.shape[1])
    spectral = jnp.einsum("nm,mcx->ncx", matrix, shaped, precision=lax.Precision.HIGHEST).reshape(values.shape)
    return FREQ * spectral + diagonal * values - neighbour_terms(values, neighbors, face_weights)


def reference(initial, source, neighbors, face_weights, damping):
    cells = initial.shape[1]
    diagonal = damping + jnp.sum(face_weights, axis=0)
    fine_matrix = spectral_matrix(NI)
    coarse_matrix = spectral_matrix(NC)
    solution = initial
    for sweep in range(SWEEPS_FINE):
        solution = solution + RELAX * (source - operate(solution, fine_matrix, neighbors, face_weights, diagonal)) / diagonal
    residual = source - operate(solution, fine_matrix, neighbors, face_weights, diagonal)
    coarse_rhs = jnp.einsum("jm,mcx->jcx", restrict_matrix(), residual.reshape(NI, COMP, cells), precision=lax.Precision.HIGHEST).reshape(NC * COMP, cells)
    correction = RELAX * coarse_rhs / diagonal
    for sweep in range(SWEEPS_COARSE - 1):
        correction = correction + RELAX * (coarse_rhs - operate(correction, coarse_matrix, neighbors, face_weights, diagonal)) / diagonal
    lifted = jnp.einsum("mj,jcx->mcx", prolong_matrix(), correction.reshape(NC, COMP, cells), precision=lax.Precision.HIGHEST)
    return solution + lifted.reshape(NI * COMP, cells)
```

```python
import functools

import jax
import jax.numpy as jnp
import numpy as np
from jax import lax
from jax.experimental import pallas as pl
from jax.experimental.pallas import tpu as pltpu
from jax.sharding import PartitionSpec as P

NI = 16
NC = 4
COMP = 5
NEIGH = 4
SWEEPS_FINE = 2
SWEEPS_COARSE = 3
PLANE = 256
FREQ = 0.15
RELAX = 0.6
KEEP = 1.0 - RELAX

LANES = 128
PB = PLANE // LANES
MODES = 16
HIGH = lax.Precision.HIGHEST

FV = SWEEPS_FINE * PB
FS = (SWEEPS_FINE - 1) * PB
MV = (SWEEPS_FINE + SWEEPS_COARSE) * PB
MS = MV - PB


def up8(count):
    return -(-count // 8) * 8


def row_map(own):
    rows = [divmod(r, COMP) for r in range(own)]
    rows += [None] * (up8(own) - own)
    other = NI * COMP - own
    rows += [divmod(own + r, COMP) for r in range(other)]
    rows += [None] * (up8(other) - other)
    return rows


def constants(own):
    rows = row_map(own)
    count = len(rows)
    derive = np.zeros((count, count))
    restrict = np.zeros((MODES, count))
    prolong = np.zeros((count, MODES))
    for i, left in enumerate(rows):
        if left is None:
            continue
        n, c = left
        phase = 2.0 * np.pi * n / NI
        shape = (1.0, np.cos(phase), np.sin(phase))
        for h in range(3):
            restrict[h * COMP + c, i] = shape[h] * (1.0 if h == 0 else 2.0) / NI
            prolong[i, h * COMP + c] = shape[h]
        for j, right in enumerate(rows):
            if right is not None and right[1] == c and right[0] != n:
                gap = n - right[0]
                derive[i, j] = 0.5 * (-1.0) ** gap / np.tan(np.pi * gap / NI)
    mode_derive = np.zeros((MODES, MODES))
    for c in range(COMP):
        mode_derive[COMP + c, 2 * COMP + c] = 1.0
        mode_derive[2 * COMP + c, COMP + c] = -1.0
    return [np.asarray(m, np.float32) for m in (derive, restrict, prolong, mode_derive)]


def dot(a, b):
    return jnp.dot(a, b, precision=HIGH, preferred_element_type=jnp.float32)


def lanes(start, count=1):
    return slice(start * LANES, (start + count) * LANES)


def lane_ds(block):
    return pl.ds(pl.multiple_of(block * LANES, LANES), LANES)


def build_table(idx_ref, wt_ref, at, near, bw, bf):
    target = near + lax.broadcasted_iota(jnp.int32, near.shape, 1)
    slot = lax.broadcasted_iota(jnp.int32, near.shape, 0)
    base = (target >> 7) + jnp.where((slot & 1) == 0, PB, 0)
    idx_ref[at, 0:NEIGH, :] = target & (LANES - 1)
    for j in range(PB + 1):
        wt_ref[at, NEIGH * j : NEIGH * (j + 1), :] = jnp.where(base == j, bw, 0.0)
    wt_ref[at, NEIGH * (PB + 1) : NEIGH * (PB + 1) + 1, :] = bf


def stencil(src_ref, center, idx_ref, wt_ref, at, groups):
    sources = [
        [src_ref[8 * g : 8 * g + 8, lane_ds(center + j - PB)] for j in range(2 * PB + 1)]
        for g in groups
    ]
    sums = [None] * len(groups)
    for k in range(NEIGH):
        index = idx_ref[at, pl.ds(k, 8, stride=0), :]
        for j in range(PB + 1):
            weight = wt_ref[at, pl.ds(NEIGH * j + k, 8, stride=0), :]
            for g in range(len(groups)):
                source = sources[g][j + (PB if k % 2 else 0)]
                term = weight * jnp.take_along_axis(source, index, axis=1)
                sums[g] = term if sums[g] is None else sums[g] + term
    return sums


def coefficient(wt_ref, at):
    return wt_ref[at, pl.ds(NEIGH * (PB + 1), 8, stride=0), :]


def blocks_loop(count, body, unroll):
    def step(i, carry):
        body(i)
        return carry

    lax.fori_loop(0, count, step, 0, unroll=min(unroll, count))


def pack_kernel(own_pad, init_ref, src_ref, near_ref, face_ref, damp_ref, restrict_ref,
                a_ref, b_ref, scaled_ref, coef_ref, mode_ref):
    cells = init_ref.shape[1]
    nblk = cells // LANES
    face = face_ref[...]
    diagonal = damp_ref[...] + jnp.sum(face, axis=0, keepdims=True)
    inverse = RELAX / diagonal
    bw = inverse * face
    coef_ref[0:NEIGH, :] = bw
    coef_ref[NEIGH : NEIGH + 1, :] = FREQ * inverse
    for g in range(own_pad // 8):
        scaled_ref[8 * g : 8 * g + 8, :] = src_ref[8 * g : 8 * g + 8, :] * inverse
    restrict = restrict_ref[:, 0:own_pad]
    mode_ref[...] = dot(restrict, scaled_ref[...])
    low_modes = dot(restrict, init_ref[:, lanes(FV, nblk - 2 * FV)])
    groups = own_pad // 8
    near = near_ref[...].astype(jnp.float32)

    def pack(out, high):
        t = 0
        first = nblk - FV if high else 0
        for g in range(groups):
            for d in range(FV):
                out[t] = init_ref[8 * g : 8 * g + 8, lanes(first + d)]
                t += 1
        first = nblk - FS if high else 0
        for g in range(groups):
            for d in range(FS):
                out[t] = scaled_ref[8 * g : 8 * g + 8, lanes(first + d)]
                t += 1
        first = nblk - MV if high else FV
        for g in range(MODES // 8):
            for d in range(MV - FV):
                out[t] = low_modes[8 * g : 8 * g + 8, lanes(first + d - FV)]
                t += 1
        first = nblk - MS if high else FS
        for g in range(MODES // 8):
            for d in range(MS - FS):
                out[t] = mode_ref[8 * g : 8 * g + 8, lanes(first + d)]
                t += 1
        first = nblk - MS if high else 0
        for d in range(MS):
            out[t, 0:NEIGH, :] = coef_ref[0:NEIGH, lanes(first + d)]
            out[t, NEIGH : 2 * NEIGH, :] = near[:, lanes(first + d)]
            t += 1
        for d in range(MS):
            out[t, d : d + 1, :] = coef_ref[NEIGH : NEIGH + 1, lanes(first + d)]

    odd = lax.axis_index("cell") & 1

    @pl.when(odd == 0)
    def _():
        pack(a_ref, True)
        pack(b_ref, False)

    @pl.when(odd == 1)
    def _():
        pack(a_ref, False)
        pack(b_ref, True)


def halo_tiles(own_pad):
    groups = own_pad // 8
    return groups * (FV + FS) + (MODES // 8) * (MV - FV + MS - FS) + MS + 1


def inner_kernel(own_pad, init_ref, scaled_ref, near_ref, coef_ref, derive_ref, restrict_ref,
                 own_ref, cross_ref, v1_ref, m1_ref, m2_ref, idx_ref, wt_ref,
                 first, deriv):
    cells = init_ref.shape[1]
    nblk = cells // LANES
    rows = derive_ref.shape[0]
    own_groups = range(own_pad // 8)
    all_groups = range(rows // 8)
    for b in range(nblk):
        build_table(idx_ref, wt_ref, b, near_ref[:, lanes(b)],
                    coef_ref[0:NEIGH, lanes(b)], coef_ref[NEIGH : NEIGH + 1, lanes(b)])
    width1 = nblk - 2 * PB
    deriv[:, 0 : width1 * LANES] = dot(derive_ref[:, 0:own_pad], init_ref[:, lanes(PB, width1)])

    def sweep1(i):
        b = i + PB
        sums = stencil(init_ref, b, idx_ref, wt_ref, b, own_groups)
        bf = coefficient(wt_ref, b)
        for g in all_groups:
            part = slice(8 * g, 8 * g + 8)
            value = -bf * deriv[part, lane_ds(i)]
            if g in own_groups:
                value = value + (KEEP * init_ref[part, lane_ds(b)] + scaled_ref[part, lane_ds(b)] + sums[g])
            first[part, lane_ds(i)] = value

    blocks_loop(width1, sweep1, 2)
    width2 = nblk - 4 * PB
    deriv[:, 0 : width2 * LANES] = dot(derive_ref[...], first[:, lanes(PB, width2)])

    def sweep2(i):
        b = i + 2 * PB
        sums = stencil(first, i + PB, idx_ref, wt_ref, b, all_groups)
        bf = coefficient(wt_ref, b)
        for g in all_groups:
            part = slice(8 * g, 8 * g + 8)
            value = KEEP * first[part, lane_ds(i + PB)] - bf * deriv[part, lane_ds(i)] + sums[g]
            if g in own_groups:
                own_ref[part, lane_ds(i)] = value + scaled_ref[part, lane_ds(b)]
            else:
                cross_ref[8 * g - own_pad : 8 * g + 8 - own_pad, lane_ds(i)] = value

    blocks_loop(width2, sweep2, 2)
    v1_ref[:, lanes(0, 2 * PB)] = first[:, lanes(0, 2 * PB)]
    v1_ref[:, lanes(2 * PB, 2 * PB)] = first[:, lanes(width1 - 2 * PB, 2 * PB)]
    m1_ref[...] = dot(restrict_ref[...], first[...])
    m2_ref[...] = dot(restrict_ref[:, 0:own_pad], own_ref[...]) + dot(
        restrict_ref[:, own_pad:], cross_ref[...]
    )


def outer_kernel(own_pad, a_ref, b_ref, init_ref, scaled_ref, smode_ref, own_ref, v1_ref,
                 m1i_ref, m2i_ref, idx_in, wt_in, derive_ref, restrict_ref, prolong_ref, turn_ref,
                 edge_ref, mid_ref, send_ref,
                 v0e, se, v1e, v2e, deriv, m0x, sx, m1x, m2x, rx, c1x, c2x, dm, idx, wt):
    cells = init_ref.shape[1]
    nblk = cells // LANES
    rows = derive_ref.shape[0]
    own_groups = range(own_pad // 8)
    all_groups = range(rows // 8)
    restrict = restrict_ref[...]
    derive = derive_ref[...]
    turn = turn_ref[...]
    idx[MS : MS + nblk] = idx_in[...]
    wt[MS : MS + nblk] = wt_in[...]
    v0e[:, lanes(FV, 2 * PB)] = init_ref[:, lanes(0, 2 * PB)]
    v0e[:, lanes(FV + 2 * PB, 2 * PB)] = init_ref[:, lanes(nblk - 2 * PB, 2 * PB)]
    se[:, lanes(FS, 2 * PB)] = scaled_ref[:, lanes(0, 2 * PB)]
    se[:, lanes(FS + 2 * PB, 2 * PB)] = scaled_ref[:, lanes(nblk - 2 * PB, 2 * PB)]
    sx[:, lanes(MS, nblk)] = smode_ref[...]
    v1e[:, lanes(2 * PB, 2 * PB)] = v1_ref[:, lanes(0, 2 * PB)]
    v1e[:, lanes(4 * PB, 2 * PB)] = v1_ref[:, lanes(2 * PB, 2 * PB)]
    m1x[:, lanes(MS + PB, nblk - 2 * PB)] = m1i_ref[...]
    far2 = MS - PB
    m2x[:, lanes(far2 + 2 * PB, nblk - 4 * PB)] = m2i_ref[...]

    def unpack(tiles, right):
        t = 0
        at = FV + 4 * PB if right else 0
        for g in own_groups:
            for d in range(FV):
                v0e[8 * g : 8 * g + 8, lanes(at + d)] = tiles[t]
                t += 1
        at = FS + 4 * PB if right else 0
        for g in own_groups:
            for d in range(FS):
                se[8 * g : 8 * g + 8, lanes(at + d)] = tiles[t]
                t += 1
        at = MV + FV if right else 0
        for g in range(MODES // 8):
            for d in range(MV - FV):
                m0x[8 * g : 8 * g + 8, lanes(at + d)] = tiles[t]
                t += 1
        at = MS + nblk + FS if right else 0
        for g in range(MODES // 8):
            for d in range(MS - FS):
                sx[8 * g : 8 * g + 8, lanes(at + d)] = tiles[t]
                t += 1
        at = MS + nblk if right else 0
        for d in range(MS):
            near = tiles[t + d, NEIGH : 2 * NEIGH, :].astype(jnp.int32)
            build_table(idx, wt, at + d, near, tiles[t + d, 0:NEIGH, :],
                        tiles[t + MS, d : d + 1, :])

    odd = lax.axis_index("cell") & 1

    @pl.when(odd == 0)
    def _():
        unpack(a_ref, True)
        unpack(b_ref, False)

    @pl.when(odd == 1)
    def _():
        unpack(a_ref, False)
        unpack(b_ref, True)

    restrict_own = restrict_ref[:, 0:own_pad]
    m0x[:, lanes(MV - FV, FV)] = dot(restrict_own, v0e[:, lanes(0, FV)])
    m0x[:, lanes(MV, FV)] = dot(restrict_own, v0e[:, lanes(FV + 4 * PB, FV)])
    sx[:, lanes(MS - FS, FS)] = dot(restrict_own, se[:, lanes(0, FS)])
    sx[:, lanes(MS + nblk, FS)] = dot(restrict_own, se[:, lanes(FS + 4 * PB, FS)])

    span = 2 * PB
    for side in range(2):
        from0 = side * (FV + 2 * PB) + PB
        deriv[:, lanes(side * span, span)] = dot(
            derive_ref[:, 0:own_pad], v0e[:, lanes(from0, span)]
        )
    for side in range(2):
        from0 = side * (FV + 2 * PB) + PB
        from_s = side * (FS + 3 * PB)
        table = MS - PB + side * nblk
        to = side * 6 * PB

        def sweep1(i, from0=from0, from_s=from_s, table=table, to=to, side=side):
            sums = stencil(v0e, i + from0, idx, wt, i + table, own_groups)
            bf = coefficient(wt, i + table)
            for g in all_groups:
                part = slice(8 * g, 8 * g + 8)
                value = -bf * deriv[part, lane_ds(i + side * span)]
                if g in own_groups:
                    value = value + (
                        KEEP * v0e[part, lane_ds(i + from0)] + se[part, lane_ds(i + from_s)] + sums[g]
                    )
                v1e[part, lane_ds(i + to)] = value

        blocks_loop(span, sweep1, 2)
    m1x[:, lanes(MS - PB, span)] = dot(restrict, v1e[:, lanes(0, span)])
    m1x[:, lanes(MS - PB + nblk, span)] = dot(restrict, v1e[:, lanes(6 * PB, span)])

    def relax(src, from_, out, to, table, count, source=None):
        dm[:, 0 : count * LANES] = dot(turn, src[:, lanes(from_, count)])
        rhs_ref, rhs_at, keep = source

        def body(i):
            sums = stencil(src, i + from_, idx, wt, i + table, range(MODES // 8))
            bf = coefficient(wt, i + table)
            for g in range(MODES // 8):
                part = slice(8 * g, 8 * g + 8)
                out[part, lane_ds(i + to)] = (
                    keep * src[part, lane_ds(i + from_)]
                    + rhs_ref[part, lane_ds(i + rhs_at)]
                    - bf * dm[part, lane_ds(i)]
                    + sums[g]
                )

        blocks_loop(count, body, 4)

    far = MS - PB
    relax(m0x, PB, m1x, 0, 0, far, (sx, 0, KEEP))
    right = MS + nblk + PB
    relax(m0x, MV + PB, m1x, right, right, far, (sx, right, KEEP))

    for side in range(2):
        deriv[:, lanes(side * span, span)] = dot(derive, v1e[:, lanes(PB + side * 4 * PB, span)])
    for side in range(2):
        from1 = PB + side * 4 * PB
        from_s = FS + side * 2 * PB
        table = MS + side * (nblk - 2 * PB)

        def sweep2(i, from1=from1, from_s=from_s, table=table, side=side):
            sums = stencil(v1e, i + from1, idx, wt, i + table, all_groups)
            bf = coefficient(wt, i + table)
            for g in all_groups:
                part = slice(8 * g, 8 * g + 8)
                value = (
                    KEEP * v1e[part, lane_ds(i + from1)]
                    - bf * deriv[part, lane_ds(i + side * span)]
                    + sums[g]
                )
                if g in own_groups:
                    value = value + se[part, lane_ds(i + from_s)]
                v2e[part, lane_ds(i + side * span)] = value

        blocks_loop(span, sweep2, 2)
    for side in range(2):
        m2x[:, lanes(far2 + side * (nblk - 2 * PB), span)] = dot(restrict, v2e[:, lanes(side * span, span)])

    relax(m1x, PB, m2x, 0, PB, far2, (sx, PB, KEEP))
    relax(m1x, MS + nblk, m2x, far2 + nblk, MS + nblk, far2, (sx, MS + nblk, KEEP))

    deep = MS - 2 * PB
    relax(m2x, PB, rx, 0, 2 * PB, nblk + 2 * deep, (sx, 2 * PB, -RELAX))
    relax(rx, PB, c1x, 0, 3 * PB, nblk + 2 * PB, (rx, PB, KEEP))
    relax(c1x, PB, c2x, 0, 4 * PB, nblk, (rx, 2 * PB, KEEP))

    prolong = prolong_ref[...]
    lead = (rows - own_pad)
    for side in range(2):
        part = lanes(side * span, span)
        lifted = v2e[:, part] + dot(prolong, c2x[:, lanes(side * (nblk - 2 * PB), span)])
        edge_ref[:, part] = lifted[0:own_pad, :]
        send_ref[0:lead, part] = lifted[own_pad:, :]
    middle = lanes(2 * PB, nblk - 4 * PB)
    send_ref[lead:, :] = c2x[:, middle]
    mid_ref[...] = own_ref[...] + dot(prolong_ref[0:own_pad, :], c2x[:, middle])


def final_kernel(count, edge_ref, mid_ref, lift_ref, *refs):
    out_ref = refs[-1]
    own_pad = edge_ref.shape[0]
    nblk = out_ref.shape[1] // LANES
    span = 2 * PB
    edge = edge_ref[...]
    mid = mid_ref[...]
    for k in range(count):
        early, late = refs[2 * k], refs[2 * k + 1]
        edge = edge + late[0:own_pad, :]
        mid = mid + early[...] + dot(lift_ref[k], late[own_pad:, :])
    out_ref[:, lanes(0, span)] = edge[:, lanes(0, span)]
    out_ref[:, lanes(nblk - span, span)] = edge[:, lanes(span, span)]
    out_ref[:, lanes(span, nblk - 2 * span)] = mid


def vm(*shape):
    return pltpu.VMEM(shape, jnp.float32)


def f32(*shape):
    return jax.ShapeDtypeStruct(shape, jnp.float32)


def call(kernel, name, out_shape, scratch, cost_us, *args):
    whole = pl.BlockSpec(memory_space=pltpu.VMEM)
    single = not isinstance(out_shape, (tuple, list))
    return pl.pallas_call(
        kernel,
        name=name,
        out_shape=out_shape,
        in_specs=[whole] * len(args),
        out_specs=whole if single else [whole] * len(out_shape),
        scratch_shapes=scratch,
        compiler_params=pltpu.CompilerParams(vmem_limit_bytes=16 * 1024 * 1024),
        cost_estimate=pl.CostEstimate(
            flops=int(cost_us * 1e8), bytes_accessed=int(cost_us * 3e6), transcendentals=0
        ),
    )(*args)


def per_device(initial, source, neighbors, face_weights, damping):
    own, cells = initial.shape
    nblk = cells // LANES
    inst_count = lax.axis_size("inst")
    cell_count = lax.axis_size("cell")
    own_pad = up8(own)
    derive, restrict, prolong, turn = constants(own)
    rows = derive.shape[0]
    cross = rows - own_pad
    if own_pad != own:
        initial = jnp.pad(initial, ((0, own_pad - own), (0, 0)))
        source = jnp.pad(source, ((0, own_pad - own), (0, 0)))
    tiles = halo_tiles(own_pad)
    span = 2 * PB
    mid_blocks = nblk - 2 * span
    slots = NEIGH * (PB + 1) + 4

    pack_a, pack_b, scaled, coef, smode = call(
        functools.partial(pack_kernel, own_pad), "pack",
        [f32(tiles, 8, LANES), f32(tiles, 8, LANES), f32(own_pad, cells), f32(8, cells),
         f32(MODES, cells)],
        [], 2, initial, source, neighbors, face_weights, damping.reshape(1, cells),
        jnp.asarray(restrict),
    )
    near_pairs = [(i, i ^ 1) for i in range(cell_count) if i ^ 1 < cell_count]
    far_pairs = []
    for i in range(1, cell_count - 1, 2):
        far_pairs += [(i, i + 1), (i + 1, i)]
    halo_b = lax.ppermute(pack_b, "cell", far_pairs)
    halo_a = lax.ppermute(pack_a, "cell", near_pairs)

    own_mid, cross_mid, v1, m1, m2, idx, wt = call(
        functools.partial(inner_kernel, own_pad), "inner",
        [f32(own_pad, mid_blocks * LANES), f32(cross, mid_blocks * LANES),
         f32(rows, 4 * PB * LANES), f32(MODES, (nblk - 2 * PB) * LANES),
         f32(MODES, mid_blocks * LANES),
         jax.ShapeDtypeStruct((nblk, 8, LANES), jnp.int32), f32(nblk, slots, LANES)],
        [vm(rows, (nblk - 2 * PB) * LANES), vm(rows, (nblk - 2 * PB) * LANES)], 5,
        initial, scaled, neighbors, coef, jnp.asarray(derive), jnp.asarray(restrict),
    )

    def share(array, k):
        if cross == own_pad:
            return array
        part = lax.slice_in_dim(array, (k - 1) * own, k * own, axis=0)
        return jnp.pad(part, ((0, own_pad - own), (0, 0)))

    def shift(k):
        return [(i, (i + k) % inst_count) for i in range(inst_count)]

    early = [lax.ppermute(share(cross_mid, k), "inst", shift(k)) for k in range(1, inst_count)]

    ext = nblk + 2 * MS
    edge, mid, send = call(
        functools.partial(outer_kernel, own_pad), "outer",
        [f32(own_pad, 2 * span * LANES), f32(own_pad, mid_blocks * LANES),
         f32(cross + MODES, 2 * span * LANES)],
        [vm(own_pad, 2 * (FV + 2 * PB) * LANES), vm(own_pad, 2 * (FS + 2 * PB) * LANES),
         vm(rows, 8 * PB * LANES), vm(rows, 2 * span * LANES), vm(rows, 2 * span * LANES),
         vm(MODES, 2 * MV * LANES), vm(MODES, ext * LANES), vm(MODES, ext * LANES),
         vm(MODES, (ext - 2 * PB) * LANES), vm(MODES, (ext - 4 * PB) * LANES),
         vm(MODES, (nblk + 2 * PB) * LANES), vm(MODES, cells), vm(MODES, ext * LANES),
         pltpu.VMEM((ext, 8, LANES), jnp.int32), vm(ext, slots, LANES)],
        8, halo_a, halo_b, initial, scaled, smode, own_mid, v1, m1, m2, idx, wt,
        jnp.asarray(derive), jnp.asarray(restrict), jnp.asarray(prolong), jnp.asarray(turn),
    )

    def share_late(k):
        if cross == own_pad:
            return send
        return jnp.concatenate([share(send[:cross], k), send[cross:]], axis=0)

    late = [lax.ppermute(share_late(k), "inst", shift(k)) for k in range(1, inst_count)]
    other = prolong[own_pad:]
    lift = np.zeros((inst_count - 1, own_pad, MODES), np.float32)
    for k in range(1, inst_count):
        lift[k - 1, :own] = other[(k - 1) * own : k * own]
    received = [r for pair in zip(early, late) for r in pair]
    out = call(
        functools.partial(final_kernel, inst_count - 1), "final", f32(own_pad, cells), [], 1,
        edge, mid, jnp.asarray(lift), *received,
    )
    return out[:own] if own_pad != own else out


def solution(mesh):
    return jax.shard_map(
        per_device,
        mesh=mesh,
        in_specs=(
            P("inst", "cell"),
            P("inst", "cell"),
            P(None, "cell"),
            P(None, "cell"),
            P("cell"),
        ),
        out_specs=P("inst", "cell"),
        check_vma=False,
    )
```

```python
import functools

import jax
import jax.numpy as jnp
import numpy as np
from jax import lax
from jax.experimental import pallas as pl
from jax.experimental.pallas import tpu as pltpu
from jax.sharding import PartitionSpec as P


NI = 16
COMP = 5
NEIGH = 4
SWEEPS_FINE = 2
SWEEPS_COARSE = 3
PLANE = 256
FREQ = 0.15
RELAX = 0.6
KEEP = 1.0 - RELAX

LANES = 128
PB = PLANE // LANES
MODES = 16

FV = SWEEPS_FINE * PB
FS = (SWEEPS_FINE - 1) * PB
MV = (SWEEPS_FINE + SWEEPS_COARSE) * PB
MS = MV - PB


def up8(count):
    return -(-count // 8) * 8


def row_map(own):
    rows = [divmod(r, COMP) for r in range(own)]
    rows += [None] * (up8(own) - own)
    other = NI * COMP - own
    rows += [divmod(own + r, COMP) for r in range(other)]
    rows += [None] * (up8(other) - other)
    return rows


def mode_row(h, c):
    if h:
        return 8 * (h - 1) + 3 + c
    return c if c < 3 else 5 + c


def split_matrix(matrix):
    high = matrix.astype(jnp.bfloat16)
    low = (matrix - high.astype(np.float64)).astype(jnp.bfloat16)
    return np.concatenate([high, low, high], axis=1)


def constants(own, inst_count):
    rows = row_map(own)
    own_pad = up8(own)
    count = len(rows)
    derive = np.zeros((count, count))
    restrict = np.zeros((MODES, count))
    prolong = np.zeros((count, MODES))
    for i, left in enumerate(rows):
        if left is None:
            continue
        n, c = left
        phase = 2.0 * np.pi * n / NI
        shape = (1.0, np.cos(phase), np.sin(phase))
        for h in range(3):
            restrict[mode_row(h, c), i] = shape[h] * (1.0 if h == 0 else 2.0) / NI
            prolong[i, mode_row(h, c)] = shape[h]
        for j, right in enumerate(rows):
            if right is not None and right[1] == c and right[0] != n:
                gap = n - right[0]
                derive[i, j] = 0.5 * (-1.0) ** gap / np.tan(np.pi * gap / NI)
    other = prolong[own_pad:]
    lifts = []
    for k in range(1, inst_count):
        lift = np.zeros((own_pad, MODES))
        lift[:own] = other[(k - 1) * own : k * own]
        lifts.append(lift)
    parts = [derive[:, :own_pad], np.concatenate([derive, restrict]), restrict[:, :own_pad], prolong]
    parts += lifts
    width = -(-3 * count // LANES) * LANES
    blocks, starts, at = [], [], 0
    for part in parts:
        wide = split_matrix(part)
        height = -(-wide.shape[0] // 16) * 16
        blocks.append(np.pad(wide, ((0, height - wide.shape[0]), (0, width - wide.shape[1]))))
        starts.append(at)
        at += height
    return np.concatenate(blocks), starts, count


def split3(values):
    high = values.astype(jnp.bfloat16).astype(jnp.float32)
    return jnp.concatenate([values, values, values - high], axis=0).astype(jnp.bfloat16)


def dot(matrix, values):
    return jnp.dot(matrix, split3(values), preferred_element_type=jnp.float32)


def matrix_of(ref, start, height, depth):
    return ref[start : start + height, 0 : 3 * depth]


def lanes(start, count=1):
    return slice(start * LANES, (start + count) * LANES)


def lane_ds(block):
    return pl.ds(pl.multiple_of(block * LANES, LANES), LANES)


def build_table(idx_ref, wt_ref, at, near, bw, bf):
    target = near + lax.broadcasted_iota(jnp.int32, near.shape, 1)
    slot = lax.broadcasted_iota(jnp.int32, near.shape, 0)
    base = (target >> 7) + jnp.where((slot & 1) == 0, PB, 0)
    idx_ref[at, 0:NEIGH, :] = target & (LANES - 1)
    for j in range(PB + 1):
        wt_ref[at, NEIGH * j : NEIGH * (j + 1), :] = jnp.where(base == j, bw, 0.0)
    wt_ref[at, NEIGH * (PB + 1) : NEIGH * (PB + 1) + 1, :] = bf


def stencil(src_ref, center, idx_ref, wt_ref, at, groups):
    sources = [
        [src_ref[8 * g : 8 * g + 8, lane_ds(center + j - PB)] for j in range(2 * PB + 1)]
        for g in groups
    ]
    sums = [None] * len(groups)
    for k in range(NEIGH):
        index = idx_ref[at, pl.ds(k, 8, stride=0), :]
        for j in range(PB + 1):
            weight = wt_ref[at, pl.ds(NEIGH * j + k, 8, stride=0), :]
            for g in range(len(groups)):
                source = sources[g][j + (PB if k % 2 else 0)]
                term = weight * jnp.take_along_axis(source, index, axis=1)
                sums[g] = term if sums[g] is None else sums[g] + term
    return sums


def chunks(groups, most=5):
    return [groups[i : i + most] for i in range(0, len(groups), most)]


def coefficient(wt_ref, at):
    return wt_ref[at, pl.ds(NEIGH * (PB + 1), 8, stride=0), :]


def blocks_loop(count, body, unroll):
    def step(i, carry):
        body(i)
        return carry

    lax.fori_loop(0, count, step, 0, unroll=min(unroll, count))


def pack_kernel(own_pad, starts, init_hbm, src_hbm, near_hbm, face_hbm, damp_hbm, matrix_hbm,
                a_ref, b_ref, init_ref, scaled_ref, near_ref, coef_ref, mode_ref, matrix_ref,
                src_ref, face_ref, damp_ref, sems):
    cells = init_ref.shape[1]
    nblk = cells // LANES
    half = own_pad // 16 * 8
    copies = [
        pltpu.make_async_copy(face_hbm, face_ref, sems.at[0]),
        pltpu.make_async_copy(damp_hbm, damp_ref, sems.at[1]),
        pltpu.make_async_copy(src_hbm.at[0:half], src_ref.at[0:half], sems.at[2]),
        pltpu.make_async_copy(src_hbm.at[half:own_pad], src_ref.at[half:own_pad], sems.at[3]),
        pltpu.make_async_copy(init_hbm.at[0:half], init_ref.at[0:half], sems.at[4]),
        pltpu.make_async_copy(init_hbm.at[half:own_pad], init_ref.at[half:own_pad], sems.at[5]),
        pltpu.make_async_copy(near_hbm, near_ref, sems.at[6]),
        pltpu.make_async_copy(matrix_hbm, matrix_ref, sems.at[7]),
    ]
    for copy in copies:
        copy.start()
    copies[0].wait()
    copies[1].wait()
    face = face_ref[...]
    inverse = RELAX / (damp_ref[...] + jnp.sum(face, axis=0, keepdims=True))
    coef_ref[0:NEIGH, :] = inverse * face
    coef_ref[NEIGH : NEIGH + 1, :] = FREQ * inverse
    copies[2].wait()
    copies[3].wait()
    groups = own_pad // 8
    for g in range(groups):
        scaled_ref[8 * g : 8 * g + 8, :] = src_ref[8 * g : 8 * g + 8, :] * inverse
    for copy in copies[4:]:
        copy.wait()
    restrict = matrix_of(matrix_ref, starts[2], MODES, own_pad)
    for d in range(0, nblk, 2):
        mode_ref[:, lanes(d, 2)] = dot(restrict, scaled_ref[:, lanes(d, 2)])
    low_modes = [
        dot(restrict, init_ref[:, lanes(d, 2)]) for d in range(FV, nblk - FV, 2)
    ]
    near = near_ref[...].astype(jnp.float32)

    def low_mode(block):
        chunk = low_modes[(block - FV) // 2]
        return chunk[:, lanes((block - FV) % 2)]

    def pack(out, high):
        t = 0
        first = nblk - FV if high else 0
        for g in range(groups):
            for d in range(FV):
                out[t] = init_ref[8 * g : 8 * g + 8, lanes(first + d)]
                t += 1
        first = nblk - FS if high else 0
        for g in range(groups):
            for d in range(FS):
                out[t] = scaled_ref[8 * g : 8 * g + 8, lanes(first + d)]
                t += 1
        first = nblk - MV if high else FV
        for g in range(MODES // 8):
            for d in range(MV - FV):
                out[t] = low_mode(first + d)[8 * g : 8 * g + 8]
                t += 1
        first = nblk - MS if high else FS
        for g in range(MODES // 8):
            for d in range(MS - FS):
                out[t] = mode_ref[8 * g : 8 * g + 8, lanes(first + d)]
                t += 1
        first = nblk - MS if high else 0
        for d in range(MS):
            out[t, 0:NEIGH, :] = coef_ref[0:NEIGH, lanes(first + d)]
            out[t, NEIGH : 2 * NEIGH, :] = near[:, lanes(first + d)]
            t += 1
        for d in range(MS):
            out[t, d : d + 1, :] = coef_ref[NEIGH : NEIGH + 1, lanes(first + d)]

    odd = lax.axis_index("cell") & 1

    @pl.when(odd == 0)
    def _():
        pack(a_ref, True)
        pack(b_ref, False)

    @pl.when(odd == 1)
    def _():
        pack(a_ref, False)
        pack(b_ref, True)


def halo_tiles(own_pad):
    groups = own_pad // 8
    return groups * (FV + FS) + (MODES // 8) * (MV - FV + MS - FS) + MS + 1


def inner_kernel(own_pad, rows, starts, init_ref, scaled_ref, near_ref, coef_ref, matrix_ref,
                 own_ref, cross_ref, v1_ref, m1_ref, m2_ref, idx_ref, wt_ref,
                 first, deriv):
    cells = init_ref.shape[1]
    nblk = cells // LANES
    own_groups = list(range(own_pad // 8))
    all_groups = list(range(rows // 8))
    for b in range(nblk):
        build_table(idx_ref, wt_ref, b, near_ref[:, lanes(b)],
                    coef_ref[0:NEIGH, lanes(b)], coef_ref[NEIGH : NEIGH + 1, lanes(b)])
    width1 = nblk - 2 * PB
    derive = matrix_of(matrix_ref, starts[0], rows, own_pad)
    for d in range(0, width1, 2):
        deriv[:, lanes(d, 2)] = dot(derive, init_ref[:, lanes(PB + d, 2)])

    def sweep1(i):
        b = i + PB
        bf = coefficient(wt_ref, b)
        sums = stencil(init_ref, b, idx_ref, wt_ref, b, own_groups)
        for g in all_groups:
            part = slice(8 * g, 8 * g + 8)
            value = -bf * deriv[part, lane_ds(i)]
            if g in own_groups:
                value = value + (KEEP * init_ref[part, lane_ds(b)] + scaled_ref[part, lane_ds(b)] + sums[g])
            first[part, lane_ds(i)] = value

    blocks_loop(width1, sweep1, 2)
    width2 = nblk - 4 * PB
    both = matrix_of(matrix_ref, starts[1], rows + MODES, rows)
    for d in range(0, width1, 2):
        mixed = dot(both, first[:, lanes(d, 2)])
        deriv[:, lanes(d, 2)] = mixed[0:rows]
        m1_ref[:, lanes(d, 2)] = mixed[rows:]

    def sweep2(i):
        b = i + 2 * PB
        bf = coefficient(wt_ref, b)
        for groups in chunks(all_groups):
            sums = stencil(first, i + PB, idx_ref, wt_ref, b, groups)
            for g, total in zip(groups, sums):
                part = slice(8 * g, 8 * g + 8)
                value = KEEP * first[part, lane_ds(i + PB)] - bf * deriv[part, lane_ds(i + PB)] + total
                if g in own_groups:
                    own_ref[part, lane_ds(i)] = value + scaled_ref[part, lane_ds(b)]
                else:
                    cross_ref[8 * g - own_pad : 8 * g + 8 - own_pad, lane_ds(i)] = value

    blocks_loop(width2, sweep2, 2)
    v1_ref[:, lanes(0, 2 * PB)] = first[:, lanes(0, 2 * PB)]
    v1_ref[:, lanes(2 * PB, 2 * PB)] = first[:, lanes(width1 - 2 * PB, 2 * PB)]
    restrict = matrix_of(matrix_ref, starts[1] + rows, MODES, rows)
    for d in range(0, width2, 2):
        values = jnp.concatenate([own_ref[:, lanes(d, 2)], cross_ref[:, lanes(d, 2)]], axis=0)
        m2_ref[:, lanes(d, 2)] = dot(restrict, values)


def outer_kernel(own_pad, rows, starts, a_ref, b_ref, init_ref, scaled_ref, smode_ref, own_ref,
                 v1_ref, m1i_ref, m2i_ref, idx_in, wt_in, matrix_ref,
                 edge_ref, mid_ref, send_ref,
                 v0e, se, v1e, v2e, deriv, m0x, sx, m1x, m2x, rx, c1x, c2x, idx, wt):
    cells = init_ref.shape[1]
    nblk = cells // LANES
    own_groups = list(range(own_pad // 8))
    all_groups = list(range(rows // 8))
    idx[MS : MS + nblk] = idx_in[...]
    wt[MS : MS + nblk] = wt_in[...]
    v0e[:, lanes(FV, 2 * PB)] = init_ref[:, lanes(0, 2 * PB)]
    v0e[:, lanes(FV + 2 * PB, 2 * PB)] = init_ref[:, lanes(nblk - 2 * PB, 2 * PB)]
    se[:, lanes(FS, 2 * PB)] = scaled_ref[:, lanes(0, 2 * PB)]
    se[:, lanes(FS + 2 * PB, 2 * PB)] = scaled_ref[:, lanes(nblk - 2 * PB, 2 * PB)]
    sx[:, lanes(MS, nblk)] = smode_ref[...]
    v1e[:, lanes(2 * PB, 2 * PB)] = v1_ref[:, lanes(0, 2 * PB)]
    v1e[:, lanes(4 * PB, 2 * PB)] = v1_ref[:, lanes(2 * PB, 2 * PB)]
    m1x[:, lanes(MS + PB, nblk - 2 * PB)] = m1i_ref[...]
    far2 = MS - PB
    m2x[:, lanes(far2 + 2 * PB, nblk - 4 * PB)] = m2i_ref[...]

    def unpack(tiles, right):
        t = 0
        at = FV + 4 * PB if right else 0
        for g in own_groups:
            for d in range(FV):
                v0e[8 * g : 8 * g + 8, lanes(at + d)] = tiles[t]
                t += 1
        at = FS + 4 * PB if right else 0
        for g in own_groups:
            for d in range(FS):
                se[8 * g : 8 * g + 8, lanes(at + d)] = tiles[t]
                t += 1
        at = MV + FV if right else 0
        for g in range(MODES // 8):
            for d in range(MV - FV):
                m0x[8 * g : 8 * g + 8, lanes(at + d)] = tiles[t]
                t += 1
        at = MS + nblk + FS if right else 0
        for g in range(MODES // 8):
            for d in range(MS - FS):
                sx[8 * g : 8 * g + 8, lanes(at + d)] = tiles[t]
                t += 1
        at = MS + nblk if right else 0
        for d in range(MS):
            near = tiles[t + d, NEIGH : 2 * NEIGH, :].astype(jnp.int32)
            build_table(idx, wt, at + d, near, tiles[t + d, 0:NEIGH, :],
                        tiles[t + MS, d : d + 1, :])

    odd = lax.axis_index("cell") & 1

    @pl.when(odd == 0)
    def _():
        unpack(a_ref, True)
        unpack(b_ref, False)

    @pl.when(odd == 1)
    def _():
        unpack(a_ref, False)
        unpack(b_ref, True)

    restrict = matrix_of(matrix_ref, starts[2], MODES, own_pad)
    for d in range(0, FV, 2):
        m0x[:, lanes(MV - FV + d, 2)] = dot(restrict, v0e[:, lanes(d, 2)])
        m0x[:, lanes(MV + d, 2)] = dot(restrict, v0e[:, lanes(FV + 4 * PB + d, 2)])
    for d in range(0, FS, 2):
        sx[:, lanes(MS - FS + d, 2)] = dot(restrict, se[:, lanes(d, 2)])
        sx[:, lanes(MS + nblk + d, 2)] = dot(restrict, se[:, lanes(FS + 4 * PB + d, 2)])

    span = 2 * PB
    derive = matrix_of(matrix_ref, starts[0], rows, own_pad)
    for side in range(2):
        for d in range(0, span, 2):
            deriv[:, lanes(side * span + d, 2)] = dot(
                derive, v0e[:, lanes(side * (FV + 2 * PB) + PB + d, 2)]
            )
    for side in range(2):
        from0 = side * (FV + 2 * PB) + PB
        from_s = side * (FS + 3 * PB)
        table = MS - PB + side * nblk
        to = side * 6 * PB

        def sweep1(i, from0=from0, from_s=from_s, table=table, to=to, side=side):
            bf = coefficient(wt, i + table)
            sums = stencil(v0e, i + from0, idx, wt, i + table, own_groups)
            for g in all_groups:
                part = slice(8 * g, 8 * g + 8)
                value = -bf * deriv[part, lane_ds(i + side * span)]
                if g in own_groups:
                    value = value + (
                        KEEP * v0e[part, lane_ds(i + from0)] + se[part, lane_ds(i + from_s)] + sums[g]
                    )
                v1e[part, lane_ds(i + to)] = value

        blocks_loop(span, sweep1, 2)
    both = matrix_of(matrix_ref, starts[1], rows + MODES, rows)
    for side in range(2):
        for d in range(0, 3 * PB, 2):
            mixed = dot(both, v1e[:, lanes(side * 5 * PB + d, 2)])
            deriv[:, lanes(side * 3 * PB + d, 2)] = mixed[0:rows]
            m1x[:, lanes(MS - PB + side * (nblk - PB) + d, 2)] = mixed[rows:]

    top = lax.broadcasted_iota(jnp.int32, (8, LANES), 0) >= 3

    def relax(src, from_, out, to, table, count, source):
        rhs_ref, rhs_at, keep = source
        low, high = slice(0, 8), slice(8, 16)

        def body(i):
            bf = jnp.where(top, coefficient(wt, i + table), 0.0)
            sums = stencil(src, i + from_, idx, wt, i + table, range(MODES // 8))
            here = lane_ds(i + from_)
            src0, src1 = src[low, here], src[high, here]
            rhs, at = lane_ds(i + rhs_at), lane_ds(i + to)
            out[low, at] = keep * src0 + rhs_ref[low, rhs] - bf * src1 + sums[0]
            out[high, at] = keep * src1 + rhs_ref[high, rhs] + bf * src0 + sums[1]

        blocks_loop(count, body, 4)

    far = MS - PB
    relax(m0x, PB, m1x, 0, 0, far, (sx, 0, KEEP))
    right = MS + nblk + PB
    relax(m0x, MV + PB, m1x, right, right, far, (sx, right, KEEP))

    for side in range(2):
        from1 = PB + side * 4 * PB
        from_d = PB + side * 2 * PB
        from_s = FS + side * 2 * PB
        table = MS + side * (nblk - 2 * PB)

        def sweep2(i, from1=from1, from_d=from_d, from_s=from_s, table=table, side=side):
            bf = coefficient(wt, i + table)
            for groups in chunks(all_groups):
                sums = stencil(v1e, i + from1, idx, wt, i + table, groups)
                for g, total in zip(groups, sums):
                    part = slice(8 * g, 8 * g + 8)
                    value = (
                        KEEP * v1e[part, lane_ds(i + from1)] - bf * deriv[part, lane_ds(i + from_d)] + total
                    )
                    if g in own_groups:
                        value = value + se[part, lane_ds(i + from_s)]
                    v2e[part, lane_ds(i + side * span)] = value

        blocks_loop(span, sweep2, 2)
    restrict_all = matrix_of(matrix_ref, starts[1] + rows, MODES, rows)
    for side in range(2):
        for d in range(0, span, 2):
            m2x[:, lanes(far2 + side * (nblk - 2 * PB) + d, 2)] = dot(
                restrict_all, v2e[:, lanes(side * span + d, 2)]
            )

    relax(m1x, PB, m2x, 0, PB, far2, (sx, PB, KEEP))
    relax(m1x, MS + nblk, m2x, far2 + nblk, MS + nblk, far2, (sx, MS + nblk, KEEP))

    deep = MS - 2 * PB
    relax(m2x, PB, rx, 0, 2 * PB, nblk + 2 * deep, (sx, 2 * PB, -RELAX))
    relax(rx, PB, c1x, 0, 3 * PB, nblk + 2 * PB, (rx, PB, KEEP))
    relax(c1x, PB, c2x, 0, 4 * PB, nblk, (rx, 2 * PB, KEEP))

    prolong = matrix_of(matrix_ref, starts[3], rows, MODES)
    lead = rows - own_pad
    for side in range(2):
        for d in range(0, span, 2):
            part = lanes(side * span + d, 2)
            lifted = v2e[:, part] + dot(prolong, c2x[:, lanes(side * (nblk - 2 * PB) + d, 2)])
            edge_ref[:, part] = lifted[0:own_pad, :]
            send_ref[0:lead, part] = lifted[own_pad:, :]
    prolong_own = matrix_of(matrix_ref, starts[3], own_pad, MODES)
    for d in range(0, nblk - 4 * PB, 2):
        modes = c2x[:, lanes(2 * PB + d, 2)]
        send_ref[lead:, lanes(d, 2)] = modes
        mid_ref[:, lanes(d, 2)] = own_ref[:, lanes(d, 2)] + dot(prolong_own, modes)


def final_kernel(count, starts, edge_ref, mid_ref, matrix_ref, *refs):
    out_ref = refs[-1]
    own_pad = edge_ref.shape[0]
    nblk = out_ref.shape[1] // LANES
    span = 2 * PB
    early, late = refs[0 : 2 * count : 2], refs[1 : 2 * count : 2]
    for d in range(0, 2 * span, 2):
        edge = edge_ref[:, lanes(d, 2)]
        for k in range(count):
            edge = edge + late[k][0:own_pad, lanes(d, 2)]
        out_ref[:, lanes(d if d < span else nblk - 2 * span + d, 2)] = edge
    for d in range(0, nblk - 2 * span, 2):
        mid = mid_ref[:, lanes(d, 2)]
        for k in range(count):
            lift = matrix_of(matrix_ref, starts[4 + k], own_pad, MODES)
            mid = mid + early[k][:, lanes(d, 2)] + dot(lift, late[k][own_pad:, lanes(d, 2)])
        out_ref[:, lanes(span + d, 2)] = mid


def vm(*shape):
    return pltpu.VMEM(shape, jnp.float32)


def f32(*shape):
    return jax.ShapeDtypeStruct(shape, jnp.float32)


def call(kernel, out_shape, scratch, cost_us, *args, fetch=False):
    whole = pl.BlockSpec(memory_space=pltpu.VMEM)
    single = not isinstance(out_shape, (tuple, list))
    return pl.pallas_call(
        kernel,
        out_shape=out_shape,
        in_specs=[pl.BlockSpec(memory_space=pltpu.HBM) if fetch else whole] * len(args),
        out_specs=whole if single else [whole] * len(out_shape),
        scratch_shapes=scratch,
        compiler_params=pltpu.CompilerParams(vmem_limit_bytes=16 * 1024 * 1024),
        cost_estimate=pl.CostEstimate(
            flops=int(cost_us * 1e8), bytes_accessed=int(cost_us * 3e6), transcendentals=0
        ),
    )(*args)


def per_device(initial, source, neighbors, face_weights, damping):
    own, cells = initial.shape
    nblk = cells // LANES
    inst_count = lax.axis_size("inst")
    cell_count = lax.axis_size("cell")
    own_pad = up8(own)
    matrices, starts, rows = constants(own, inst_count)
    matrices = jnp.asarray(matrices)
    cross = rows - own_pad
    if own_pad != own:
        initial = jnp.pad(initial, ((0, own_pad - own), (0, 0)))
        source = jnp.pad(source, ((0, own_pad - own), (0, 0)))
    tiles = halo_tiles(own_pad)
    span = 2 * PB
    mid_blocks = nblk - 2 * span
    slots = NEIGH * (PB + 1) + 4

    def int32(*shape):
        return jax.ShapeDtypeStruct(shape, jnp.int32)

    pack_a, pack_b, initial, scaled, neighbors, coef, smode, matrices = call(
        functools.partial(pack_kernel, own_pad, starts),
        [f32(tiles, 8, LANES), f32(tiles, 8, LANES), f32(own_pad, cells), f32(own_pad, cells),
         int32(NEIGH, cells), f32(8, cells), f32(MODES, cells),
         jax.ShapeDtypeStruct(matrices.shape, matrices.dtype)],
        [vm(own_pad, cells), vm(NEIGH, cells), vm(1, cells), pltpu.SemaphoreType.DMA((8,))], 2,
        *[
            pltpu.with_memory_space_constraint(x, pltpu.HBM)
            for x in (initial, source, neighbors, face_weights, damping.reshape(1, cells), matrices)
        ],
        fetch=True,
    )
    near_pairs = [(i, i ^ 1) for i in range(cell_count) if i ^ 1 < cell_count]
    far_pairs = []
    for i in range(1, cell_count - 1, 2):
        far_pairs += [(i, i + 1), (i + 1, i)]
    halo_b = lax.ppermute(pack_b, "cell", far_pairs)
    halo_a = lax.ppermute(pack_a, "cell", near_pairs)

    own_mid, cross_mid, v1, m1, m2, idx, wt = call(
        functools.partial(inner_kernel, own_pad, rows, starts),
        [f32(own_pad, mid_blocks * LANES), f32(cross, mid_blocks * LANES),
         f32(rows, 4 * PB * LANES), f32(MODES, (nblk - 2 * PB) * LANES),
         f32(MODES, mid_blocks * LANES), int32(nblk, 8, LANES), f32(nblk, slots, LANES)],
        [vm(rows, (nblk - 2 * PB) * LANES), vm(rows, (nblk - 2 * PB) * LANES)], 5,
        initial, scaled, neighbors, coef, matrices,
    )

    def share(array, k):
        if cross == own_pad:
            return array
        part = lax.slice_in_dim(array, (k - 1) * own, k * own, axis=0)
        return jnp.pad(part, ((0, own_pad - own), (0, 0)))

    def shift(k):
        return [(i, (i + k) % inst_count) for i in range(inst_count)]

    early = [lax.ppermute(share(cross_mid, k), "inst", shift(k)) for k in range(1, inst_count)]

    ext = nblk + 2 * MS
    edge, mid, send = call(
        functools.partial(outer_kernel, own_pad, rows, starts),
        [f32(own_pad, 2 * span * LANES), f32(own_pad, mid_blocks * LANES),
         f32(cross + MODES, 2 * span * LANES)],
        [vm(own_pad, 2 * (FV + 2 * PB) * LANES), vm(own_pad, 2 * (FS + 2 * PB) * LANES),
         vm(rows, 8 * PB * LANES), vm(rows, 2 * span * LANES), vm(rows, 6 * PB * LANES),
         vm(MODES, 2 * MV * LANES), vm(MODES, ext * LANES), vm(MODES, ext * LANES),
         vm(MODES, (ext - 2 * PB) * LANES), vm(MODES, (ext - 4 * PB) * LANES),
         vm(MODES, (nblk + 2 * PB) * LANES), vm(MODES, cells),
         pltpu.VMEM((ext, 8, LANES), jnp.int32), vm(ext, slots, LANES)],
        8, halo_a, halo_b, initial, scaled, smode, own_mid, v1, m1, m2, idx, wt, matrices,
    )

    def share_late(k):
        if cross == own_pad:
            return send
        return jnp.concatenate([share(send[:cross], k), send[cross:]], axis=0)

    late = [lax.ppermute(share_late(k), "inst", shift(k)) for k in range(1, inst_count)]
    received = [r for pair in zip(early, late) for r in pair]
    out = call(
        functools.partial(final_kernel, inst_count - 1, starts), f32(own_pad, cells), [], 1,
        edge, mid, matrices, *received,
    )
    return out[:own] if own_pad != own else out


def solution(mesh):
    return jax.shard_map(
        per_device,
        mesh=mesh,
        in_specs=(
            P("inst", "cell"),
            P("inst", "cell"),
            P(None, "cell"),
            P(None, "cell"),
            P("cell"),
        ),
        out_specs=P("inst", "cell"),
        check_vma=False,
    )
```

```python
import functools

import jax
import jax.numpy as jnp
import numpy as np
from jax import lax
from jax.experimental import pallas as pl
from jax.experimental.pallas import tpu as pltpu
from jax.sharding import PartitionSpec as P


NI = 16
COMP = 5
NEIGH = 4
PLANE = 256
FREQ = 0.15
RELAX = 0.6
KEEP = 1.0 - RELAX

LANES = 128
PB = PLANE // LANES
MODES = 16


def up8(count):
    return -(-count // 8) * 8


def row_map(own):
    rows = [divmod(r, COMP) for r in range(own)]
    rows += [None] * (up8(own) - own)
    other = NI * COMP - own
    rows += [divmod(own + r, COMP) for r in range(other)]
    rows += [None] * (up8(other) - other)
    return rows


def mode_row(h, c):
    if h:
        return 8 * (h - 1) + 3 + c
    return c if c < 3 else 5 + c


def split_matrix(matrix):
    high = matrix.astype(jnp.bfloat16)
    low = (matrix - high.astype(np.float64)).astype(jnp.bfloat16)
    return np.concatenate([high, low, high], axis=1)


def constants(own, inst_count):
    rows = row_map(own)
    own_pad = up8(own)
    count = len(rows)
    derive = np.zeros((count, count))
    restrict = np.zeros((MODES, count))
    prolong = np.zeros((count, MODES))
    for i, left in enumerate(rows):
        if left is None:
            continue
        n, c = left
        phase = 2.0 * np.pi * n / NI
        shape = (1.0, np.cos(phase), np.sin(phase))
        for h in range(3):
            restrict[mode_row(h, c), i] = shape[h] * (1.0 if h == 0 else 2.0) / NI
            prolong[i, mode_row(h, c)] = shape[h]
        for j, right in enumerate(rows):
            if right is not None and right[1] == c and right[0] != n:
                gap = n - right[0]
                derive[i, j] = 0.5 * (-1.0) ** gap / np.tan(np.pi * gap / NI)
    other = prolong[own_pad:]
    lifts = []
    for k in range(1, inst_count):
        lift = np.zeros((own_pad, MODES))
        lift[:own] = other[(k - 1) * own : k * own]
        lifts.append(lift)
    parts = [derive[:, :own_pad], np.concatenate([derive, restrict]), restrict[:, :own_pad], prolong]
    parts += lifts
    width = -(-3 * count // LANES) * LANES
    blocks, starts, at = [], [], 0
    for part in parts:
        wide = split_matrix(part)
        height = -(-wide.shape[0] // 16) * 16
        blocks.append(np.pad(wide, ((0, height - wide.shape[0]), (0, width - wide.shape[1]))))
        starts.append(at)
        at += height
    return np.concatenate(blocks), starts, count


def split3(values):
    high = values.astype(jnp.bfloat16).astype(jnp.float32)
    return jnp.concatenate([values, values, values - high], axis=0).astype(jnp.bfloat16)


def dot(matrix, values):
    return jnp.dot(matrix, split3(values), preferred_element_type=jnp.float32)


def matrix_of(ref, start, height, depth):
    return ref[start : start + height, 0 : 3 * depth]


def lanes(start, count=1):
    return slice(start * LANES, (start + count) * LANES)


def build_table(idx_ref, wt_ref, at, near, bw, bf):
    target = near + lax.broadcasted_iota(jnp.int32, near.shape, 1)
    slot = lax.broadcasted_iota(jnp.int32, near.shape, 0)
    base = (target >> 7) + jnp.where((slot & 1) == 0, PB, 0)
    idx_ref[at, 0:NEIGH, :] = target & (LANES - 1)
    for j in range(PB + 1):
        wt_ref[at, NEIGH * j : NEIGH * (j + 1), :] = jnp.where(base == j, bw, 0.0)
    wt_ref[at, NEIGH * (PB + 1) : NEIGH * (PB + 1) + 1, :] = bf


def coefficient(table):
    _, wt_ref, at = table
    return wt_ref[at, pl.ds(NEIGH * (PB + 1), 8, stride=0), :]


def stencil(read, block, table, groups, known=None):
    idx_ref, wt_ref, at = table
    sums, cache = [None] * len(groups), {}

    def source(g, b):
        if (g, b) not in cache:
            cache[g, b] = read(g, b)
        return cache[g, b]

    for k in range(NEIGH):
        index = None
        for j in range(PB + 1):
            b = block + j - (0 if k % 2 else PB)
            if known is not None and not known(b):
                continue
            if index is None:
                index = idx_ref[at, pl.ds(k, 8, stride=0), :]
            weight = wt_ref[at, pl.ds(NEIGH * j + k, 8, stride=0), :]
            for i, g in enumerate(groups):
                term = weight * jnp.take_along_axis(source(g, b), index, axis=1)
                sums[i] = term if sums[i] is None else sums[i] + term
    return [0.0 if total is None else total for total in sums]


def turned(values, table, keep):
    top = lax.broadcasted_iota(jnp.int32, (8, LANES), 0) >= 3
    bf = jnp.where(top, coefficient(table), 0.0)
    low, high = values
    return keep * low - bf * high, keep * high + bf * low


def rows8(g):
    return slice(8 * g, 8 * g + 8)


MODE_GROUPS = list(range(MODES // 8))
NEAR, FAR, DEEP = range(PB), range(PB, 2 * PB), range(2 * PB, 3 * PB)


def halo_layout(own_pad):
    fine, mode = own_pad // 8 * PB, MODES // 8 * PB
    sizes = [fine, fine, mode, mode, mode, mode, 2 * PB, 1]
    starts = [sum(sizes[:i]) for i in range(len(sizes))]
    return starts, sum(sizes)


def pack_kernel(own_pad, starts, init_hbm, src_hbm, near_hbm, face_hbm, damp_hbm, matrix_hbm,
                a_ref, b_ref, init_ref, scaled_ref, mode_ref, edge_ref, idx_ref, wt_ref, matrix_ref,
                src_ref, near_ref, face_ref, damp_ref, coef_ref, m0, m1, m2, rp, sems):
    cells = init_ref.shape[1]
    nblk = cells // LANES
    half = own_pad // 16 * 8
    copies = [
        pltpu.make_async_copy(face_hbm, face_ref, sems.at[0]),
        pltpu.make_async_copy(damp_hbm, damp_ref, sems.at[1]),
        pltpu.make_async_copy(near_hbm, near_ref, sems.at[2]),
        pltpu.make_async_copy(src_hbm.at[0:half], src_ref.at[0:half], sems.at[3]),
        pltpu.make_async_copy(src_hbm.at[half:own_pad], src_ref.at[half:own_pad], sems.at[4]),
        pltpu.make_async_copy(init_hbm.at[0:half], init_ref.at[0:half], sems.at[5]),
        pltpu.make_async_copy(init_hbm.at[half:own_pad], init_ref.at[half:own_pad], sems.at[6]),
        pltpu.make_async_copy(matrix_hbm, matrix_ref, sems.at[7]),
    ]
    for copy in copies:
        copy.start()
    for copy in copies[0:3]:
        copy.wait()
    face = face_ref[...]
    inverse = RELAX / (damp_ref[...] + jnp.sum(face, axis=0, keepdims=True))
    coef_ref[0:NEIGH, :] = inverse * face
    coef_ref[NEIGH : NEIGH + 1, :] = FREQ * inverse
    for b in range(nblk):
        build_table(idx_ref, wt_ref, b, near_ref[:, lanes(b)],
                    coef_ref[0:NEIGH, lanes(b)], coef_ref[NEIGH : NEIGH + 1, lanes(b)])
    for copy in copies[3:]:
        copy.wait()
    groups = list(range(own_pad // 8))
    for g in groups:
        scaled_ref[rows8(g), :] = src_ref[rows8(g), :] * inverse
    restrict = matrix_of(matrix_ref, starts[2], MODES, own_pad)
    for d in range(0, nblk, 2):
        m0[:, lanes(d, 2)] = dot(restrict, init_ref[:, lanes(d, 2)])
    for d in range(0, nblk, 2):
        mode_ref[:, lanes(d, 2)] = dot(restrict, scaled_ref[:, lanes(d, 2)])

    def table(b):
        return idx_ref, wt_ref, b

    def reader(ref, first=0):
        return lambda g, b: ref[rows8(g), lanes(b - first)]

    derive = matrix_of(matrix_ref, starts[0], own_pad, own_pad)
    for side in range(2):
        at = side * (nblk - PB)
        deriv = dot(derive, init_ref[:, lanes(at, PB)])
        for i in NEAR:
            b = at + i
            sums = stencil(reader(init_ref), b, table(b), groups, lambda s: 0 <= s < nblk)
            bf = coefficient(table(b))
            for g in groups:
                edge_ref[rows8(g), lanes(side * PB + i)] = (
                    KEEP * init_ref[rows8(g), lanes(b)]
                    + scaled_ref[rows8(g), lanes(b)]
                    - bf * deriv[rows8(g), lanes(i)]
                    + sums[g]
                )

    def modes(src, first, out, to, b, known, keep):
        sums = stencil(reader(src, first), b, table(b), MODE_GROUPS, known)
        parts = (0.0, 0.0)
        if keep is not None:
            parts = turned([src[rows8(g), lanes(b - first)] for g in MODE_GROUPS], table(b), keep)
        for g in MODE_GROUPS:
            out[rows8(g), lanes(to)] = parts[g] + sums[g] + mode_ref[rows8(g), lanes(b)]

    for b in range(PB, nblk - PB):
        modes(m0, 0, m1, b - PB, b, None, KEEP)
    for side in range(2):
        for d in list(FAR) + list(DEEP):
            b = nblk - 1 - d if side else d
            modes(m1, PB, m2, b - PB, b, lambda s: PB <= s < nblk - PB, KEEP)
    for side in range(2):
        for d in FAR:
            b = nblk - 1 - d if side else d
            deep = [nblk - 1 - e if side else e for e in DEEP]
            modes(m2, PB, rp, b - PB, b, lambda s, deep=deep: s in deep, None)

    near = near_ref[...].astype(jnp.float32)
    first_tiles, _ = halo_layout(own_pad)

    def pack(out, high):
        near_at = nblk - PB if high else 0
        far_at = nblk - 2 * PB if high else PB
        edge_at = PB if high else 0
        all_at = nblk - 2 * PB if high else 0
        for i in range(PB):
            for g in groups:
                out[first_tiles[0] + g * PB + i] = init_ref[rows8(g), lanes(near_at + i)]
                out[first_tiles[1] + g * PB + i] = edge_ref[rows8(g), lanes(edge_at + i)]
            for g in MODE_GROUPS:
                t = g * PB + i
                out[first_tiles[2] + t] = mode_ref[rows8(g), lanes(near_at + i)]
                out[first_tiles[3] + t] = m1[rows8(g), lanes(far_at + i - PB)]
                out[first_tiles[4] + t] = m2[rows8(g), lanes(far_at + i - PB)]
                out[first_tiles[5] + t] = rp[rows8(g), lanes(far_at + i - PB)]
        for i in range(2 * PB):
            out[first_tiles[6] + i, 0:NEIGH, :] = coef_ref[0:NEIGH, lanes(all_at + i)]
            out[first_tiles[6] + i, NEIGH : 2 * NEIGH, :] = near[:, lanes(all_at + i)]
            out[first_tiles[7], i : i + 1, :] = coef_ref[NEIGH : NEIGH + 1, lanes(all_at + i)]

    odd = lax.axis_index("cell") & 1

    @pl.when(odd == 0)
    def _():
        pack(a_ref, True)
        pack(b_ref, False)

    @pl.when(odd == 1)
    def _():
        pack(a_ref, False)
        pack(b_ref, True)


def inner_kernel(own_pad, rows, starts, init_ref, scaled_ref, smode_ref, idx_ref, wt_ref, matrix_ref,
                 own_ref, cross_ref, part_ref, cpart_ref, cend_ref, m2_ref, rp_ref,
                 first, deriv):
    cells = init_ref.shape[1]
    nblk = cells // LANES
    own_groups = list(range(own_pad // 8))
    cross_groups = list(range(own_pad // 8, rows // 8))

    def table(b):
        return idx_ref, wt_ref, b

    derive = matrix_of(matrix_ref, starts[0], rows, own_pad)
    for d in range(0, nblk, 2):
        deriv[:, lanes(d, 2)] = dot(derive, init_ref[:, lanes(d, 2)])

    def read_init(g, b):
        return init_ref[rows8(g), lanes(b)]

    def read_first(g, b):
        return first[rows8(g), lanes(b)]

    inside = range(PB, nblk - PB)
    for b in range(nblk):
        bf = coefficient(table(b))
        for g in cross_groups:
            first[rows8(g), lanes(b)] = -bf * deriv[rows8(g), lanes(b)]
        if b in inside:
            sums = stencil(read_init, b, table(b), own_groups)
            for g in own_groups:
                first[rows8(g), lanes(b)] = (
                    KEEP * init_ref[rows8(g), lanes(b)]
                    + scaled_ref[rows8(g), lanes(b)]
                    - bf * deriv[rows8(g), lanes(b)]
                    + sums[g]
                )
    derive = matrix_of(matrix_ref, starts[1], rows, rows)
    for d in range(PB, nblk - PB, 2):
        deriv[:, lanes(d, 2)] = dot(derive, first[:, lanes(d, 2)])

    def local(g, b):
        bf = coefficient(table(b))
        return KEEP * first[rows8(g), lanes(b)] - bf * deriv[rows8(g), lanes(b)]

    for b in range(nblk):
        sums = stencil(read_first, b, table(b), cross_groups, lambda s: 0 <= s < nblk)
        for g, total in zip(cross_groups, sums):
            part = rows8(g - len(own_groups))
            if b in inside:
                cross_ref[part, lanes(b - PB)] = local(g, b) + total
            else:
                at = lanes(b if b < PB else b - nblk + 2 * PB)
                cpart_ref[part, at] = total
                cend_ref[part, at] = first[rows8(g), lanes(b)]
    middle = range(2 * PB, nblk - 2 * PB)
    for b in range(nblk):
        sums = stencil(read_first, b, table(b), own_groups, lambda s: s in inside)
        for g, total in zip(own_groups, sums):
            if b in inside:
                total = total + local(g, b) + scaled_ref[rows8(g), lanes(b)]
            if b in middle:
                own_ref[rows8(g), lanes(b - 2 * PB)] = total
            else:
                part_ref[rows8(g), lanes(b if b < 2 * PB else b - nblk + 4 * PB)] = total
    restrict = matrix_of(matrix_ref, starts[1] + rows, MODES, rows)
    for d in range(0, nblk - 4 * PB, 2):
        values = jnp.concatenate([own_ref[:, lanes(d, 2)], cross_ref[:, lanes(PB + d, 2)]], axis=0)
        m2_ref[:, lanes(d, 2)] = dot(restrict, values)

    def read_m2(g, b):
        return m2_ref[rows8(g), lanes(b - 2 * PB)]

    for b in range(nblk):
        sums = stencil(read_m2, b, table(b), MODE_GROUPS, lambda s: s in middle)
        if b in middle:
            parts = turned([read_m2(g, b) for g in MODE_GROUPS], table(b), -RELAX)
            sums = [total + part for total, part in zip(sums, parts)]
        for g in MODE_GROUPS:
            rp_ref[rows8(g), lanes(b)] = sums[g] + smode_ref[rows8(g), lanes(b)]


def outer_kernel(own_pad, rows, starts, a_ref, b_ref, init_ref, scaled_ref, smode_ref, edge_ref,
                 own_ref, cross_ref, part_ref, cpart_ref, cend_ref, m2i_ref, rp_ref, idx_in, wt_in,
                 matrix_ref, base_ref, send_ref,
                 halo, v1, v2, deriv, m1x, m2x, rx, c1x, c2x, idx, wt):
    cells = init_ref.shape[1]
    nblk = cells // LANES
    lead = own_pad // 8
    own_groups = list(range(lead))
    cross_groups = list(range(lead, rows // 8))
    tiles, _ = halo_layout(own_pad)
    odd = lax.axis_index("cell") & 1

    @pl.when(odd == 0)
    def _():
        halo[1] = a_ref[...]
        halo[0] = b_ref[...]

    @pl.when(odd == 1)
    def _():
        halo[0] = a_ref[...]
        halo[1] = b_ref[...]

    def side_of(b):
        return (0, b + 2 * PB) if b < 0 else (1, b - nblk)

    for side in range(2):
        for i in range(2 * PB):
            tile = tiles[6] + i
            build_table(idx, wt, side * 2 * PB + i, halo[side, tile, NEIGH : 2 * NEIGH, :].astype(jnp.int32),
                        halo[side, tile, 0:NEIGH, :], halo[side, tiles[7], i : i + 1, :])

    def table(b):
        if 0 <= b < nblk:
            return idx_in, wt_in, b
        side, i = side_of(b)
        return idx, wt, side * 2 * PB + i

    def section(number, g, b, far=False):
        side, i = side_of(b)
        if (side == 1) == far:
            i -= PB
        return halo[side, tiles[number] + g * PB + i]

    def own(b):
        return 0 <= b < nblk

    def read_init(g, b):
        return init_ref[rows8(g), lanes(b)] if own(b) else section(0, g, b)

    ring = list(range(-PB, PB)) + list(range(nblk - PB, nblk + PB))
    place = {b: i for i, b in enumerate(ring)}

    def read_v1(g, b):
        return v1[rows8(g), lanes(place[b])]

    derive_cross = matrix_of(matrix_ref, starts[0], rows, own_pad)
    for side in range(2):
        first = nblk if side else -PB
        values = jnp.concatenate(
            [
                jnp.concatenate([section(0, g, first + i) for i in range(PB)], axis=1)
                for g in own_groups
            ],
            axis=0,
        )
        turn = dot(derive_cross, values)
        for i in range(PB):
            b = first + i
            bf = coefficient(table(b))
            for g in cross_groups:
                v1[rows8(g), lanes(place[b])] = -bf * turn[rows8(g), lanes(i)]
            sums = stencil(read_init, b, table(b), own_groups, own)
            for g in own_groups:
                v1[rows8(g), lanes(place[b])] = section(1, g, b) + sums[g]
        for i in range(PB):
            b = nblk - PB + i if side else i
            at = lanes(side * PB + i)
            sums = stencil(read_init, b, table(b), own_groups, lambda s: not own(s))
            for g in own_groups:
                v1[rows8(g), lanes(place[b])] = edge_ref[rows8(g), at] + sums[g]
            for g in cross_groups:
                v1[rows8(g), lanes(place[b])] = cend_ref[rows8(g - lead), at]
    both = matrix_of(matrix_ref, starts[1], rows + MODES, rows)
    restrict = matrix_of(matrix_ref, starts[1] + rows, MODES, rows)
    low = -2 * PB
    for side in range(2):
        b = nblk if side else -PB
        m1x[:, lanes(b - low, PB)] = dot(restrict, v1[:, lanes(place[b], PB)])
        b = nblk - PB if side else 0
        mixed = dot(both, v1[:, lanes(place[b], PB)])
        deriv[:, lanes(side * PB, PB)] = mixed[0:rows]
        m1x[:, lanes(b - low, PB)] = mixed[rows:]
    for b in list(range(-2 * PB, -PB)) + list(range(nblk + PB, nblk + 2 * PB)):
        for g in MODE_GROUPS:
            m1x[rows8(g), lanes(b - low)] = section(3, g, b, True)

    outer_own = list(range(2 * PB)) + list(range(nblk - 2 * PB, nblk))
    place2 = {b: i for i, b in enumerate(outer_own)}
    ends = list(range(PB)) + list(range(nblk - PB, nblk))
    for b in outer_own:
        at = lanes(place2[b])
        sums = stencil(read_v1, b, table(b), own_groups, lambda s: s in place)
        bf = coefficient(table(b))
        for g in own_groups:
            total = part_ref[rows8(g), at] + sums[g]
            if b in ends:
                total = total + (
                    KEEP * read_v1(g, b)
                    + scaled_ref[rows8(g), lanes(b)]
                    - bf * deriv[rows8(g), lanes(ends.index(b))]
                )
            v2[rows8(g), at] = total
        if b in ends:
            sums = stencil(read_v1, b, table(b), cross_groups, lambda s: not own(s))
        for i, g in enumerate(cross_groups):
            if b in ends:
                end = lanes(ends.index(b))
                v2[rows8(g), at] = (
                    cpart_ref[rows8(i), end] + sums[i] + KEEP * read_v1(g, b) - bf * deriv[rows8(g), end]
                )
            else:
                v2[rows8(g), at] = cross_ref[rows8(i), lanes(b - PB)]
    for d in range(0, 4 * PB, 2):
        m2x[:, lanes(outer_own[d] - low, 2)] = dot(restrict, v2[:, lanes(d, 2)])
    m2x[:, lanes(2 * PB - low, nblk - 4 * PB)] = m2i_ref[...]

    def reader(ref, first):
        return lambda g, b: ref[rows8(g), lanes(b - first)]

    def modes(src, first, b, keep, known=None):
        read = reader(src, first)
        sums = stencil(read, b, table(b), MODE_GROUPS, known)
        if keep is None:
            return sums
        parts = turned([read(g, b) for g in MODE_GROUPS], table(b), keep)
        return [total + part for total, part in zip(sums, parts)]

    near = list(range(-PB, 0)) + list(range(nblk, nblk + PB))
    far = list(range(-2 * PB, -PB)) + list(range(nblk + PB, nblk + 2 * PB))
    for b in far:
        sums = modes(m1x, low, b, None, lambda s: s in place)
        for g in MODE_GROUPS:
            m2x[rows8(g), lanes(b - low)] = section(4, g, b, True) + sums[g]
    for b in near:
        sums = modes(m1x, low, b, KEEP)
        for g in MODE_GROUPS:
            m2x[rows8(g), lanes(b - low)] = section(2, g, b) + sums[g]

    middle = range(2 * PB, nblk - 2 * PB)
    for b in range(-2 * PB, nblk + 2 * PB):
        if b in middle:
            sums = modes(m2x, low, b, None, lambda s: s not in middle)
        elif own(b):
            sums = modes(m2x, low, b, -RELAX, lambda s: s not in middle)
        else:
            sums = modes(m2x, low, b, -RELAX, lambda s: -2 * PB <= s < nblk + 2 * PB)
        for g in MODE_GROUPS:
            if own(b):
                ready = rp_ref[rows8(g), lanes(b)]
            else:
                ready = section(5, g, b, True) if b in far else section(2, g, b)
            rx[rows8(g), lanes(b - low)] = ready + sums[g]
    for b in range(-PB, nblk + PB):
        sums = modes(rx, low, b, KEEP)
        for g in MODE_GROUPS:
            c1x[rows8(g), lanes(b + PB)] = sums[g] + rx[rows8(g), lanes(b - low)]
    for b in range(nblk):
        sums = modes(c1x, -PB, b, KEEP)
        for g in MODE_GROUPS:
            c2x[rows8(g), lanes(b)] = sums[g] + rx[rows8(g), lanes(b - low)]

    prolong = matrix_of(matrix_ref, starts[3], rows, MODES)
    prolong_own = matrix_of(matrix_ref, starts[3], own_pad, MODES)
    cross = rows - own_pad
    for b in range(0, nblk, 2):
        values = c2x[:, lanes(b, 2)]
        if b in middle:
            base_ref[:, lanes(b, 2)] = own_ref[:, lanes(b - 2 * PB, 2)] + dot(prolong_own, values)
        elif b in ends:
            lifted = v2[:, lanes(place2[b], 2)] + dot(prolong, values)
            base_ref[:, lanes(b, 2)] = lifted[0:own_pad]
            send_ref[0:cross, lanes(ends.index(b), 2)] = lifted[own_pad:]
        else:
            base_ref[:, lanes(b, 2)] = v2[0:own_pad, lanes(place2[b], 2)] + dot(prolong_own, values)
        if b not in ends:
            fold, at = divmod(b - PB, 2 * PB)
            send_ref[cross + fold * MODES : cross + (fold + 1) * MODES, lanes(at, 2)] = values


def final_kernel(count, starts, base_ref, matrix_ref, *refs):
    out_ref = refs[-1]
    own_pad = base_ref.shape[0]
    nblk = out_ref.shape[1] // LANES
    early, late = refs[0 : 2 * count : 2], refs[1 : 2 * count : 2]
    ends = list(range(PB)) + list(range(nblk - PB, nblk))
    for b in range(0, nblk, 2):
        total = base_ref[:, lanes(b, 2)]
        for k in range(count):
            if b in ends:
                total = total + late[k][0:own_pad, lanes(ends.index(b), 2)]
            else:
                fold, at = divmod(b - PB, 2 * PB)
                lift = matrix_of(matrix_ref, starts[4 + k], own_pad, MODES)
                first = own_pad + fold * MODES
                total = (
                    total
                    + early[k][:, lanes(b - PB, 2)]
                    + dot(lift, late[k][first : first + MODES, lanes(at, 2)])
                )
        out_ref[:, lanes(b, 2)] = total


def vm(*shape):
    return pltpu.VMEM(shape, jnp.float32)


def f32(*shape):
    return jax.ShapeDtypeStruct(shape, jnp.float32)


def call(kernel, out_shape, scratch, cost_us, *args, fetch=False):
    whole = pl.BlockSpec(memory_space=pltpu.VMEM)
    single = not isinstance(out_shape, (tuple, list))
    return pl.pallas_call(
        kernel,
        out_shape=out_shape,
        in_specs=[pl.BlockSpec(memory_space=pltpu.HBM) if fetch else whole] * len(args),
        out_specs=whole if single else [whole] * len(out_shape),
        scratch_shapes=scratch,
        compiler_params=pltpu.CompilerParams(vmem_limit_bytes=16 * 1024 * 1024),
        cost_estimate=pl.CostEstimate(
            flops=int(cost_us * 1e8), bytes_accessed=int(cost_us * 3e6), transcendentals=0
        ),
    )(*args)


def per_device(initial, source, neighbors, face_weights, damping):
    own, cells = initial.shape
    nblk = cells // LANES
    inst_count = lax.axis_size("inst")
    cell_count = lax.axis_size("cell")
    own_pad = up8(own)
    matrices, starts, rows = constants(own, inst_count)
    matrices = jnp.asarray(matrices)
    cross = rows - own_pad
    if own_pad != own:
        initial = jnp.pad(initial, ((0, own_pad - own), (0, 0)))
        source = jnp.pad(source, ((0, own_pad - own), (0, 0)))
    _, tiles = halo_layout(own_pad)
    assert nblk >= 8 * PB and nblk % 2 == 0
    slots = NEIGH * (PB + 1) + 4
    folds = -(-(nblk - 2 * PB) // (2 * PB))

    def wide(height, blocks):
        return f32(height, blocks * LANES)

    def scratch(height, blocks):
        return vm(height, blocks * LANES)

    def int32(*shape):
        return jax.ShapeDtypeStruct(shape, jnp.int32)

    pack_a, pack_b, initial, scaled, smode, ends, idx, wt, matrices = call(
        functools.partial(pack_kernel, own_pad, starts),
        [f32(tiles, 8, LANES), f32(tiles, 8, LANES), wide(own_pad, nblk), wide(own_pad, nblk),
         wide(MODES, nblk), wide(own_pad, 2 * PB), int32(nblk, 8, LANES), f32(nblk, slots, LANES),
         jax.ShapeDtypeStruct(matrices.shape, matrices.dtype)],
        [scratch(own_pad, nblk), pltpu.VMEM((NEIGH, cells), jnp.int32), vm(NEIGH, cells), vm(1, cells),
         vm(8, cells), scratch(MODES, nblk), scratch(MODES, nblk - 2 * PB),
         scratch(MODES, nblk - 2 * PB), scratch(MODES, nblk - 2 * PB), pltpu.SemaphoreType.DMA((8,))],
        2,
        *[
            pltpu.with_memory_space_constraint(x, pltpu.HBM)
            for x in (initial, source, neighbors, face_weights, damping.reshape(1, cells), matrices)
        ],
        fetch=True,
    )
    near_pairs = [(i, i ^ 1) for i in range(cell_count) if i ^ 1 < cell_count]
    far_pairs = []
    for i in range(1, cell_count - 1, 2):
        far_pairs += [(i, i + 1), (i + 1, i)]
    halo_b = lax.ppermute(pack_b, "cell", far_pairs)
    halo_a = lax.ppermute(pack_a, "cell", near_pairs)

    own_mid, cross_mid, part, cpart, cend, m2, rp = call(
        functools.partial(inner_kernel, own_pad, rows, starts),
        [wide(own_pad, nblk - 4 * PB), wide(cross, nblk - 2 * PB), wide(own_pad, 4 * PB),
         wide(cross, 2 * PB), wide(cross, 2 * PB), wide(MODES, nblk - 4 * PB), wide(MODES, nblk)],
        [scratch(rows, nblk), scratch(rows, nblk)], 5,
        initial, scaled, smode, idx, wt, matrices,
    )

    def share(array, k):
        if cross == own_pad:
            return array
        part = lax.slice_in_dim(array, (k - 1) * own, k * own, axis=0)
        return jnp.pad(part, ((0, own_pad - own), (0, 0)))

    def shift(k):
        return [(i, (i + k) % inst_count) for i in range(inst_count)]

    early = [lax.ppermute(share(cross_mid, k), "inst", shift(k)) for k in range(1, inst_count)]

    base, send = call(
        functools.partial(outer_kernel, own_pad, rows, starts),
        [wide(own_pad, nblk), wide(cross + folds * MODES, 2 * PB)],
        [pltpu.VMEM((2, tiles, 8, LANES), jnp.float32), scratch(rows, 4 * PB), scratch(rows, 4 * PB),
         scratch(rows, 2 * PB), scratch(MODES, nblk + 4 * PB), scratch(MODES, nblk + 4 * PB),
         scratch(MODES, nblk + 4 * PB), scratch(MODES, nblk + 2 * PB), scratch(MODES, nblk),
         pltpu.VMEM((4 * PB, 8, LANES), jnp.int32), vm(4 * PB, slots, LANES)],
        8, halo_a, halo_b, initial, scaled, smode, ends, own_mid, cross_mid, part, cpart, cend, m2, rp,
        idx, wt, matrices,
    )

    def share_late(k):
        if cross == own_pad:
            return send
        return jnp.concatenate([share(send[:cross], k), send[cross:]], axis=0)

    late = [lax.ppermute(share_late(k), "inst", shift(k)) for k in range(1, inst_count)]
    received = [r for pair in zip(early, late) for r in pair]
    out = call(
        functools.partial(final_kernel, inst_count - 1, starts), f32(own_pad, cells), [], 1,
        base, matrices, *received,
    )
    return out[:own] if own_pad != own else out


def solution(mesh):
    return jax.shard_map(
        per_device,
        mesh=mesh,
        in_specs=(
            P("inst", "cell"),
            P("inst", "cell"),
            P(None, "cell"),
            P(None, "cell"),
            P("cell"),
        ),
        out_specs=P("inst", "cell"),
        check_vma=False,
    )
```

```python
import functools

import jax
import jax.numpy as jnp
import numpy as np
from jax import lax
from jax.experimental import pallas as pl
from jax.experimental.pallas import tpu as pltpu
from jax.sharding import PartitionSpec as P


NI = 16
COMP = 5
NEIGH = 4
PLANE = 256
FREQ = 0.15
RELAX = 0.6
KEEP = 1.0 - RELAX

LANES = 128
PB = PLANE // LANES
MODES = 16


def up8(count):
    return -(-count // 8) * 8


def row_map(own):
    rows = [divmod(r, COMP) for r in range(own)]
    rows += [None] * (up8(own) - own)
    other = NI * COMP - own
    rows += [divmod(own + r, COMP) for r in range(other)]
    rows += [None] * (up8(other) - other)
    return rows


def mode_row(h, c):
    if h:
        return 8 * (h - 1) + 3 + c
    return c if c < 3 else 5 + c


def split_matrix(matrix):
    high = matrix.astype(jnp.bfloat16)
    low = (matrix - high.astype(np.float64)).astype(jnp.bfloat16)
    return np.concatenate([high, low, high], axis=1)


def constants(own, inst_count):
    rows = row_map(own)
    own_pad = up8(own)
    count = len(rows)
    derive = np.zeros((count, count))
    restrict = np.zeros((MODES, count))
    prolong = np.zeros((count, MODES))
    for i, left in enumerate(rows):
        if left is None:
            continue
        n, c = left
        phase = 2.0 * np.pi * n / NI
        shape = (1.0, np.cos(phase), np.sin(phase))
        for h in range(3):
            restrict[mode_row(h, c), i] = shape[h] * (1.0 if h == 0 else 2.0) / NI
            prolong[i, mode_row(h, c)] = shape[h]
        for j, right in enumerate(rows):
            if right is not None and right[1] == c and right[0] != n:
                gap = n - right[0]
                derive[i, j] = 0.5 * (-1.0) ** gap / np.tan(np.pi * gap / NI)
    other = prolong[own_pad:]
    lifts = []
    for k in range(1, inst_count):
        lift = np.zeros((own_pad, MODES))
        lift[:own] = other[(k - 1) * own : k * own]
        lifts.append(lift)
    parts = [derive[:, :own_pad], np.concatenate([derive, restrict]), restrict[:, :own_pad], prolong]
    parts += lifts
    width = -(-3 * count // LANES) * LANES
    blocks, starts, at = [], [], 0
    for part in parts:
        wide = split_matrix(part)
        height = -(-wide.shape[0] // 16) * 16
        blocks.append(np.pad(wide, ((0, height - wide.shape[0]), (0, width - wide.shape[1]))))
        starts.append(at)
        at += height
    return np.concatenate(blocks), starts, count


def split3(values):
    high = values.astype(jnp.bfloat16).astype(jnp.float32)
    return jnp.concatenate([values, values, values - high], axis=0).astype(jnp.bfloat16)


def dot(matrix, values):
    return jnp.dot(matrix, split3(values), preferred_element_type=jnp.float32)


def matrix_of(ref, start, height, depth):
    return ref[start : start + height, 0 : 3 * depth]


def lanes(start, count=1):
    return slice(start * LANES, (start + count) * LANES)


def build_table(idx_ref, wt_ref, at, near, bw, bf):
    target = near + lax.broadcasted_iota(jnp.int32, near.shape, 1)
    slot = lax.broadcasted_iota(jnp.int32, near.shape, 0)
    base = (target >> 7) + jnp.where((slot & 1) == 0, PB, 0)
    idx_ref[at, 0:NEIGH, :] = target & (LANES - 1)
    for j in range(PB + 1):
        wt_ref[at, NEIGH * j : NEIGH * (j + 1), :] = jnp.where(base == j, bw, 0.0)
    wt_ref[at, NEIGH * (PB + 1) : NEIGH * (PB + 1) + 1, :] = bf


def coefficient(table):
    _, wt_ref, at = table
    return wt_ref[at, pl.ds(NEIGH * (PB + 1), 8, stride=0), :]


def stencil(read, block, table, groups, known=None):
    idx_ref, wt_ref, at = table
    sums, cache = [None] * len(groups), {}

    def source(g, b):
        if (g, b) not in cache:
            cache[g, b] = read(g, b)
        return cache[g, b]

    for k in range(NEIGH):
        index = None
        for j in range(PB + 1):
            b = block + j - (0 if k % 2 else PB)
            if known is not None and not known(b):
                continue
            if index is None:
                index = idx_ref[at, pl.ds(k, 8, stride=0), :]
            weight = wt_ref[at, pl.ds(NEIGH * j + k, 8, stride=0), :]
            for i, g in enumerate(groups):
                term = weight * jnp.take_along_axis(source(g, b), index, axis=1)
                sums[i] = term if sums[i] is None else sums[i] + term
    return [0.0 if total is None else total for total in sums]


def turned(values, table, keep):
    top = lax.broadcasted_iota(jnp.int32, (8, LANES), 0) >= 3
    bf = jnp.where(top, coefficient(table), 0.0)
    low, high = values
    return keep * low - bf * high, keep * high + bf * low


def rows8(g):
    return slice(8 * g, 8 * g + 8)


MODE_GROUPS = list(range(MODES // 8))
NEAR, FAR, DEEP = range(PB), range(PB, 2 * PB), range(2 * PB, 3 * PB)


def halo_layout(own_pad):
    fine, mode = own_pad // 8 * PB, MODES // 8 * PB
    sizes = [fine, fine, mode, mode, mode, mode, 2 * PB, 1]
    starts = [sum(sizes[:i]) for i in range(len(sizes))]
    return starts, sum(sizes)


def pack_kernel(own_pad, starts, init_hbm, src_hbm, near_hbm, face_hbm, damp_hbm, matrix_hbm,
                a_ref, b_ref, init_ref, scaled_ref, mode_ref, edge_ref, idx_ref, wt_ref, matrix_ref,
                src_ref, near_ref, face_ref, damp_ref, coef_ref, m0, m1, m2, rp, sems):
    cells = init_ref.shape[1]
    nblk = cells // LANES
    half = own_pad // 16 * 8
    copies = [
        pltpu.make_async_copy(face_hbm, face_ref, sems.at[0]),
        pltpu.make_async_copy(damp_hbm, damp_ref, sems.at[1]),
        pltpu.make_async_copy(near_hbm, near_ref, sems.at[2]),
        pltpu.make_async_copy(src_hbm.at[0:half], src_ref.at[0:half], sems.at[3]),
        pltpu.make_async_copy(src_hbm.at[half:own_pad], src_ref.at[half:own_pad], sems.at[4]),
        pltpu.make_async_copy(init_hbm.at[0:half], init_ref.at[0:half], sems.at[5]),
        pltpu.make_async_copy(init_hbm.at[half:own_pad], init_ref.at[half:own_pad], sems.at[6]),
        pltpu.make_async_copy(matrix_hbm, matrix_ref, sems.at[7]),
    ]
    for copy in copies:
        copy.start()
    for copy in copies[0:3]:
        copy.wait()
    face = face_ref[...]
    inverse = RELAX / (damp_ref[...] + jnp.sum(face, axis=0, keepdims=True))
    coef_ref[0:NEIGH, :] = inverse * face
    coef_ref[NEIGH : NEIGH + 1, :] = FREQ * inverse
    for b in range(nblk):
        build_table(idx_ref, wt_ref, b, near_ref[:, lanes(b)],
                    coef_ref[0:NEIGH, lanes(b)], coef_ref[NEIGH : NEIGH + 1, lanes(b)])
    for copy in copies[3:]:
        copy.wait()
    groups = list(range(own_pad // 8))
    for g in groups:
        scaled_ref[rows8(g), :] = src_ref[rows8(g), :] * inverse
    restrict = matrix_of(matrix_ref, starts[2], MODES, own_pad)
    for d in range(0, nblk, 2):
        m0[:, lanes(d, 2)] = dot(restrict, init_ref[:, lanes(d, 2)])
    for d in range(0, nblk, 2):
        mode_ref[:, lanes(d, 2)] = dot(restrict, scaled_ref[:, lanes(d, 2)])

    def table(b):
        return idx_ref, wt_ref, b

    def reader(ref, first=0):
        return lambda g, b: ref[rows8(g), lanes(b - first)]

    derive = matrix_of(matrix_ref, starts[0], own_pad, own_pad)
    for side in range(2):
        at = side * (nblk - PB)
        deriv = dot(derive, init_ref[:, lanes(at, PB)])
        for i in NEAR:
            b = at + i
            sums = stencil(reader(init_ref), b, table(b), groups, lambda s: 0 <= s < nblk)
            bf = coefficient(table(b))
            for g in groups:
                edge_ref[rows8(g), lanes(side * PB + i)] = (
                    KEEP * init_ref[rows8(g), lanes(b)]
                    + scaled_ref[rows8(g), lanes(b)]
                    - bf * deriv[rows8(g), lanes(i)]
                    + sums[g]
                )

    def modes(src, first, out, to, b, known, keep):
        sums = stencil(reader(src, first), b, table(b), MODE_GROUPS, known)
        parts = (0.0, 0.0)
        if keep is not None:
            parts = turned([src[rows8(g), lanes(b - first)] for g in MODE_GROUPS], table(b), keep)
        for g in MODE_GROUPS:
            out[rows8(g), lanes(to)] = parts[g] + sums[g] + mode_ref[rows8(g), lanes(b)]

    for b in range(PB, nblk - PB):
        modes(m0, 0, m1, b - PB, b, None, KEEP)
    for side in range(2):
        for d in list(FAR) + list(DEEP):
            b = nblk - 1 - d if side else d
            modes(m1, PB, m2, b - PB, b, lambda s: PB <= s < nblk - PB, KEEP)
    for side in range(2):
        for d in FAR:
            b = nblk - 1 - d if side else d
            deep = [nblk - 1 - e if side else e for e in DEEP]
            modes(m2, PB, rp, b - PB, b, lambda s, deep=deep: s in deep, None)

    near = near_ref[...].astype(jnp.float32)
    first_tiles, _ = halo_layout(own_pad)

    def pack(out, high):
        near_at = nblk - PB if high else 0
        far_at = nblk - 2 * PB if high else PB
        edge_at = PB if high else 0
        all_at = nblk - 2 * PB if high else 0
        for i in range(PB):
            for g in groups:
                out[first_tiles[0] + g * PB + i] = init_ref[rows8(g), lanes(near_at + i)]
                out[first_tiles[1] + g * PB + i] = edge_ref[rows8(g), lanes(edge_at + i)]
            for g in MODE_GROUPS:
                t = g * PB + i
                out[first_tiles[2] + t] = mode_ref[rows8(g), lanes(near_at + i)]
                out[first_tiles[3] + t] = m1[rows8(g), lanes(far_at + i - PB)]
                out[first_tiles[4] + t] = m2[rows8(g), lanes(far_at + i - PB)]
                out[first_tiles[5] + t] = rp[rows8(g), lanes(far_at + i - PB)]
        for i in range(2 * PB):
            out[first_tiles[6] + i, 0:NEIGH, :] = coef_ref[0:NEIGH, lanes(all_at + i)]
            out[first_tiles[6] + i, NEIGH : 2 * NEIGH, :] = near[:, lanes(all_at + i)]
            out[first_tiles[7], i : i + 1, :] = coef_ref[NEIGH : NEIGH + 1, lanes(all_at + i)]

    odd = lax.axis_index("cell") & 1

    @pl.when(odd == 0)
    def _():
        pack(a_ref, True)
        pack(b_ref, False)

    @pl.when(odd == 1)
    def _():
        pack(a_ref, False)
        pack(b_ref, True)


def cross_kernel(own_pad, rows, starts, init_ref, scaled_ref, idx_ref, wt_ref, matrix_ref,
                 cross_ref, first, deriv):
    cells = init_ref.shape[1]
    nblk = cells // LANES
    own_groups = list(range(own_pad // 8))
    cross_groups = list(range(own_pad // 8, rows // 8))

    def table(b):
        return idx_ref, wt_ref, b

    derive = matrix_of(matrix_ref, starts[0], rows, own_pad)
    for d in range(0, nblk, 2):
        deriv[:, lanes(d, 2)] = dot(derive, init_ref[:, lanes(d, 2)])

    def read_init(g, b):
        return init_ref[rows8(g), lanes(b)]

    def read_first(g, b):
        return first[rows8(g), lanes(b)]

    inside = range(PB, nblk - PB)
    for b in range(nblk):
        bf = coefficient(table(b))
        for g in cross_groups:
            first[rows8(g), lanes(b)] = -bf * deriv[rows8(g), lanes(b)]
        if b in inside:
            sums = stencil(read_init, b, table(b), own_groups)
            for g in own_groups:
                first[rows8(g), lanes(b)] = (
                    KEEP * init_ref[rows8(g), lanes(b)]
                    + scaled_ref[rows8(g), lanes(b)]
                    - bf * deriv[rows8(g), lanes(b)]
                    + sums[g]
                )
    derive = matrix_of(matrix_ref, starts[1], rows, rows)
    for d in range(PB, nblk - PB, 2):
        deriv[:, lanes(d, 2)] = dot(derive, first[:, lanes(d, 2)])
    for b in inside:
        sums = stencil(read_first, b, table(b), cross_groups)
        bf = coefficient(table(b))
        for g, total in zip(cross_groups, sums):
            cross_ref[rows8(g - len(own_groups)), lanes(b - PB)] = (
                KEEP * read_first(g, b) - bf * deriv[rows8(g), lanes(b)] + total
            )


def inner_kernel(own_pad, rows, starts, first, deriv, scaled_ref, smode_ref, cross_ref, idx_ref, wt_ref,
                 matrix_ref, own_ref, part_ref, cpart_ref, m2_ref, rp_ref):
    cells = scaled_ref.shape[1]
    nblk = cells // LANES
    own_groups = list(range(own_pad // 8))
    cross_groups = list(range(own_pad // 8, rows // 8))
    inside = range(PB, nblk - PB)
    middle = range(2 * PB, nblk - 2 * PB)

    def table(b):
        return idx_ref, wt_ref, b

    def read_first(g, b):
        return first[rows8(g), lanes(b)]

    for b in range(nblk):
        bf = coefficient(table(b))
        sums = stencil(read_first, b, table(b), own_groups, lambda s: s in inside)
        for g, total in zip(own_groups, sums):
            if b in inside:
                total = total + (
                    KEEP * read_first(g, b) - bf * deriv[rows8(g), lanes(b)] + scaled_ref[rows8(g), lanes(b)]
                )
            if b in middle:
                own_ref[rows8(g), lanes(b - 2 * PB)] = total
            else:
                part_ref[rows8(g), lanes(b if b < 2 * PB else b - nblk + 4 * PB)] = total
    restrict = matrix_of(matrix_ref, starts[1] + rows, MODES, rows)
    for d in range(0, nblk - 4 * PB, 2):
        values = jnp.concatenate([own_ref[:, lanes(d, 2)], cross_ref[:, lanes(PB + d, 2)]], axis=0)
        m2_ref[:, lanes(d, 2)] = dot(restrict, values)
    for b in list(range(PB)) + list(range(nblk - PB, nblk)):
        sums = stencil(read_first, b, table(b), cross_groups, lambda s: 0 <= s < nblk)
        for g, total in zip(cross_groups, sums):
            part = rows8(g - len(own_groups))
            cpart_ref[part, lanes(b if b < PB else b - nblk + 2 * PB)] = total

    def read_m2(g, b):
        return m2_ref[rows8(g), lanes(b - 2 * PB)]

    for b in range(nblk):
        sums = stencil(read_m2, b, table(b), MODE_GROUPS, lambda s: s in middle)
        if b in middle:
            parts = turned([read_m2(g, b) for g in MODE_GROUPS], table(b), -RELAX)
            sums = [total + part for total, part in zip(sums, parts)]
        for g in MODE_GROUPS:
            rp_ref[rows8(g), lanes(b)] = sums[g] + smode_ref[rows8(g), lanes(b)]


def outer_kernel(own_pad, rows, starts, a_ref, b_ref, init_ref, scaled_ref, smode_ref, edge_ref,
                 own_ref, cross_ref, part_ref, cpart_ref, first_ref, m2i_ref, rp_ref, idx_in, wt_in,
                 matrix_ref, base_ref, send_ref,
                 halo, v1, v2, deriv, m1x, m2x, rx, c1x, c2x, idx, wt):
    cells = init_ref.shape[1]
    nblk = cells // LANES
    lead = own_pad // 8
    own_groups = list(range(lead))
    cross_groups = list(range(lead, rows // 8))
    tiles, _ = halo_layout(own_pad)
    odd = lax.axis_index("cell") & 1

    @pl.when(odd == 0)
    def _():
        halo[1] = a_ref[...]
        halo[0] = b_ref[...]

    @pl.when(odd == 1)
    def _():
        halo[0] = a_ref[...]
        halo[1] = b_ref[...]

    def side_of(b):
        return (0, b + 2 * PB) if b < 0 else (1, b - nblk)

    for side in range(2):
        for i in range(2 * PB):
            tile = tiles[6] + i
            build_table(idx, wt, side * 2 * PB + i, halo[side, tile, NEIGH : 2 * NEIGH, :].astype(jnp.int32),
                        halo[side, tile, 0:NEIGH, :], halo[side, tiles[7], i : i + 1, :])

    def table(b):
        if 0 <= b < nblk:
            return idx_in, wt_in, b
        side, i = side_of(b)
        return idx, wt, side * 2 * PB + i

    def section(number, g, b, far=False):
        side, i = side_of(b)
        if (side == 1) == far:
            i -= PB
        return halo[side, tiles[number] + g * PB + i]

    def own(b):
        return 0 <= b < nblk

    def read_init(g, b):
        return init_ref[rows8(g), lanes(b)] if own(b) else section(0, g, b)

    ring = list(range(-PB, PB)) + list(range(nblk - PB, nblk + PB))
    place = {b: i for i, b in enumerate(ring)}

    def read_v1(g, b):
        return v1[rows8(g), lanes(place[b])]

    derive_cross = matrix_of(matrix_ref, starts[0], rows, own_pad)
    for side in range(2):
        first = nblk if side else -PB
        values = jnp.concatenate(
            [
                jnp.concatenate([section(0, g, first + i) for i in range(PB)], axis=1)
                for g in own_groups
            ],
            axis=0,
        )
        turn = dot(derive_cross, values)
        for i in range(PB):
            b = first + i
            bf = coefficient(table(b))
            for g in cross_groups:
                v1[rows8(g), lanes(place[b])] = -bf * turn[rows8(g), lanes(i)]
            sums = stencil(read_init, b, table(b), own_groups, own)
            for g in own_groups:
                v1[rows8(g), lanes(place[b])] = section(1, g, b) + sums[g]
        for i in range(PB):
            b = nblk - PB + i if side else i
            at = lanes(side * PB + i)
            sums = stencil(read_init, b, table(b), own_groups, lambda s: not own(s))
            for g in own_groups:
                v1[rows8(g), lanes(place[b])] = edge_ref[rows8(g), at] + sums[g]
            for g in cross_groups:
                v1[rows8(g), lanes(place[b])] = first_ref[rows8(g), lanes(b)]
    both = matrix_of(matrix_ref, starts[1], rows + MODES, rows)
    restrict = matrix_of(matrix_ref, starts[1] + rows, MODES, rows)
    low = -2 * PB
    for side in range(2):
        b = nblk if side else -PB
        m1x[:, lanes(b - low, PB)] = dot(restrict, v1[:, lanes(place[b], PB)])
        b = nblk - PB if side else 0
        mixed = dot(both, v1[:, lanes(place[b], PB)])
        deriv[:, lanes(side * PB, PB)] = mixed[0:rows]
        m1x[:, lanes(b - low, PB)] = mixed[rows:]
    for b in list(range(-2 * PB, -PB)) + list(range(nblk + PB, nblk + 2 * PB)):
        for g in MODE_GROUPS:
            m1x[rows8(g), lanes(b - low)] = section(3, g, b, True)

    outer_own = list(range(2 * PB)) + list(range(nblk - 2 * PB, nblk))
    place2 = {b: i for i, b in enumerate(outer_own)}
    ends = list(range(PB)) + list(range(nblk - PB, nblk))
    for b in outer_own:
        at = lanes(place2[b])
        sums = stencil(read_v1, b, table(b), own_groups, lambda s: s in place)
        bf = coefficient(table(b))
        for g in own_groups:
            total = part_ref[rows8(g), at] + sums[g]
            if b in ends:
                total = total + (
                    KEEP * read_v1(g, b)
                    + scaled_ref[rows8(g), lanes(b)]
                    - bf * deriv[rows8(g), lanes(ends.index(b))]
                )
            v2[rows8(g), at] = total
        if b in ends:
            sums = stencil(read_v1, b, table(b), cross_groups, lambda s: not own(s))
        for i, g in enumerate(cross_groups):
            if b in ends:
                end = lanes(ends.index(b))
                v2[rows8(g), at] = (
                    cpart_ref[rows8(i), end] + sums[i] + KEEP * read_v1(g, b) - bf * deriv[rows8(g), end]
                )
            else:
                v2[rows8(g), at] = cross_ref[rows8(i), lanes(b - PB)]
    for d in range(0, 4 * PB, 2):
        m2x[:, lanes(outer_own[d] - low, 2)] = dot(restrict, v2[:, lanes(d, 2)])
    m2x[:, lanes(2 * PB - low, nblk - 4 * PB)] = m2i_ref[...]

    def reader(ref, first):
        return lambda g, b: ref[rows8(g), lanes(b - first)]

    def modes(src, first, b, keep, known=None):
        read = reader(src, first)
        sums = stencil(read, b, table(b), MODE_GROUPS, known)
        if keep is None:
            return sums
        parts = turned([read(g, b) for g in MODE_GROUPS], table(b), keep)
        return [total + part for total, part in zip(sums, parts)]

    near = list(range(-PB, 0)) + list(range(nblk, nblk + PB))
    far = list(range(-2 * PB, -PB)) + list(range(nblk + PB, nblk + 2 * PB))
    for b in far:
        sums = modes(m1x, low, b, None, lambda s: s in place)
        for g in MODE_GROUPS:
            m2x[rows8(g), lanes(b - low)] = section(4, g, b, True) + sums[g]
    for b in near:
        sums = modes(m1x, low, b, KEEP)
        for g in MODE_GROUPS:
            m2x[rows8(g), lanes(b - low)] = section(2, g, b) + sums[g]

    middle = range(2 * PB, nblk - 2 * PB)
    for b in range(-2 * PB, nblk + 2 * PB):
        if b in middle:
            sums = modes(m2x, low, b, None, lambda s: s not in middle)
        elif own(b):
            sums = modes(m2x, low, b, -RELAX, lambda s: s not in middle)
        else:
            sums = modes(m2x, low, b, -RELAX, lambda s: -2 * PB <= s < nblk + 2 * PB)
        for g in MODE_GROUPS:
            if own(b):
                ready = rp_ref[rows8(g), lanes(b)]
            else:
                ready = section(5, g, b, True) if b in far else section(2, g, b)
            rx[rows8(g), lanes(b - low)] = ready + sums[g]
    for b in range(-PB, nblk + PB):
        sums = modes(rx, low, b, KEEP)
        for g in MODE_GROUPS:
            c1x[rows8(g), lanes(b + PB)] = sums[g] + rx[rows8(g), lanes(b - low)]
    for b in range(nblk):
        sums = modes(c1x, -PB, b, KEEP)
        for g in MODE_GROUPS:
            c2x[rows8(g), lanes(b)] = sums[g] + rx[rows8(g), lanes(b - low)]

    prolong = matrix_of(matrix_ref, starts[3], rows, MODES)
    prolong_own = matrix_of(matrix_ref, starts[3], own_pad, MODES)
    cross = rows - own_pad
    for b in range(0, nblk, 2):
        values = c2x[:, lanes(b, 2)]
        if b in middle:
            base_ref[:, lanes(b, 2)] = own_ref[:, lanes(b - 2 * PB, 2)] + dot(prolong_own, values)
        elif b in ends:
            lifted = v2[:, lanes(place2[b], 2)] + dot(prolong, values)
            base_ref[:, lanes(b, 2)] = lifted[0:own_pad]
            send_ref[0:cross, lanes(ends.index(b), 2)] = lifted[own_pad:]
        else:
            base_ref[:, lanes(b, 2)] = v2[0:own_pad, lanes(place2[b], 2)] + dot(prolong_own, values)
        if b not in ends:
            fold, at = divmod(b - PB, 2 * PB)
            send_ref[cross + fold * MODES : cross + (fold + 1) * MODES, lanes(at, 2)] = values


def final_kernel(count, starts, base_ref, matrix_ref, *refs):
    out_hbm, out_ref, sems = refs[2 * count :]
    own_pad = base_ref.shape[0]
    nblk = out_ref.shape[1] // LANES
    early, late = refs[0 : 2 * count : 2], refs[1 : 2 * count : 2]
    copies = []
    ends = list(range(PB)) + list(range(nblk - PB, nblk))
    for b in range(0, nblk, 2):
        total = base_ref[:, lanes(b, 2)]
        for k in range(count):
            if b in ends:
                total = total + late[k][0:own_pad, lanes(ends.index(b), 2)]
            else:
                fold, at = divmod(b - PB, 2 * PB)
                lift = matrix_of(matrix_ref, starts[4 + k], own_pad, MODES)
                first = own_pad + fold * MODES
                total = (
                    total
                    + early[k][:, lanes(b - PB, 2)]
                    + dot(lift, late[k][first : first + MODES, lanes(at, 2)])
                )
        out_ref[:, lanes(b, 2)] = total
        if b % 4 == 2:
            piece = (slice(None), lanes(b - 2, 4))
            copies.append(pltpu.make_async_copy(out_ref.at[piece], out_hbm.at[piece], sems.at[b // 4]))
            copies[-1].start()
    for copy in copies:
        copy.wait()


def vm(*shape):
    return pltpu.VMEM(shape, jnp.float32)


def f32(*shape):
    return jax.ShapeDtypeStruct(shape, jnp.float32)


def call(kernel, out_shape, scratch, cost_us, *args, fetch=False, store=False):
    whole = pl.BlockSpec(memory_space=pltpu.VMEM)
    single = not isinstance(out_shape, (tuple, list))
    return pl.pallas_call(
        kernel,
        out_shape=out_shape,
        in_specs=[pl.BlockSpec(memory_space=pltpu.HBM) if fetch else whole] * len(args),
        out_specs=(pl.BlockSpec(memory_space=pltpu.HBM) if store else whole) if single else [whole] * len(out_shape),
        scratch_shapes=scratch,
        compiler_params=pltpu.CompilerParams(vmem_limit_bytes=16 * 1024 * 1024),
        cost_estimate=pl.CostEstimate(
            flops=int(cost_us * 1e8), bytes_accessed=int(cost_us * 3e6), transcendentals=0
        ),
    )(*args)


def per_device(initial, source, neighbors, face_weights, damping):
    own, cells = initial.shape
    nblk = cells // LANES
    inst_count = lax.axis_size("inst")
    cell_count = lax.axis_size("cell")
    own_pad = up8(own)
    matrices, starts, rows = constants(own, inst_count)
    matrices = jnp.asarray(matrices)
    cross = rows - own_pad
    if own_pad != own:
        initial = jnp.pad(initial, ((0, own_pad - own), (0, 0)))
        source = jnp.pad(source, ((0, own_pad - own), (0, 0)))
    _, tiles = halo_layout(own_pad)
    assert nblk >= 8 * PB and nblk % 4 == 0
    slots = NEIGH * (PB + 1) + 4
    folds = -(-(nblk - 2 * PB) // (2 * PB))

    def wide(height, blocks):
        return f32(height, blocks * LANES)

    def scratch(height, blocks):
        return vm(height, blocks * LANES)

    def int32(*shape):
        return jax.ShapeDtypeStruct(shape, jnp.int32)

    pack_a, pack_b, initial, scaled, smode, ends, idx, wt, matrices = call(
        functools.partial(pack_kernel, own_pad, starts),
        [f32(tiles, 8, LANES), f32(tiles, 8, LANES), wide(own_pad, nblk), wide(own_pad, nblk),
         wide(MODES, nblk), wide(own_pad, 2 * PB), int32(nblk, 8, LANES), f32(nblk, slots, LANES),
         jax.ShapeDtypeStruct(matrices.shape, matrices.dtype)],
        [scratch(own_pad, nblk), pltpu.VMEM((NEIGH, cells), jnp.int32), vm(NEIGH, cells), vm(1, cells),
         vm(8, cells), scratch(MODES, nblk), scratch(MODES, nblk - 2 * PB),
         scratch(MODES, nblk - 2 * PB), scratch(MODES, nblk - 2 * PB), pltpu.SemaphoreType.DMA((8,))],
        2,
        *[
            pltpu.with_memory_space_constraint(x, pltpu.HBM)
            for x in (initial, source, neighbors, face_weights, damping.reshape(1, cells), matrices)
        ],
        fetch=True,
    )
    near_pairs = [(i, i ^ 1) for i in range(cell_count) if i ^ 1 < cell_count]
    far_pairs = []
    for i in range(1, cell_count - 1, 2):
        far_pairs += [(i, i + 1), (i + 1, i)]
    halo_b = lax.ppermute(pack_b, "cell", far_pairs)
    halo_a = lax.ppermute(pack_a, "cell", near_pairs)

    cross_mid, first, deriv = call(
        functools.partial(cross_kernel, own_pad, rows, starts),
        [wide(cross, nblk - 2 * PB), wide(rows, nblk), wide(rows, nblk)], [], 3,
        initial, scaled, idx, wt, matrices,
    )

    def share(array, k):
        if cross == own_pad:
            return array
        part = lax.slice_in_dim(array, (k - 1) * own, k * own, axis=0)
        return jnp.pad(part, ((0, own_pad - own), (0, 0)))

    def shift(k):
        return [(i, (i + k) % inst_count) for i in range(inst_count)]

    early = [lax.ppermute(share(cross_mid, k), "inst", shift(k)) for k in range(1, inst_count)]

    own_mid, part, cpart, m2, rp = call(
        functools.partial(inner_kernel, own_pad, rows, starts),
        [wide(own_pad, nblk - 4 * PB), wide(own_pad, 4 * PB), wide(cross, 2 * PB),
         wide(MODES, nblk - 4 * PB), wide(MODES, nblk)], [], 3,
        first, deriv, scaled, smode, cross_mid, idx, wt, matrices,
    )
    base, send = call(
        functools.partial(outer_kernel, own_pad, rows, starts),
        [wide(own_pad, nblk), wide(cross + folds * MODES, 2 * PB)],
        [pltpu.VMEM((2, tiles, 8, LANES), jnp.float32), scratch(rows, 4 * PB), scratch(rows, 4 * PB),
         scratch(rows, 2 * PB), scratch(MODES, nblk + 4 * PB), scratch(MODES, nblk + 4 * PB),
         scratch(MODES, nblk + 4 * PB), scratch(MODES, nblk + 2 * PB), scratch(MODES, nblk),
         pltpu.VMEM((4 * PB, 8, LANES), jnp.int32), vm(4 * PB, slots, LANES)],
        8, halo_a, halo_b, initial, scaled, smode, ends, own_mid, cross_mid, part, cpart, first, m2, rp,
        idx, wt, matrices,
    )

    def share_late(k):
        if cross == own_pad:
            return send
        return jnp.concatenate([share(send[:cross], k), send[cross:]], axis=0)

    late = [lax.ppermute(share_late(k), "inst", shift(k)) for k in range(1, inst_count)]
    received = [r for pair in zip(early, late) for r in pair]
    out = call(
        functools.partial(final_kernel, inst_count - 1, starts), f32(own_pad, cells),
        [vm(own_pad, cells), pltpu.SemaphoreType.DMA((nblk // 4,))], 1,
        base, matrices, *received, store=True,
    )
    return out[:own] if own_pad != own else out


def solution(mesh):
    return jax.shard_map(
        per_device,
        mesh=mesh,
        in_specs=(
            P("inst", "cell"),
            P("inst", "cell"),
            P(None, "cell"),
            P(None, "cell"),
            P("cell"),
        ),
        out_specs=P("inst", "cell"),
        check_vma=False,
    )
```

```python
import functools

import jax
import jax.numpy as jnp
import numpy as np
from jax import lax
from jax.experimental import pallas as pl
from jax.experimental.pallas import tpu as pltpu
from jax.sharding import PartitionSpec as P


NI = 16
COMP = 5
NEIGH = 4
PLANE = 256
FREQ = 0.15
RELAX = 0.6
KEEP = 1.0 - RELAX

LANES = 128
PB = PLANE // LANES
MODES = 16


def up8(count):
    return -(-count // 8) * 8


def row_map(own):
    rows = [divmod(r, COMP) for r in range(own)]
    rows += [None] * (up8(own) - own)
    other = NI * COMP - own
    rows += [divmod(own + r, COMP) for r in range(other)]
    rows += [None] * (up8(other) - other)
    return rows


def mode_row(h, c):
    if h:
        return 8 * (h - 1) + 3 + c
    return c if c < 3 else 5 + c


def split_matrix(matrix):
    high = matrix.astype(jnp.bfloat16)
    low = (matrix - high.astype(np.float64)).astype(jnp.bfloat16)
    return np.concatenate([high, low, high], axis=1)


def constants(own, inst_count):
    rows = row_map(own)
    own_pad = up8(own)
    count = len(rows)
    derive = np.zeros((count, count))
    restrict = np.zeros((MODES, count))
    prolong = np.zeros((count, MODES))
    for i, left in enumerate(rows):
        if left is None:
            continue
        n, c = left
        phase = 2.0 * np.pi * n / NI
        shape = (1.0, np.cos(phase), np.sin(phase))
        for h in range(3):
            restrict[mode_row(h, c), i] = shape[h] * (1.0 if h == 0 else 2.0) / NI
            prolong[i, mode_row(h, c)] = shape[h]
        for j, right in enumerate(rows):
            if right is not None and right[1] == c and right[0] != n:
                gap = n - right[0]
                derive[i, j] = 0.5 * (-1.0) ** gap / np.tan(np.pi * gap / NI)
    other = prolong[own_pad:]
    lifts = []
    for k in range(1, inst_count):
        lift = np.zeros((own_pad, MODES))
        lift[:own] = other[(k - 1) * own : k * own]
        lifts.append(lift)
    parts = [derive[:, :own_pad], np.concatenate([derive, restrict]), restrict[:, :own_pad], prolong]
    parts += lifts
    width = -(-3 * count // LANES) * LANES
    blocks, starts, at = [], [], 0
    for part in parts:
        wide = split_matrix(part)
        height = -(-wide.shape[0] // 16) * 16
        blocks.append(np.pad(wide, ((0, height - wide.shape[0]), (0, width - wide.shape[1]))))
        starts.append(at)
        at += height
    return np.concatenate(blocks), starts, count


def split3(values):
    high = values.astype(jnp.bfloat16).astype(jnp.float32)
    return jnp.concatenate([values, values, values - high], axis=0).astype(jnp.bfloat16)


def dot(matrix, values):
    return jnp.dot(matrix, split3(values), preferred_element_type=jnp.float32)


def matrix_of(ref, start, height, depth):
    return ref[start : start + height, 0 : 3 * depth]


def lanes(start, count=1):
    return slice(start * LANES, (start + count) * LANES)


def build_table(idx_ref, wt_ref, at, near, bw, bf):
    target = near + lax.broadcasted_iota(jnp.int32, near.shape, 1)
    slot = lax.broadcasted_iota(jnp.int32, near.shape, 0)
    base = (target >> 7) + jnp.where((slot & 1) == 0, PB, 0)
    idx_ref[at, 0:NEIGH, :] = target & (LANES - 1)
    for j in range(PB + 1):
        wt_ref[at, NEIGH * j : NEIGH * (j + 1), :] = jnp.where(base == j, bw, 0.0)
    wt_ref[at, NEIGH * (PB + 1) : NEIGH * (PB + 1) + 1, :] = bf


def coefficient(table):
    _, wt_ref, at = table
    return wt_ref[at, pl.ds(NEIGH * (PB + 1), 8, stride=0), :]


def stencil(read, block, table, groups, known=None):
    idx_ref, wt_ref, at = table
    sums, cache = [None] * len(groups), {}

    def source(g, b):
        if (g, b) not in cache:
            cache[g, b] = read(g, b)
        return cache[g, b]

    for k in range(NEIGH):
        index = None
        for j in range(PB + 1):
            b = block + j - (0 if k % 2 else PB)
            if known is not None and not known(b):
                continue
            if index is None:
                index = idx_ref[at, pl.ds(k, 8, stride=0), :]
            weight = wt_ref[at, pl.ds(NEIGH * j + k, 8, stride=0), :]
            for i, g in enumerate(groups):
                term = weight * jnp.take_along_axis(source(g, b), index, axis=1)
                sums[i] = term if sums[i] is None else sums[i] + term
    return [0.0 if total is None else total for total in sums]


def turned(values, table, keep):
    top = lax.broadcasted_iota(jnp.int32, (8, LANES), 0) >= 3
    bf = jnp.where(top, coefficient(table), 0.0)
    low, high = values
    return keep * low - bf * high, keep * high + bf * low


def rows8(g):
    return slice(8 * g, 8 * g + 8)


MODE_GROUPS = list(range(MODES // 8))
NEAR, FAR, DEEP = range(PB), range(PB, 2 * PB), range(2 * PB, 3 * PB)


def halo_layout(own_pad):
    fine, mode = own_pad // 8 * PB, MODES // 8 * PB
    sizes = [fine, fine, mode, mode, mode, mode, 2 * PB, 1]
    starts = [sum(sizes[:i]) for i in range(len(sizes))]
    return starts, sum(sizes)


def pack_kernel(own_pad, starts, init_hbm, src_hbm, near_hbm, face_hbm, damp_hbm, matrix_hbm,
                a_ref, b_ref, init_ref, scaled_ref, mode_ref, edge_ref, m1, m2, idx_ref, wt_ref, matrix_ref,
                src_ref, near_ref, face_ref, damp_ref, coef_ref, m0, rp, sems):
    cells = init_ref.shape[1]
    nblk = cells // LANES
    half = own_pad // 16 * 8
    copies = [
        pltpu.make_async_copy(face_hbm, face_ref, sems.at[0]),
        pltpu.make_async_copy(damp_hbm, damp_ref, sems.at[1]),
        pltpu.make_async_copy(near_hbm, near_ref, sems.at[2]),
        pltpu.make_async_copy(src_hbm.at[0:half], src_ref.at[0:half], sems.at[3]),
        pltpu.make_async_copy(src_hbm.at[half:own_pad], src_ref.at[half:own_pad], sems.at[4]),
        pltpu.make_async_copy(init_hbm.at[0:half], init_ref.at[0:half], sems.at[5]),
        pltpu.make_async_copy(init_hbm.at[half:own_pad], init_ref.at[half:own_pad], sems.at[6]),
        pltpu.make_async_copy(matrix_hbm, matrix_ref, sems.at[7]),
    ]
    for copy in copies:
        copy.start()
    for copy in copies[0:3]:
        copy.wait()
    face = face_ref[...]
    inverse = RELAX / (damp_ref[...] + jnp.sum(face, axis=0, keepdims=True))
    coef_ref[0:NEIGH, :] = inverse * face
    coef_ref[NEIGH : NEIGH + 1, :] = FREQ * inverse
    for b in range(nblk):
        build_table(idx_ref, wt_ref, b, near_ref[:, lanes(b)],
                    coef_ref[0:NEIGH, lanes(b)], coef_ref[NEIGH : NEIGH + 1, lanes(b)])
    for copy in copies[3:]:
        copy.wait()
    groups = list(range(own_pad // 8))
    for g in groups:
        scaled_ref[rows8(g), :] = src_ref[rows8(g), :] * inverse
    restrict = matrix_of(matrix_ref, starts[2], MODES, own_pad)
    for d in range(0, nblk, 2):
        m0[:, lanes(d, 2)] = dot(restrict, init_ref[:, lanes(d, 2)])
    for d in range(0, nblk, 2):
        mode_ref[:, lanes(d, 2)] = dot(restrict, scaled_ref[:, lanes(d, 2)])

    def table(b):
        return idx_ref, wt_ref, b

    def reader(ref, first=0):
        return lambda g, b: ref[rows8(g), lanes(b - first)]

    derive = matrix_of(matrix_ref, starts[0], own_pad, own_pad)
    for side in range(2):
        at = side * (nblk - PB)
        deriv = dot(derive, init_ref[:, lanes(at, PB)])
        for i in NEAR:
            b = at + i
            sums = stencil(reader(init_ref), b, table(b), groups, lambda s: 0 <= s < nblk)
            bf = coefficient(table(b))
            for g in groups:
                edge_ref[rows8(g), lanes(side * PB + i)] = (
                    KEEP * init_ref[rows8(g), lanes(b)]
                    + scaled_ref[rows8(g), lanes(b)]
                    - bf * deriv[rows8(g), lanes(i)]
                    + sums[g]
                )

    def modes(src, first, out, to, b, known, keep):
        sums = stencil(reader(src, first), b, table(b), MODE_GROUPS, known)
        parts = (0.0, 0.0)
        if keep is not None:
            parts = turned([src[rows8(g), lanes(b - first)] for g in MODE_GROUPS], table(b), keep)
        for g in MODE_GROUPS:
            out[rows8(g), lanes(to)] = parts[g] + sums[g] + mode_ref[rows8(g), lanes(b)]

    for b in range(PB, nblk - PB):
        modes(m0, 0, m1, b - PB, b, None, KEEP)
    for side in range(2):
        for d in list(FAR) + list(DEEP):
            b = nblk - 1 - d if side else d
            modes(m1, PB, m2, b - PB, b, lambda s: PB <= s < nblk - PB, KEEP)
    for side in range(2):
        for d in FAR:
            b = nblk - 1 - d if side else d
            deep = [nblk - 1 - e if side else e for e in DEEP]
            modes(m2, PB, rp, b - PB, b, lambda s, deep=deep: s in deep, None)

    near = near_ref[...].astype(jnp.float32)
    first_tiles, _ = halo_layout(own_pad)

    def pack(out, high):
        near_at = nblk - PB if high else 0
        far_at = nblk - 2 * PB if high else PB
        edge_at = PB if high else 0
        all_at = nblk - 2 * PB if high else 0
        for i in range(PB):
            for g in groups:
                out[first_tiles[0] + g * PB + i] = init_ref[rows8(g), lanes(near_at + i)]
                out[first_tiles[1] + g * PB + i] = edge_ref[rows8(g), lanes(edge_at + i)]
            for g in MODE_GROUPS:
                t = g * PB + i
                out[first_tiles[2] + t] = mode_ref[rows8(g), lanes(near_at + i)]
                out[first_tiles[3] + t] = m1[rows8(g), lanes(far_at + i - PB)]
                out[first_tiles[4] + t] = m2[rows8(g), lanes(far_at + i - PB)]
                out[first_tiles[5] + t] = rp[rows8(g), lanes(far_at + i - PB)]
        for i in range(2 * PB):
            out[first_tiles[6] + i, 0:NEIGH, :] = coef_ref[0:NEIGH, lanes(all_at + i)]
            out[first_tiles[6] + i, NEIGH : 2 * NEIGH, :] = near[:, lanes(all_at + i)]
            out[first_tiles[7], i : i + 1, :] = coef_ref[NEIGH : NEIGH + 1, lanes(all_at + i)]

    odd = lax.axis_index("cell") & 1

    @pl.when(odd == 0)
    def _():
        pack(a_ref, True)
        pack(b_ref, False)

    @pl.when(odd == 1)
    def _():
        pack(a_ref, False)
        pack(b_ref, True)


def cross_kernel(own_pad, rows, starts, init_ref, scaled_ref, idx_ref, wt_ref, matrix_ref,
                 cross_ref, first, deriv):
    cells = init_ref.shape[1]
    nblk = cells // LANES
    own_groups = list(range(own_pad // 8))
    cross_groups = list(range(own_pad // 8, rows // 8))

    def table(b):
        return idx_ref, wt_ref, b

    derive = matrix_of(matrix_ref, starts[0], rows, own_pad)
    for d in range(0, nblk, 2):
        deriv[:, lanes(d, 2)] = dot(derive, init_ref[:, lanes(d, 2)])

    def read_init(g, b):
        return init_ref[rows8(g), lanes(b)]

    def read_first(g, b):
        return first[rows8(g), lanes(b)]

    inside = range(PB, nblk - PB)
    for b in range(nblk):
        bf = coefficient(table(b))
        for g in cross_groups:
            first[rows8(g), lanes(b)] = -bf * deriv[rows8(g), lanes(b)]
        if b in inside:
            sums = stencil(read_init, b, table(b), own_groups)
            for g in own_groups:
                first[rows8(g), lanes(b)] = (
                    KEEP * init_ref[rows8(g), lanes(b)]
                    + scaled_ref[rows8(g), lanes(b)]
                    - bf * deriv[rows8(g), lanes(b)]
                    + sums[g]
                )
    derive = matrix_of(matrix_ref, starts[1], rows, rows)
    for d in range(PB, nblk - PB, 2):
        deriv[:, lanes(d, 2)] = dot(derive, first[:, lanes(d, 2)])
    for b in inside:
        sums = stencil(read_first, b, table(b), cross_groups)
        bf = coefficient(table(b))
        for g, total in zip(cross_groups, sums):
            cross_ref[rows8(g - len(own_groups)), lanes(b - PB)] = (
                KEEP * read_first(g, b) - bf * deriv[rows8(g), lanes(b)] + total
            )


def inner_kernel(own_pad, rows, first, smode_ref, m1_ref, m2_ref, idx_ref, wt_ref,
                 cpart_ref, mpart_ref, m2_out, rp_ref):
    cells = smode_ref.shape[1]
    nblk = cells // LANES
    cross_groups = list(range(own_pad // 8, rows // 8))
    inside = range(PB, nblk - PB)
    middle = range(2 * PB, nblk - 2 * PB)
    ends = list(range(PB)) + list(range(nblk - PB, nblk))

    def table(b):
        return idx_ref, wt_ref, b

    def read_first(g, b):
        return first[rows8(g), lanes(b)]

    def read_m1(g, b):
        return m1_ref[rows8(g), lanes(b - PB)]

    def read_m2(g, b):
        return m2_out[rows8(g), lanes(b - PB)]

    m2_out[...] = m2_ref[...]
    for b in range(3 * PB, nblk - 3 * PB):
        sums = stencil(read_m1, b, table(b), MODE_GROUPS)
        parts = turned([read_m1(g, b) for g in MODE_GROUPS], table(b), KEEP)
        for g in MODE_GROUPS:
            m2_out[rows8(g), lanes(b - PB)] = parts[g] + sums[g] + smode_ref[rows8(g), lanes(b)]
    for i, b in enumerate(ends):
        sums = stencil(read_m1, b, table(b), MODE_GROUPS, lambda s: s in inside)
        for g in MODE_GROUPS:
            mpart_ref[rows8(g), lanes(i)] = sums[g] + smode_ref[rows8(g), lanes(b)]
    for i, b in enumerate(ends):
        sums = stencil(read_first, b, table(b), cross_groups, lambda s: 0 <= s < nblk)
        for g, total in zip(cross_groups, sums):
            cpart_ref[rows8(g - own_pad // 8), lanes(i)] = total
    for b in range(nblk):
        sums = stencil(read_m2, b, table(b), MODE_GROUPS, lambda s: s in middle)
        if b in middle:
            parts = turned([read_m2(g, b) for g in MODE_GROUPS], table(b), -RELAX)
            sums = [total + part for total, part in zip(sums, parts)]
        for g in MODE_GROUPS:
            rp_ref[rows8(g), lanes(b)] = sums[g] + smode_ref[rows8(g), lanes(b)]


def outer_kernel(own_pad, rows, starts, a_ref, b_ref, init_ref, smode_ref, edge_ref,
                 cpart_ref, mpart_ref, first_ref, m1i_ref, m2i_ref, rp_ref, idx_in, wt_in,
                 matrix_ref, send_ref, v1, deriv, c2x,
                 halo, v2, m1x, m2x, rx, c1x, idx, wt):
    cells = init_ref.shape[1]
    nblk = cells // LANES
    lead = own_pad // 8
    own_groups = list(range(lead))
    cross_groups = list(range(lead, rows // 8))
    tiles, _ = halo_layout(own_pad)
    odd = lax.axis_index("cell") & 1

    @pl.when(odd == 0)
    def _():
        halo[1] = a_ref[...]
        halo[0] = b_ref[...]

    @pl.when(odd == 1)
    def _():
        halo[0] = a_ref[...]
        halo[1] = b_ref[...]

    def side_of(b):
        return (0, b + 2 * PB) if b < 0 else (1, b - nblk)

    for side in range(2):
        for i in range(2 * PB):
            tile = tiles[6] + i
            build_table(idx, wt, side * 2 * PB + i, halo[side, tile, NEIGH : 2 * NEIGH, :].astype(jnp.int32),
                        halo[side, tile, 0:NEIGH, :], halo[side, tiles[7], i : i + 1, :])

    def table(b):
        if 0 <= b < nblk:
            return idx_in, wt_in, b
        side, i = side_of(b)
        return idx, wt, side * 2 * PB + i

    def section(number, g, b, far=False):
        side, i = side_of(b)
        if (side == 1) == far:
            i -= PB
        return halo[side, tiles[number] + g * PB + i]

    def own(b):
        return 0 <= b < nblk

    def read_init(g, b):
        return init_ref[rows8(g), lanes(b)] if own(b) else section(0, g, b)

    ring = list(range(-PB, PB)) + list(range(nblk - PB, nblk + PB))
    place = {b: i for i, b in enumerate(ring)}

    def read_v1(g, b):
        return v1[rows8(g), lanes(place[b])]

    derive_cross = matrix_of(matrix_ref, starts[0], rows, own_pad)
    for side in range(2):
        first = nblk if side else -PB
        values = jnp.concatenate(
            [
                jnp.concatenate([section(0, g, first + i) for i in range(PB)], axis=1)
                for g in own_groups
            ],
            axis=0,
        )
        turn = dot(derive_cross, values)
        for i in range(PB):
            b = first + i
            bf = coefficient(table(b))
            for g in cross_groups:
                v1[rows8(g), lanes(place[b])] = -bf * turn[rows8(g), lanes(i)]
            sums = stencil(read_init, b, table(b), own_groups, own)
            for g in own_groups:
                v1[rows8(g), lanes(place[b])] = section(1, g, b) + sums[g]
        for i in range(PB):
            b = nblk - PB + i if side else i
            at = lanes(side * PB + i)
            sums = stencil(read_init, b, table(b), own_groups, lambda s: not own(s))
            for g in own_groups:
                v1[rows8(g), lanes(place[b])] = edge_ref[rows8(g), at] + sums[g]
            for g in cross_groups:
                v1[rows8(g), lanes(place[b])] = first_ref[rows8(g), lanes(b)]
    both = matrix_of(matrix_ref, starts[1], rows + MODES, rows)
    restrict = matrix_of(matrix_ref, starts[1] + rows, MODES, rows)
    low = -2 * PB
    for side in range(2):
        b = nblk if side else -PB
        m1x[:, lanes(b - low, PB)] = dot(restrict, v1[:, lanes(place[b], PB)])
        b = nblk - PB if side else 0
        mixed = dot(both, v1[:, lanes(place[b], PB)])
        deriv[:, lanes(side * PB, PB)] = mixed[0:rows]
        m1x[:, lanes(b - low, PB)] = mixed[rows:]
    m1x[:, lanes(PB - low, nblk - 2 * PB)] = m1i_ref[...]
    for b in list(range(-2 * PB, -PB)) + list(range(nblk + PB, nblk + 2 * PB)):
        for g in MODE_GROUPS:
            m1x[rows8(g), lanes(b - low)] = section(3, g, b, True)

    ends = list(range(PB)) + list(range(nblk - PB, nblk))
    for i, b in enumerate(ends):
        at = lanes(i)
        sums = stencil(read_v1, b, table(b), cross_groups, lambda s: not own(s))
        bf = coefficient(table(b))
        for g, total in zip(cross_groups, sums):
            part = rows8(g - lead)
            v2[part, at] = cpart_ref[part, at] + total + KEEP * read_v1(g, b) - bf * deriv[rows8(g), at]

    def reader(ref, first):
        return lambda g, b: ref[rows8(g), lanes(b - first)]

    def modes(src, first, b, keep, known=None):
        read = reader(src, first)
        sums = stencil(read, b, table(b), MODE_GROUPS, known)
        if keep is None:
            return sums
        parts = turned([read(g, b) for g in MODE_GROUPS], table(b), keep)
        return [total + part for total, part in zip(sums, parts)]

    near = list(range(-PB, 0)) + list(range(nblk, nblk + PB))
    far = list(range(-2 * PB, -PB)) + list(range(nblk + PB, nblk + 2 * PB))
    for b in far:
        sums = modes(m1x, low, b, None, lambda s: s in place)
        for g in MODE_GROUPS:
            m2x[rows8(g), lanes(b - low)] = section(4, g, b, True) + sums[g]
    for b in near:
        sums = modes(m1x, low, b, KEEP)
        for g in MODE_GROUPS:
            m2x[rows8(g), lanes(b - low)] = section(2, g, b) + sums[g]
    for i, b in enumerate(ends):
        sums = modes(m1x, low, b, KEEP, lambda s: s in place)
        for g in MODE_GROUPS:
            m2x[rows8(g), lanes(b - low)] = mpart_ref[rows8(g), lanes(i)] + sums[g]
    m2x[:, lanes(2 * PB - low, nblk - 4 * PB)] = m2i_ref[:, lanes(PB, nblk - 4 * PB)]
    for b in list(range(PB, 2 * PB)) + list(range(nblk - 2 * PB, nblk - PB)):
        sums = modes(m1x, low, b, None, lambda s: s in place)
        for g in MODE_GROUPS:
            m2x[rows8(g), lanes(b - low)] = m2i_ref[rows8(g), lanes(b - PB)] + sums[g]

    middle = range(2 * PB, nblk - 2 * PB)
    for b in range(-2 * PB, nblk + 2 * PB):
        if b in middle:
            sums = modes(m2x, low, b, None, lambda s: s not in middle)
        elif own(b):
            sums = modes(m2x, low, b, -RELAX, lambda s: s not in middle)
        else:
            sums = modes(m2x, low, b, -RELAX, lambda s: -2 * PB <= s < nblk + 2 * PB)
        for g in MODE_GROUPS:
            if own(b):
                ready = rp_ref[rows8(g), lanes(b)]
            else:
                ready = section(5, g, b, True) if b in far else section(2, g, b)
            rx[rows8(g), lanes(b - low)] = ready + sums[g]
    for b in range(-PB, nblk + PB):
        sums = modes(rx, low, b, KEEP)
        for g in MODE_GROUPS:
            c1x[rows8(g), lanes(b + PB)] = sums[g] + rx[rows8(g), lanes(b - low)]
    for b in range(nblk):
        sums = modes(c1x, -PB, b, KEEP)
        for g in MODE_GROUPS:
            c2x[rows8(g), lanes(b)] = sums[g] + rx[rows8(g), lanes(b - low)]

    cross = rows - own_pad
    prolong = matrix_of(matrix_ref, starts[3] + own_pad, cross, MODES)
    for b in range(0, nblk, 2):
        values = c2x[:, lanes(b, 2)]
        if b in ends:
            at = lanes(ends.index(b), 2)
            send_ref[0:cross, at] = v2[:, at] + dot(prolong, values)
        else:
            fold, at = divmod(b - PB, 2 * PB)
            send_ref[cross + fold * MODES : cross + (fold + 1) * MODES, lanes(at, 2)] = values


def own_kernel(own_pad, starts, first, deriv, v1_ref, ends_ref, scaled_ref, c2_ref, idx_ref, wt_ref,
               matrix_ref, base_ref):
    cells = scaled_ref.shape[1]
    nblk = cells // LANES
    groups = list(range(own_pad // 8))
    ring = list(range(-PB, PB)) + list(range(nblk - PB, nblk + PB))
    ends = list(range(PB)) + list(range(nblk - PB, nblk))
    prolong = matrix_of(matrix_ref, starts[3], own_pad, MODES)

    def read(g, b):
        if b in ring:
            return v1_ref[rows8(g), lanes(ring.index(b))]
        return first[rows8(g), lanes(b)]

    for d in range(0, nblk, 2):
        lifted = dot(prolong, c2_ref[:, lanes(d, 2)])
        for b in range(d, d + 2):
            table = (idx_ref, wt_ref, b)
            bf = coefficient(table)
            sums = stencil(read, b, table, groups)
            for g in groups:
                if b in ends:
                    turn = ends_ref[rows8(g), lanes(ends.index(b))]
                else:
                    turn = deriv[rows8(g), lanes(b)]
                base_ref[rows8(g), lanes(b)] = (
                    KEEP * read(g, b)
                    + scaled_ref[rows8(g), lanes(b)]
                    - bf * turn
                    + sums[g]
                    + lifted[rows8(g), lanes(b - d)]
                )


def final_kernel(count, starts, base_ref, matrix_ref, *refs):
    out_hbm, out_ref, sems = refs[2 * count :]
    own_pad = base_ref.shape[0]
    nblk = out_ref.shape[1] // LANES
    early, late = refs[0 : 2 * count : 2], refs[1 : 2 * count : 2]
    copies = []
    ends = list(range(PB)) + list(range(nblk - PB, nblk))
    for b in range(0, nblk, 2):
        total = base_ref[:, lanes(b, 2)]
        for k in range(count):
            if b in ends:
                total = total + late[k][0:own_pad, lanes(ends.index(b), 2)]
            else:
                fold, at = divmod(b - PB, 2 * PB)
                lift = matrix_of(matrix_ref, starts[4 + k], own_pad, MODES)
                first = own_pad + fold * MODES
                total = (
                    total
                    + early[k][:, lanes(b - PB, 2)]
                    + dot(lift, late[k][first : first + MODES, lanes(at, 2)])
                )
        out_ref[:, lanes(b, 2)] = total
        if b % 4 == 2:
            piece = (slice(None), lanes(b - 2, 4))
            copies.append(pltpu.make_async_copy(out_ref.at[piece], out_hbm.at[piece], sems.at[b // 4]))
            copies[-1].start()
    for copy in copies:
        copy.wait()


def vm(*shape):
    return pltpu.VMEM(shape, jnp.float32)


def f32(*shape):
    return jax.ShapeDtypeStruct(shape, jnp.float32)


def call(kernel, out_shape, scratch, cost_us, *args, fetch=False, store=False):
    whole = pl.BlockSpec(memory_space=pltpu.VMEM)
    single = not isinstance(out_shape, (tuple, list))
    return pl.pallas_call(
        kernel,
        out_shape=out_shape,
        in_specs=[pl.BlockSpec(memory_space=pltpu.HBM) if fetch else whole] * len(args),
        out_specs=(pl.BlockSpec(memory_space=pltpu.HBM) if store else whole) if single else [whole] * len(out_shape),
        scratch_shapes=scratch,
        compiler_params=pltpu.CompilerParams(vmem_limit_bytes=16 * 1024 * 1024),
        cost_estimate=pl.CostEstimate(
            flops=int(cost_us * 1e8), bytes_accessed=int(cost_us * 3e6), transcendentals=0
        ),
    )(*args)


def per_device(initial, source, neighbors, face_weights, damping):
    own, cells = initial.shape
    nblk = cells // LANES
    inst_count = lax.axis_size("inst")
    cell_count = lax.axis_size("cell")
    own_pad = up8(own)
    matrices, starts, rows = constants(own, inst_count)
    matrices = jnp.asarray(matrices)
    cross = rows - own_pad
    if own_pad != own:
        initial = jnp.pad(initial, ((0, own_pad - own), (0, 0)))
        source = jnp.pad(source, ((0, own_pad - own), (0, 0)))
    _, tiles = halo_layout(own_pad)
    assert nblk >= 8 * PB and nblk % 4 == 0
    slots = NEIGH * (PB + 1) + 4
    folds = -(-(nblk - 2 * PB) // (2 * PB))

    def wide(height, blocks):
        return f32(height, blocks * LANES)

    def scratch(height, blocks):
        return vm(height, blocks * LANES)

    def int32(*shape):
        return jax.ShapeDtypeStruct(shape, jnp.int32)

    pack_a, pack_b, initial, scaled, smode, ends, m1, m2, idx, wt, matrices = call(
        functools.partial(pack_kernel, own_pad, starts),
        [f32(tiles, 8, LANES), f32(tiles, 8, LANES), wide(own_pad, nblk), wide(own_pad, nblk),
         wide(MODES, nblk), wide(own_pad, 2 * PB), wide(MODES, nblk - 2 * PB), wide(MODES, nblk - 2 * PB),
         int32(nblk, 8, LANES), f32(nblk, slots, LANES),
         jax.ShapeDtypeStruct(matrices.shape, matrices.dtype)],
        [scratch(own_pad, nblk), pltpu.VMEM((NEIGH, cells), jnp.int32), vm(NEIGH, cells), vm(1, cells),
         vm(8, cells), scratch(MODES, nblk), scratch(MODES, nblk - 2 * PB), pltpu.SemaphoreType.DMA((8,))],
        2,
        *[
            pltpu.with_memory_space_constraint(x, pltpu.HBM)
            for x in (initial, source, neighbors, face_weights, damping.reshape(1, cells), matrices)
        ],
        fetch=True,
    )
    near_pairs = [(i, i ^ 1) for i in range(cell_count) if i ^ 1 < cell_count]
    far_pairs = []
    for i in range(1, cell_count - 1, 2):
        far_pairs += [(i, i + 1), (i + 1, i)]
    halo_b = lax.ppermute(pack_b, "cell", far_pairs)
    halo_a = lax.ppermute(pack_a, "cell", near_pairs)

    cross_mid, first, deriv = call(
        functools.partial(cross_kernel, own_pad, rows, starts),
        [wide(cross, nblk - 2 * PB), wide(rows, nblk), wide(rows, nblk)], [], 3,
        initial, scaled, idx, wt, matrices,
    )

    def share(array, k):
        if cross == own_pad:
            return array
        part = lax.slice_in_dim(array, (k - 1) * own, k * own, axis=0)
        return jnp.pad(part, ((0, own_pad - own), (0, 0)))

    def shift(k):
        return [(i, (i + k) % inst_count) for i in range(inst_count)]

    early = [lax.ppermute(share(cross_mid, k), "inst", shift(k)) for k in range(1, inst_count)]

    cpart, mpart, m2, rp = call(
        functools.partial(inner_kernel, own_pad, rows),
        [wide(cross, 2 * PB), wide(MODES, 2 * PB), wide(MODES, nblk - 2 * PB), wide(MODES, nblk)], [], 3,
        first, smode, m1, m2, idx, wt,
    )
    send, v1, dends, c2 = call(
        functools.partial(outer_kernel, own_pad, rows, starts),
        [wide(cross + folds * MODES, 2 * PB), wide(rows, 4 * PB), wide(rows, 2 * PB), wide(MODES, nblk)],
        [pltpu.VMEM((2, tiles, 8, LANES), jnp.float32), scratch(cross, 2 * PB),
         scratch(MODES, nblk + 4 * PB), scratch(MODES, nblk + 4 * PB),
         scratch(MODES, nblk + 4 * PB), scratch(MODES, nblk + 2 * PB),
         pltpu.VMEM((4 * PB, 8, LANES), jnp.int32), vm(4 * PB, slots, LANES)],
        8, halo_a, halo_b, initial, smode, ends, cpart, mpart, first, m1, m2, rp, idx, wt, matrices,
    )

    def share_late(k):
        if cross == own_pad:
            return send
        return jnp.concatenate([share(send[:cross], k), send[cross:]], axis=0)

    late = [lax.ppermute(share_late(k), "inst", shift(k)) for k in range(1, inst_count)]
    base = call(
        functools.partial(own_kernel, own_pad, starts), wide(own_pad, nblk), [], 2,
        first, deriv, v1, dends, scaled, c2, idx, wt, matrices,
    )
    received = [r for pair in zip(early, late) for r in pair]
    out = call(
        functools.partial(final_kernel, inst_count - 1, starts), f32(own_pad, cells),
        [vm(own_pad, cells), pltpu.SemaphoreType.DMA((nblk // 4,))], 1,
        base, matrices, *received, store=True,
    )
    return out[:own] if own_pad != own else out


def solution(mesh):
    return jax.shard_map(
        per_device,
        mesh=mesh,
        in_specs=(
            P("inst", "cell"),
            P("inst", "cell"),
            P(None, "cell"),
            P(None, "cell"),
            P("cell"),
        ),
        out_specs=P("inst", "cell"),
        check_vma=False,
    )
```

```python
import functools

import jax
import jax.numpy as jnp
import numpy as np
from jax import lax
from jax.experimental import pallas as pl
from jax.experimental.pallas import tpu as pltpu
from jax.sharding import PartitionSpec as P


NI = 16
COMP = 5
NEIGH = 4
PLANE = 256
FREQ = 0.15
RELAX = 0.6
KEEP = 1.0 - RELAX

LANES = 128
PB = PLANE // LANES
MODES = 16


def up8(count):
    return -(-count // 8) * 8


def row_map(own):
    rows = [divmod(r, COMP) for r in range(own)]
    rows += [None] * (up8(own) - own)
    other = NI * COMP - own
    rows += [divmod(own + r, COMP) for r in range(other)]
    rows += [None] * (up8(other) - other)
    return rows


def mode_row(h, c):
    if h:
        return 8 * (h - 1) + 3 + c
    return c if c < 3 else 5 + c


def split_matrix(matrix):
    high = matrix.astype(jnp.bfloat16)
    low = (matrix - high.astype(np.float64)).astype(jnp.bfloat16)
    return np.concatenate([high, low, high], axis=1)


def constants(own, inst_count):
    rows = row_map(own)
    own_pad = up8(own)
    count = len(rows)
    derive = np.zeros((count, count))
    restrict = np.zeros((MODES, count))
    prolong = np.zeros((count, MODES))
    for i, left in enumerate(rows):
        if left is None:
            continue
        n, c = left
        phase = 2.0 * np.pi * n / NI
        shape = (1.0, np.cos(phase), np.sin(phase))
        for h in range(3):
            restrict[mode_row(h, c), i] = shape[h] * (1.0 if h == 0 else 2.0) / NI
            prolong[i, mode_row(h, c)] = shape[h]
        for j, right in enumerate(rows):
            if right is not None and right[1] == c and right[0] != n:
                gap = n - right[0]
                derive[i, j] = 0.5 * (-1.0) ** gap / np.tan(np.pi * gap / NI)
    other = prolong[own_pad:]
    lifts = []
    for k in range(1, inst_count):
        lift = np.zeros((own_pad, MODES))
        lift[:own] = other[(k - 1) * own : k * own]
        lifts.append(lift)
    parts = [derive[:, :own_pad], np.concatenate([derive, restrict]), restrict[:, :own_pad], prolong]
    parts += lifts
    width = -(-3 * count // LANES) * LANES
    blocks, starts, at = [], [], 0
    for part in parts:
        wide = split_matrix(part)
        height = -(-wide.shape[0] // 16) * 16
        blocks.append(np.pad(wide, ((0, height - wide.shape[0]), (0, width - wide.shape[1]))))
        starts.append(at)
        at += height
    return np.concatenate(blocks), starts, count


def split3(values):
    high = values.astype(jnp.bfloat16).astype(jnp.float32)
    return jnp.concatenate([values, values, values - high], axis=0).astype(jnp.bfloat16)


def dot(matrix, values):
    return jnp.dot(matrix, split3(values), preferred_element_type=jnp.float32)


def matrix_of(ref, start, height, depth):
    return ref[start : start + height, 0 : 3 * depth]


def lanes(start, count=1):
    return slice(start * LANES, (start + count) * LANES)


def build_table(idx_ref, wt_ref, at, near, bw, bf):
    target = near + lax.broadcasted_iota(jnp.int32, near.shape, 1)
    slot = lax.broadcasted_iota(jnp.int32, near.shape, 0)
    base = (target >> 7) + jnp.where((slot & 1) == 0, PB, 0)
    idx_ref[at, 0:NEIGH, :] = target & (LANES - 1)
    idx_ref[at, NEIGH : 2 * NEIGH, :] = target & (LANES - 1)
    for j in range(PB + 1):
        wt_ref[at, NEIGH * j : NEIGH * (j + 1), :] = jnp.where(base == j, bw, 0.0)
    wt_ref[at, NEIGH * (PB + 1) : NEIGH * (PB + 1) + 1, :] = bf


def build_product(ut_ref, at, table, block, coefs):
    idx_ref, wt_ref, to = table
    even = (lax.broadcasted_iota(jnp.int32, (8, LANES), 0) & 1) == 0
    for j in range(PB + 1):
        low = jnp.broadcast_to(coefs(block + j - PB), (8, LANES))
        high = jnp.broadcast_to(coefs(block + j), (8, LANES))
        taken = jnp.take_along_axis(jnp.where(even, low, high), idx_ref[to], axis=1)
        part = slice(NEIGH * j, NEIGH * (j + 1))
        ut_ref[at, part, :] = wt_ref[to, part, :] * taken[0:NEIGH]


def coefficient(table):
    _, wt_ref, at = table
    return wt_ref[at, pl.ds(NEIGH * (PB + 1), 8, stride=0), :]


def stencil(read, block, table, groups, known=None, product=None):
    idx_ref, wt_ref, at = table
    sums, others, cache = [0.0] * len(groups), [0.0] * len(groups), {}

    def source(g, b):
        if (g, b) not in cache:
            cache[g, b] = read(g, b)
        return cache[g, b]

    for k in range(NEIGH):
        index = None
        for j in range(PB + 1):
            b = block + j - (0 if k % 2 else PB)
            if known is not None and not known(b):
                continue
            if index is None:
                index = idx_ref[at, pl.ds(k, 8, stride=0), :]
            row = pl.ds(NEIGH * j + k, 8, stride=0)
            weight = wt_ref[at, row, :]
            if product is not None:
                other = product[0][product[1], row, :]
            for i, g in enumerate(groups):
                taken = jnp.take_along_axis(source(g, b), index, axis=1)
                sums[i] = sums[i] + weight * taken
                if product is not None:
                    others[i] = others[i] + other * taken
    return sums if product is None else (sums, others)


def turned(values, table, keep):
    top = lax.broadcasted_iota(jnp.int32, (8, LANES), 0) >= 3
    bf = jnp.where(top, coefficient(table), 0.0)
    low, high = values
    return keep * low - bf * high, keep * high + bf * low


def rows8(g):
    return slice(8 * g, 8 * g + 8)


MODE_GROUPS = list(range(MODES // 8))
NEAR, FAR, DEEP = range(PB), range(PB, 2 * PB), range(2 * PB, 3 * PB)


def halo_layout(own_pad):
    fine, mode = own_pad // 8 * PB, MODES // 8 * PB
    sizes = [fine, fine, mode, mode, mode, mode, 2 * PB, 1]
    starts = [sum(sizes[:i]) for i in range(len(sizes))]
    return starts, sum(sizes)


def pack_kernel(own_pad, starts, init_hbm, src_hbm, near_hbm, face_hbm, damp_hbm, matrix_hbm,
                a_ref, b_ref, init_ref, scaled_ref, mode_ref, edge_ref, push_ref, m1, m2, idx_ref, wt_ref, matrix_ref,
                src_ref, near_ref, face_ref, damp_ref, coef_ref, m0, rp, ut, sems):
    cells = init_ref.shape[1]
    nblk = cells // LANES
    half = own_pad // 16 * 8
    copies = [
        pltpu.make_async_copy(face_hbm, face_ref, sems.at[0]),
        pltpu.make_async_copy(damp_hbm, damp_ref, sems.at[1]),
        pltpu.make_async_copy(near_hbm, near_ref, sems.at[2]),
        pltpu.make_async_copy(src_hbm.at[0:half], src_ref.at[0:half], sems.at[3]),
        pltpu.make_async_copy(src_hbm.at[half:own_pad], src_ref.at[half:own_pad], sems.at[4]),
        pltpu.make_async_copy(init_hbm.at[0:half], init_ref.at[0:half], sems.at[5]),
        pltpu.make_async_copy(init_hbm.at[half:own_pad], init_ref.at[half:own_pad], sems.at[6]),
        pltpu.make_async_copy(matrix_hbm, matrix_ref, sems.at[7]),
    ]
    for copy in copies:
        copy.start()
    for copy in copies[0:3]:
        copy.wait()
    face = face_ref[...]
    inverse = RELAX / (damp_ref[...] + jnp.sum(face, axis=0, keepdims=True))
    coef_ref[0:NEIGH, :] = inverse * face
    coef_ref[NEIGH : NEIGH + 1, :] = FREQ * inverse
    for b in range(nblk):
        build_table(idx_ref, wt_ref, b, near_ref[:, lanes(b)],
                    coef_ref[0:NEIGH, lanes(b)], coef_ref[NEIGH : NEIGH + 1, lanes(b)])
    for copy in copies[3:]:
        copy.wait()
    groups = list(range(own_pad // 8))
    for g in groups:
        scaled_ref[rows8(g), :] = src_ref[rows8(g), :] * inverse
    restrict = matrix_of(matrix_ref, starts[2], MODES, own_pad)
    for d in range(0, nblk, 2):
        m0[:, lanes(d, 2)] = dot(restrict, init_ref[:, lanes(d, 2)])
    for d in range(0, nblk, 2):
        mode_ref[:, lanes(d, 2)] = dot(restrict, scaled_ref[:, lanes(d, 2)])

    def table(b):
        return idx_ref, wt_ref, b

    def reader(ref, first=0):
        return lambda g, b: ref[rows8(g), lanes(b - first)]

    derive = matrix_of(matrix_ref, starts[0], own_pad, own_pad)
    for side in range(2):
        at = side * (nblk - PB)
        deriv = dot(derive, init_ref[:, lanes(at, PB)])
        for i in NEAR:
            b = at + i
            at2 = side * PB + i

            def coefs(s):
                if not 0 <= s < nblk:
                    return jnp.zeros((1, LANES), jnp.float32)
                return coef_ref[NEIGH : NEIGH + 1, lanes(s)]

            build_product(ut, at2, table(b), b, coefs)
            sums, pushes = stencil(
                reader(init_ref), b, table(b), groups, lambda s: 0 <= s < nblk, (ut, at2)
            )
            bf = coefficient(table(b))
            for g in groups:
                push_ref[rows8(g), lanes(at2)] = pushes[g]
                edge_ref[rows8(g), lanes(side * PB + i)] = (
                    KEEP * init_ref[rows8(g), lanes(b)]
                    + scaled_ref[rows8(g), lanes(b)]
                    - bf * deriv[rows8(g), lanes(i)]
                    + sums[g]
                )

    def modes(src, first, out, to, b, known, keep):
        sums = stencil(reader(src, first), b, table(b), MODE_GROUPS, known)
        parts = (0.0, 0.0)
        if keep is not None:
            parts = turned([src[rows8(g), lanes(b - first)] for g in MODE_GROUPS], table(b), keep)
        for g in MODE_GROUPS:
            out[rows8(g), lanes(to)] = parts[g] + sums[g] + mode_ref[rows8(g), lanes(b)]

    for b in range(PB, nblk - PB):
        modes(m0, 0, m1, b - PB, b, None, KEEP)
    for side in range(2):
        for d in list(FAR) + list(DEEP):
            b = nblk - 1 - d if side else d
            modes(m1, PB, m2, b - PB, b, lambda s: PB <= s < nblk - PB, KEEP)
    for side in range(2):
        for d in FAR:
            b = nblk - 1 - d if side else d
            deep = [nblk - 1 - e if side else e for e in DEEP]
            modes(m2, PB, rp, b - PB, b, lambda s, deep=deep: s in deep, None)

    near = near_ref[...].astype(jnp.float32)
    first_tiles, _ = halo_layout(own_pad)

    def pack(out, high):
        near_at = nblk - PB if high else 0
        far_at = nblk - 2 * PB if high else PB
        edge_at = PB if high else 0
        all_at = nblk - 2 * PB if high else 0
        for i in range(PB):
            for g in groups:
                out[first_tiles[0] + g * PB + i] = init_ref[rows8(g), lanes(near_at + i)]
                out[first_tiles[1] + g * PB + i] = edge_ref[rows8(g), lanes(edge_at + i)]
            for g in MODE_GROUPS:
                t = g * PB + i
                out[first_tiles[2] + t] = mode_ref[rows8(g), lanes(near_at + i)]
                out[first_tiles[3] + t] = m1[rows8(g), lanes(far_at + i - PB)]
                out[first_tiles[4] + t] = m2[rows8(g), lanes(far_at + i - PB)]
                out[first_tiles[5] + t] = rp[rows8(g), lanes(far_at + i - PB)]
        for i in range(2 * PB):
            out[first_tiles[6] + i, 0:NEIGH, :] = coef_ref[0:NEIGH, lanes(all_at + i)]
            out[first_tiles[6] + i, NEIGH : 2 * NEIGH, :] = near[:, lanes(all_at + i)]
            out[first_tiles[7], i : i + 1, :] = coef_ref[NEIGH : NEIGH + 1, lanes(all_at + i)]

    odd = lax.axis_index("cell") & 1

    @pl.when(odd == 0)
    def _():
        pack(a_ref, True)
        pack(b_ref, False)

    @pl.when(odd == 1)
    def _():
        pack(a_ref, False)
        pack(b_ref, True)


def cross_kernel(own_pad, rows, starts, init_ref, scaled_ref, idx_ref, wt_ref, matrix_ref,
                 cross_ref, first, deriv, push, ut):
    cells = init_ref.shape[1]
    nblk = cells // LANES
    own_groups = list(range(own_pad // 8))
    cross_groups = list(range(own_pad // 8, rows // 8))

    def table(b):
        return idx_ref, wt_ref, b

    derive = matrix_of(matrix_ref, starts[0], rows, own_pad)
    for d in range(0, nblk, 2):
        deriv[:, lanes(d, 2)] = dot(derive, init_ref[:, lanes(d, 2)])

    def read_init(g, b):
        return init_ref[rows8(g), lanes(b)]

    def read_first(g, b):
        return first[rows8(g), lanes(b)]

    inside = range(PB, nblk - PB)

    def coefs(s):
        return wt_ref[s, NEIGH * (PB + 1) : NEIGH * (PB + 1) + 1, :]

    for b in range(nblk):
        bf = coefficient(table(b))
        for g in cross_groups:
            first[rows8(g), lanes(b)] = -bf * deriv[rows8(g), lanes(b)]
        if b in inside:
            build_product(ut, b - PB, table(b), b, coefs)
            sums, pushes = stencil(read_init, b, table(b), own_groups, None, (ut, b - PB))
            for g in own_groups:
                push[rows8(g), lanes(b - PB)] = pushes[g]
                first[rows8(g), lanes(b)] = (
                    KEEP * init_ref[rows8(g), lanes(b)]
                    + scaled_ref[rows8(g), lanes(b)]
                    - bf * deriv[rows8(g), lanes(b)]
                    + sums[g]
                )
    derive = matrix_of(matrix_ref, starts[1], rows, rows)
    couple = matrix_of(matrix_ref, starts[0] + own_pad, rows - own_pad, own_pad)
    for d in range(PB, nblk - PB, 2):
        deriv[:, lanes(d, 2)] = dot(derive, first[:, lanes(d, 2)])
        turn = dot(couple, push[:, lanes(d - PB, 2)])
        for b in range(d, d + 2):
            bf = coefficient(table(b))
            for g in cross_groups:
                part = rows8(g - len(own_groups))
                cross_ref[part, lanes(b - PB)] = (
                    KEEP * read_first(g, b) - bf * deriv[rows8(g), lanes(b)] - turn[part, lanes(b - d)]
                )


def inner_kernel(smode_ref, m1_ref, m2_ref, idx_ref, wt_ref, mpart_ref, m2_out, rp_ref):
    cells = smode_ref.shape[1]
    nblk = cells // LANES
    inside = range(PB, nblk - PB)
    middle = range(2 * PB, nblk - 2 * PB)
    ends = list(range(PB)) + list(range(nblk - PB, nblk))

    def table(b):
        return idx_ref, wt_ref, b

    def read_m1(g, b):
        return m1_ref[rows8(g), lanes(b - PB)]

    def read_m2(g, b):
        return m2_out[rows8(g), lanes(b - PB)]

    m2_out[...] = m2_ref[...]
    for b in range(3 * PB, nblk - 3 * PB):
        sums = stencil(read_m1, b, table(b), MODE_GROUPS)
        parts = turned([read_m1(g, b) for g in MODE_GROUPS], table(b), KEEP)
        for g in MODE_GROUPS:
            m2_out[rows8(g), lanes(b - PB)] = parts[g] + sums[g] + smode_ref[rows8(g), lanes(b)]
    for i, b in enumerate(ends):
        sums = stencil(read_m1, b, table(b), MODE_GROUPS, lambda s: s in inside)
        for g in MODE_GROUPS:
            mpart_ref[rows8(g), lanes(i)] = sums[g] + smode_ref[rows8(g), lanes(b)]
    for b in range(nblk):
        sums = stencil(read_m2, b, table(b), MODE_GROUPS, lambda s: s in middle)
        if b in middle:
            parts = turned([read_m2(g, b) for g in MODE_GROUPS], table(b), -RELAX)
            sums = [total + part for total, part in zip(sums, parts)]
        for g in MODE_GROUPS:
            rp_ref[rows8(g), lanes(b)] = sums[g] + smode_ref[rows8(g), lanes(b)]


def outer_kernel(own_pad, rows, starts, a_ref, b_ref, init_ref, smode_ref, edge_ref,
                 push_ref, mpart_ref, first_ref, m1i_ref, m2i_ref, rp_ref, idx_in, wt_in,
                 matrix_ref, send_ref, v1, deriv, c2x,
                 halo, v2, push, m1x, m2x, rx, c1x, idx, wt, ut):
    cells = init_ref.shape[1]
    nblk = cells // LANES
    lead = own_pad // 8
    own_groups = list(range(lead))
    cross_groups = list(range(lead, rows // 8))
    tiles, _ = halo_layout(own_pad)
    odd = lax.axis_index("cell") & 1

    @pl.when(odd == 0)
    def _():
        halo[1] = a_ref[...]
        halo[0] = b_ref[...]

    @pl.when(odd == 1)
    def _():
        halo[0] = a_ref[...]
        halo[1] = b_ref[...]

    def side_of(b):
        return (0, b + 2 * PB) if b < 0 else (1, b - nblk)

    for side in range(2):
        for i in range(2 * PB):
            tile = tiles[6] + i
            build_table(idx, wt, side * 2 * PB + i, halo[side, tile, NEIGH : 2 * NEIGH, :].astype(jnp.int32),
                        halo[side, tile, 0:NEIGH, :], halo[side, tiles[7], i : i + 1, :])

    def table(b):
        if 0 <= b < nblk:
            return idx_in, wt_in, b
        side, i = side_of(b)
        return idx, wt, side * 2 * PB + i

    def section(number, g, b, far=False):
        side, i = side_of(b)
        if (side == 1) == far:
            i -= PB
        return halo[side, tiles[number] + g * PB + i]

    def own(b):
        return 0 <= b < nblk

    def read_init(g, b):
        return init_ref[rows8(g), lanes(b)] if own(b) else section(0, g, b)

    ring = list(range(-PB, PB)) + list(range(nblk - PB, nblk + PB))
    place = {b: i for i, b in enumerate(ring)}

    def read_v1(g, b):
        return v1[rows8(g), lanes(place[b])]

    def coefs(b):
        if own(b):
            return jnp.zeros((1, LANES), jnp.float32)
        side, i = side_of(b)
        return halo[side, tiles[7], i : i + 1, :]

    derive_cross = matrix_of(matrix_ref, starts[0], rows, own_pad)
    for side in range(2):
        first = nblk if side else -PB
        values = jnp.concatenate(
            [
                jnp.concatenate([section(0, g, first + i) for i in range(PB)], axis=1)
                for g in own_groups
            ],
            axis=0,
        )
        turn = dot(derive_cross, values)
        for i in range(PB):
            b = first + i
            bf = coefficient(table(b))
            for g in cross_groups:
                v1[rows8(g), lanes(place[b])] = -bf * turn[rows8(g), lanes(i)]
            sums = stencil(read_init, b, table(b), own_groups, own)
            for g in own_groups:
                v1[rows8(g), lanes(place[b])] = section(1, g, b) + sums[g]
        for i in range(PB):
            b = nblk - PB + i if side else i
            at = lanes(side * PB + i)
            build_product(ut, side * PB + i, table(b), b, coefs)
            sums, pushes = stencil(
                read_init, b, table(b), own_groups, lambda s: not own(s), (ut, side * PB + i)
            )
            for g in own_groups:
                push[rows8(g), at] = push_ref[rows8(g), at] + pushes[g]
                v1[rows8(g), lanes(place[b])] = edge_ref[rows8(g), at] + sums[g]
            for g in cross_groups:
                v1[rows8(g), lanes(place[b])] = first_ref[rows8(g), lanes(b)]
    both = matrix_of(matrix_ref, starts[1], rows + MODES, rows)
    restrict = matrix_of(matrix_ref, starts[1] + rows, MODES, rows)
    low = -2 * PB
    for side in range(2):
        b = nblk if side else -PB
        m1x[:, lanes(b - low, PB)] = dot(restrict, v1[:, lanes(place[b], PB)])
        b = nblk - PB if side else 0
        mixed = dot(both, v1[:, lanes(place[b], PB)])
        deriv[:, lanes(side * PB, PB)] = mixed[0:rows]
        m1x[:, lanes(b - low, PB)] = mixed[rows:]
    m1x[:, lanes(PB - low, nblk - 2 * PB)] = m1i_ref[...]
    for b in list(range(-2 * PB, -PB)) + list(range(nblk + PB, nblk + 2 * PB)):
        for g in MODE_GROUPS:
            m1x[rows8(g), lanes(b - low)] = section(3, g, b, True)

    ends = list(range(PB)) + list(range(nblk - PB, nblk))
    couple = matrix_of(matrix_ref, starts[0] + own_pad, rows - own_pad, own_pad)
    for side in range(2):
        turn = dot(couple, push[:, lanes(side * PB, PB)])
        for i in range(PB):
            b, at = ends[side * PB + i], lanes(side * PB + i)
            bf = coefficient(table(b))
            for g in cross_groups:
                part = rows8(g - lead)
                v2[part, at] = KEEP * read_v1(g, b) - bf * deriv[rows8(g), at] - turn[part, lanes(i)]

    def reader(ref, first):
        return lambda g, b: ref[rows8(g), lanes(b - first)]

    def modes(src, first, b, keep, known=None):
        read = reader(src, first)
        sums = stencil(read, b, table(b), MODE_GROUPS, known)
        if keep is None:
            return sums
        parts = turned([read(g, b) for g in MODE_GROUPS], table(b), keep)
        return [total + part for total, part in zip(sums, parts)]

    near = list(range(-PB, 0)) + list(range(nblk, nblk + PB))
    far = list(range(-2 * PB, -PB)) + list(range(nblk + PB, nblk + 2 * PB))
    for b in far:
        sums = modes(m1x, low, b, None, lambda s: s in place)
        for g in MODE_GROUPS:
            m2x[rows8(g), lanes(b - low)] = section(4, g, b, True) + sums[g]
    for b in near:
        sums = modes(m1x, low, b, KEEP)
        for g in MODE_GROUPS:
            m2x[rows8(g), lanes(b - low)] = section(2, g, b) + sums[g]
    for i, b in enumerate(ends):
        sums = modes(m1x, low, b, KEEP, lambda s: s in place)
        for g in MODE_GROUPS:
            m2x[rows8(g), lanes(b - low)] = mpart_ref[rows8(g), lanes(i)] + sums[g]
    m2x[:, lanes(2 * PB - low, nblk - 4 * PB)] = m2i_ref[:, lanes(PB, nblk - 4 * PB)]
    for b in list(range(PB, 2 * PB)) + list(range(nblk - 2 * PB, nblk - PB)):
        sums = modes(m1x, low, b, None, lambda s: s in place)
        for g in MODE_GROUPS:
            m2x[rows8(g), lanes(b - low)] = m2i_ref[rows8(g), lanes(b - PB)] + sums[g]

    middle = range(2 * PB, nblk - 2 * PB)
    for b in range(-2 * PB, nblk + 2 * PB):
        if b in middle:
            sums = modes(m2x, low, b, None, lambda s: s not in middle)
        elif own(b):
            sums = modes(m2x, low, b, -RELAX, lambda s: s not in middle)
        else:
            sums = modes(m2x, low, b, -RELAX, lambda s: -2 * PB <= s < nblk + 2 * PB)
        for g in MODE_GROUPS:
            if own(b):
                ready = rp_ref[rows8(g), lanes(b)]
            else:
                ready = section(5, g, b, True) if b in far else section(2, g, b)
            rx[rows8(g), lanes(b - low)] = ready + sums[g]
    for b in range(-PB, nblk + PB):
        sums = modes(rx, low, b, KEEP)
        for g in MODE_GROUPS:
            c1x[rows8(g), lanes(b + PB)] = sums[g] + rx[rows8(g), lanes(b - low)]
    for b in range(nblk):
        sums = modes(c1x, -PB, b, KEEP)
        for g in MODE_GROUPS:
            c2x[rows8(g), lanes(b)] = sums[g] + rx[rows8(g), lanes(b - low)]

    cross = rows - own_pad
    prolong = matrix_of(matrix_ref, starts[3] + own_pad, cross, MODES)
    for b in range(0, nblk, 2):
        values = c2x[:, lanes(b, 2)]
        if b in ends:
            at = lanes(ends.index(b), 2)
            send_ref[0:cross, at] = v2[:, at] + dot(prolong, values)
        else:
            fold, at = divmod(b - PB, 2 * PB)
            send_ref[cross + fold * MODES : cross + (fold + 1) * MODES, lanes(at, 2)] = values


def own_kernel(own_pad, starts, first, deriv, v1_ref, ends_ref, scaled_ref, c2_ref, idx_ref, wt_ref,
               matrix_ref, base_ref):
    cells = scaled_ref.shape[1]
    nblk = cells // LANES
    groups = list(range(own_pad // 8))
    ring = list(range(-PB, PB)) + list(range(nblk - PB, nblk + PB))
    ends = list(range(PB)) + list(range(nblk - PB, nblk))
    prolong = matrix_of(matrix_ref, starts[3], own_pad, MODES)

    def read(g, b):
        if b in ring:
            return v1_ref[rows8(g), lanes(ring.index(b))]
        return first[rows8(g), lanes(b)]

    for d in range(0, nblk, 2):
        lifted = dot(prolong, c2_ref[:, lanes(d, 2)])
        for b in range(d, d + 2):
            table = (idx_ref, wt_ref, b)
            bf = coefficient(table)
            sums = stencil(read, b, table, groups)
            for g in groups:
                if b in ends:
                    turn = ends_ref[rows8(g), lanes(ends.index(b))]
                else:
                    turn = deriv[rows8(g), lanes(b)]
                base_ref[rows8(g), lanes(b)] = (
                    KEEP * read(g, b)
                    + scaled_ref[rows8(g), lanes(b)]
                    - bf * turn
                    + sums[g]
                    + lifted[rows8(g), lanes(b - d)]
                )


def final_kernel(count, starts, base_ref, matrix_ref, *refs):
    out_hbm, out_ref, sems = refs[2 * count :]
    own_pad = base_ref.shape[0]
    nblk = out_ref.shape[1] // LANES
    early, late = refs[0 : 2 * count : 2], refs[1 : 2 * count : 2]
    copies = []
    ends = list(range(PB)) + list(range(nblk - PB, nblk))
    for b in range(0, nblk, 2):
        total = base_ref[:, lanes(b, 2)]
        for k in range(count):
            if b in ends:
                total = total + late[k][0:own_pad, lanes(ends.index(b), 2)]
            else:
                fold, at = divmod(b - PB, 2 * PB)
                lift = matrix_of(matrix_ref, starts[4 + k], own_pad, MODES)
                first = own_pad + fold * MODES
                total = (
                    total
                    + early[k][:, lanes(b - PB, 2)]
                    + dot(lift, late[k][first : first + MODES, lanes(at, 2)])
                )
        out_ref[:, lanes(b, 2)] = total
        if b % 4 == 2:
            piece = (slice(None), lanes(b - 2, 4))
            copies.append(pltpu.make_async_copy(out_ref.at[piece], out_hbm.at[piece], sems.at[b // 4]))
            copies[-1].start()
    for copy in copies:
        copy.wait()


def vm(*shape):
    return pltpu.VMEM(shape, jnp.float32)


def f32(*shape):
    return jax.ShapeDtypeStruct(shape, jnp.float32)


def call(kernel, out_shape, scratch, cost_us, *args, fetch=False, store=False):
    whole = pl.BlockSpec(memory_space=pltpu.VMEM)
    single = not isinstance(out_shape, (tuple, list))
    return pl.pallas_call(
        kernel,
        out_shape=out_shape,
        in_specs=[pl.BlockSpec(memory_space=pltpu.HBM) if fetch else whole] * len(args),
        out_specs=(pl.BlockSpec(memory_space=pltpu.HBM) if store else whole) if single else [whole] * len(out_shape),
        scratch_shapes=scratch,
        compiler_params=pltpu.CompilerParams(vmem_limit_bytes=16 * 1024 * 1024),
        cost_estimate=pl.CostEstimate(
            flops=int(cost_us * 1e8), bytes_accessed=int(cost_us * 3e6), transcendentals=0
        ),
    )(*args)


def per_device(initial, source, neighbors, face_weights, damping):
    own, cells = initial.shape
    nblk = cells // LANES
    inst_count = lax.axis_size("inst")
    cell_count = lax.axis_size("cell")
    own_pad = up8(own)
    matrices, starts, rows = constants(own, inst_count)
    matrices = jnp.asarray(matrices)
    cross = rows - own_pad
    if own_pad != own:
        initial = jnp.pad(initial, ((0, own_pad - own), (0, 0)))
        source = jnp.pad(source, ((0, own_pad - own), (0, 0)))
    _, tiles = halo_layout(own_pad)
    assert nblk >= 8 * PB and nblk % 4 == 0
    slots = NEIGH * (PB + 1) + 4
    folds = -(-(nblk - 2 * PB) // (2 * PB))

    def wide(height, blocks):
        return f32(height, blocks * LANES)

    def scratch(height, blocks):
        return vm(height, blocks * LANES)

    def int32(*shape):
        return jax.ShapeDtypeStruct(shape, jnp.int32)

    pack_a, pack_b, initial, scaled, smode, ends, push, m1, m2, idx, wt, matrices = call(
        functools.partial(pack_kernel, own_pad, starts),
        [f32(tiles, 8, LANES), f32(tiles, 8, LANES), wide(own_pad, nblk), wide(own_pad, nblk),
         wide(MODES, nblk), wide(own_pad, 2 * PB), wide(own_pad, 2 * PB), wide(MODES, nblk - 2 * PB),
         wide(MODES, nblk - 2 * PB),
         int32(nblk, 8, LANES), f32(nblk, slots, LANES),
         jax.ShapeDtypeStruct(matrices.shape, matrices.dtype)],
        [scratch(own_pad, nblk), pltpu.VMEM((NEIGH, cells), jnp.int32), vm(NEIGH, cells), vm(1, cells),
         vm(8, cells), scratch(MODES, nblk), scratch(MODES, nblk - 2 * PB), vm(2 * PB, slots, LANES),
         pltpu.SemaphoreType.DMA((8,))],
        2,
        *[
            pltpu.with_memory_space_constraint(x, pltpu.HBM)
            for x in (initial, source, neighbors, face_weights, damping.reshape(1, cells), matrices)
        ],
        fetch=True,
    )
    near_pairs = [(i, i ^ 1) for i in range(cell_count) if i ^ 1 < cell_count]
    far_pairs = []
    for i in range(1, cell_count - 1, 2):
        far_pairs += [(i, i + 1), (i + 1, i)]
    halo_b = lax.ppermute(pack_b, "cell", far_pairs)
    halo_a = lax.ppermute(pack_a, "cell", near_pairs)

    cross_mid, first, deriv = call(
        functools.partial(cross_kernel, own_pad, rows, starts),
        [wide(cross, nblk - 2 * PB), wide(rows, nblk), wide(rows, nblk)],
        [scratch(own_pad, nblk - 2 * PB), vm(nblk - 2 * PB, slots, LANES)], 3,
        initial, scaled, idx, wt, matrices,
    )

    def share(array, k):
        if cross == own_pad:
            return array
        part = lax.slice_in_dim(array, (k - 1) * own, k * own, axis=0)
        return jnp.pad(part, ((0, own_pad - own), (0, 0)))

    def shift(k):
        return [(i, (i + k) % inst_count) for i in range(inst_count)]

    early = [lax.ppermute(share(cross_mid, k), "inst", shift(k)) for k in range(1, inst_count)]

    mpart, m2, rp = call(
        inner_kernel,
        [wide(MODES, 2 * PB), wide(MODES, nblk - 2 * PB), wide(MODES, nblk)], [], 3,
        smode, m1, m2, idx, wt,
    )
    send, v1, dends, c2 = call(
        functools.partial(outer_kernel, own_pad, rows, starts),
        [wide(cross + folds * MODES, 2 * PB), wide(rows, 4 * PB), wide(rows, 2 * PB), wide(MODES, nblk)],
        [pltpu.VMEM((2, tiles, 8, LANES), jnp.float32), scratch(cross, 2 * PB),
         scratch(own_pad, 2 * PB), scratch(MODES, nblk + 4 * PB), scratch(MODES, nblk + 4 * PB),
         scratch(MODES, nblk + 4 * PB), scratch(MODES, nblk + 2 * PB),
         pltpu.VMEM((4 * PB, 8, LANES), jnp.int32), vm(4 * PB, slots, LANES), vm(2 * PB, slots, LANES)],
        8, halo_a, halo_b, initial, smode, ends, push, mpart, first, m1, m2, rp, idx, wt, matrices,
    )

    def share_late(k):
        if cross == own_pad:
            return send
        return jnp.concatenate([share(send[:cross], k), send[cross:]], axis=0)

    late = [lax.ppermute(share_late(k), "inst", shift(k)) for k in range(1, inst_count)]
    base = call(
        functools.partial(own_kernel, own_pad, starts), wide(own_pad, nblk), [], 2,
        first, deriv, v1, dends, scaled, c2, idx, wt, matrices,
    )
    received = [r for pair in zip(early, late) for r in pair]
    out = call(
        functools.partial(final_kernel, inst_count - 1, starts), f32(own_pad, cells),
        [vm(own_pad, cells), pltpu.SemaphoreType.DMA((nblk // 4,))], 1,
        base, matrices, *received, store=True,
    )
    return out[:own] if own_pad != own else out


def solution(mesh):
    return jax.shard_map(
        per_device,
        mesh=mesh,
        in_specs=(
            P("inst", "cell"),
            P("inst", "cell"),
            P(None, "cell"),
            P(None, "cell"),
            P("cell"),
        ),
        out_specs=P("inst", "cell"),
        check_vma=False,
    )
```

```python
import functools

import jax
import jax.numpy as jnp
import numpy as np
from jax import lax
from jax.experimental import pallas as pl
from jax.experimental.pallas import tpu as pltpu
from jax.sharding import PartitionSpec as P


NI = 16
COMP = 5
NEIGH = 4
PLANE = 256
FREQ = 0.15
RELAX = 0.6
KEEP = 1.0 - RELAX

LANES = 128
PB = PLANE // LANES
MODES = 16


def up8(count):
    return -(-count // 8) * 8


def row_map(own):
    rows = [divmod(r, COMP) for r in range(own)]
    rows += [None] * (up8(own) - own)
    other = NI * COMP - own
    rows += [divmod(own + r, COMP) for r in range(other)]
    rows += [None] * (up8(other) - other)
    return rows


def mode_row(h, c):
    if h:
        return 8 * (h - 1) + 3 + c
    return c if c < 3 else 5 + c


def split_matrix(matrix):
    high = matrix.astype(jnp.bfloat16)
    low = (matrix - high.astype(np.float64)).astype(jnp.bfloat16)
    return np.concatenate([high, low, high], axis=1)


def constants(own, inst_count):
    rows = row_map(own)
    own_pad = up8(own)
    count = len(rows)
    derive = np.zeros((count, count))
    restrict = np.zeros((MODES, count))
    prolong = np.zeros((count, MODES))
    for i, left in enumerate(rows):
        if left is None:
            continue
        n, c = left
        phase = 2.0 * np.pi * n / NI
        shape = (1.0, np.cos(phase), np.sin(phase))
        for h in range(3):
            restrict[mode_row(h, c), i] = shape[h] * (1.0 if h == 0 else 2.0) / NI
            prolong[i, mode_row(h, c)] = shape[h]
        for j, right in enumerate(rows):
            if right is not None and right[1] == c and right[0] != n:
                gap = n - right[0]
                derive[i, j] = 0.5 * (-1.0) ** gap / np.tan(np.pi * gap / NI)
    other = prolong[own_pad:]
    lifts = []
    for k in range(1, inst_count):
        lift = np.zeros((own_pad, MODES))
        lift[:own] = other[(k - 1) * own : k * own]
        lifts.append(lift)
    early = [derive[:, :own_pad], restrict[:, :own_pad]]
    late = [np.concatenate([derive, restrict]), prolong] + lifts
    (lead, lead_starts), (rest, rest_starts) = stack(early), stack(late)
    starts = [lead_starts[0], rest_starts[0], lead_starts[1]] + rest_starts[1:]
    return lead, rest, starts, count


def stack(parts):
    wides = [split_matrix(part) for part in parts]
    width = -(-max(wide.shape[1] for wide in wides) // LANES) * LANES
    blocks, starts, at = [], [], 0
    for wide in wides:
        height = -(-wide.shape[0] // 16) * 16
        blocks.append(np.pad(wide, ((0, height - wide.shape[0]), (0, width - wide.shape[1]))))
        starts.append(at)
        at += height
    return np.concatenate(blocks), starts


def split3(values):
    high = values.astype(jnp.bfloat16).astype(jnp.float32)
    return jnp.concatenate([values, values, values - high], axis=0).astype(jnp.bfloat16)


def dot(matrix, values):
    return jnp.dot(matrix, split3(values), preferred_element_type=jnp.float32)


def matrix_of(ref, start, height, depth):
    return ref[start : start + height, 0 : 3 * depth]


def lanes(start, count=1):
    return slice(start * LANES, (start + count) * LANES)


def build_table(idx_ref, wt_ref, at, near, bw, bf):
    target = near + lax.broadcasted_iota(jnp.int32, near.shape, 1)
    slot = lax.broadcasted_iota(jnp.int32, near.shape, 0)
    base = (target >> 7) + jnp.where((slot & 1) == 0, PB, 0)
    idx_ref[at, 0:NEIGH, :] = target & (LANES - 1)
    idx_ref[at, NEIGH : 2 * NEIGH, :] = target & (LANES - 1)
    for j in range(PB + 1):
        wt_ref[at, NEIGH * j : NEIGH * (j + 1), :] = jnp.where(base == j, bw, 0.0)
    wt_ref[at, NEIGH * (PB + 1) : NEIGH * (PB + 1) + 1, :] = bf


def build_product(ut_ref, at, table, block, coefs):
    idx_ref, wt_ref, to = table
    even = (lax.broadcasted_iota(jnp.int32, (8, LANES), 0) & 1) == 0
    for j in range(PB + 1):
        low = jnp.broadcast_to(coefs(block + j - PB), (8, LANES))
        high = jnp.broadcast_to(coefs(block + j), (8, LANES))
        taken = jnp.take_along_axis(jnp.where(even, low, high), idx_ref[to], axis=1)
        part = slice(NEIGH * j, NEIGH * (j + 1))
        ut_ref[at, part, :] = wt_ref[to, part, :] * taken[0:NEIGH]


def coefficient(table):
    _, wt_ref, at = table
    return wt_ref[at, pl.ds(NEIGH * (PB + 1), 8, stride=0), :]


def stencil(read, block, table, groups, known=None, product=None):
    idx_ref, wt_ref, at = table
    sums, others, cache = [0.0] * len(groups), [0.0] * len(groups), {}

    def source(g, b):
        if (g, b) not in cache:
            cache[g, b] = read(g, b)
        return cache[g, b]

    for k in range(NEIGH):
        index = None
        for j in range(PB + 1):
            b = block + j - (0 if k % 2 else PB)
            if known is not None and not known(b):
                continue
            if index is None:
                index = idx_ref[at, pl.ds(k, 8, stride=0), :]
            row = pl.ds(NEIGH * j + k, 8, stride=0)
            weight = wt_ref[at, row, :]
            if product is not None:
                other = product[0][product[1], row, :]
            for i, g in enumerate(groups):
                taken = jnp.take_along_axis(source(g, b), index, axis=1)
                sums[i] = sums[i] + weight * taken
                if product is not None:
                    others[i] = others[i] + other * taken
    return sums if product is None else (sums, others)


def turned(values, table, keep):
    top = lax.broadcasted_iota(jnp.int32, (8, LANES), 0) >= 3
    bf = jnp.where(top, coefficient(table), 0.0)
    low, high = values
    return keep * low - bf * high, keep * high + bf * low


def rows8(g):
    return slice(8 * g, 8 * g + 8)


MODE_GROUPS = list(range(MODES // 8))


def halo_layout(own_pad):
    fine, mode = own_pad // 8 * PB, MODES // 8 * PB
    sizes = [fine, fine, mode, mode, mode, mode, 2 * PB, 1]
    starts = [sum(sizes[:i]) for i in range(len(sizes))]
    return starts, sum(sizes)


def pack_kernel(own_pad, starts, init_hbm, src_hbm, near_hbm, face_hbm, damp_hbm, lead_hbm, matrix_hbm,
                a_ref, b_ref, init_ref, scaled_ref, mode_ref, edge_ref, push_ref, m1, m2, idx_ref, wt_ref,
                lead_ref, matrix_ref,
                src_ref, near_ref, face_ref, damp_ref, coef_ref, m0, rp, ut, sems):
    cells = init_ref.shape[1]
    nblk = cells // LANES
    half = own_pad // 16 * 8
    copies = [
        pltpu.make_async_copy(face_hbm, face_ref, sems.at[0]),
        pltpu.make_async_copy(damp_hbm, damp_ref, sems.at[1]),
        pltpu.make_async_copy(near_hbm, near_ref, sems.at[2]),
        pltpu.make_async_copy(lead_hbm, lead_ref, sems.at[3]),
        pltpu.make_async_copy(init_hbm.at[0:half], init_ref.at[0:half], sems.at[4]),
        pltpu.make_async_copy(init_hbm.at[half:own_pad], init_ref.at[half:own_pad], sems.at[5]),
        pltpu.make_async_copy(src_hbm.at[0:half], src_ref.at[0:half], sems.at[6]),
        pltpu.make_async_copy(src_hbm.at[half:own_pad], src_ref.at[half:own_pad], sems.at[7]),
        pltpu.make_async_copy(matrix_hbm, matrix_ref, sems.at[8]),
    ]
    for copy in copies:
        copy.start()
    for copy in copies[0:3]:
        copy.wait()
    face = face_ref[...]
    inverse = RELAX / (damp_ref[...] + jnp.sum(face, axis=0, keepdims=True))
    coef_ref[0:NEIGH, :] = inverse * face
    coef_ref[NEIGH : NEIGH + 1, :] = FREQ * inverse
    for b in range(nblk):
        build_table(idx_ref, wt_ref, b, near_ref[:, lanes(b)],
                    coef_ref[0:NEIGH, lanes(b)], coef_ref[NEIGH : NEIGH + 1, lanes(b)])

    def table(b):
        return idx_ref, wt_ref, b

    def reader(ref, first=0):
        return lambda g, b: ref[rows8(g), lanes(b - first)]

    def coefs(s):
        if not 0 <= s < nblk:
            return jnp.zeros((1, LANES), jnp.float32)
        return coef_ref[NEIGH : NEIGH + 1, lanes(s)]

    ends = list(range(PB)) + list(range(nblk - PB, nblk))
    for i, b in enumerate(ends):
        build_product(ut, i, table(b), b, coefs)
    for copy in copies[3:6]:
        copy.wait()
    groups = list(range(own_pad // 8))
    restrict = matrix_of(lead_ref, starts[2], MODES, own_pad)
    derive = matrix_of(lead_ref, starts[0], own_pad, own_pad)
    for d in range(0, nblk, 2):
        m0[:, lanes(d, 2)] = dot(restrict, init_ref[:, lanes(d, 2)])

    for side in range(2):
        at = side * (nblk - PB)
        deriv = dot(derive, init_ref[:, lanes(at, PB)])
        for i in range(PB):
            b, here = at + i, lanes(side * PB + i)
            sums, pushes = stencil(
                reader(init_ref), b, table(b), groups, lambda s: 0 <= s < nblk, (ut, side * PB + i)
            )
            bf = coefficient(table(b))
            for g in groups:
                push_ref[rows8(g), here] = pushes[g]
                edge_ref[rows8(g), here] = (
                    KEEP * init_ref[rows8(g), lanes(b)] - bf * deriv[rows8(g), lanes(i)] + sums[g]
                )
    for copy in copies[6:8]:
        copy.wait()
    for g in groups:
        scaled_ref[rows8(g), :] = src_ref[rows8(g), :] * inverse
    for i, b in enumerate(ends):
        for g in groups:
            edge_ref[rows8(g), lanes(i)] = edge_ref[rows8(g), lanes(i)] + scaled_ref[rows8(g), lanes(b)]
    for d in range(0, nblk, 2):
        mode_ref[:, lanes(d, 2)] = dot(restrict, scaled_ref[:, lanes(d, 2)])

    def modes(src, first, out, to, b, known, keep):
        sums = stencil(reader(src, first), b, table(b), MODE_GROUPS, known)
        parts = (0.0, 0.0)
        if keep is not None:
            parts = turned([src[rows8(g), lanes(b - first)] for g in MODE_GROUPS], table(b), keep)
        for g in MODE_GROUPS:
            out[rows8(g), lanes(to)] = parts[g] + sums[g] + mode_ref[rows8(g), lanes(b)]

    near, far, deep = range(PB), range(PB, 2 * PB), range(2 * PB, 3 * PB)
    for b in range(PB, nblk - PB):
        modes(m0, 0, m1, b - PB, b, None, KEEP)
    for side in range(2):
        for d in list(far) + list(deep):
            b = nblk - 1 - d if side else d
            modes(m1, PB, m2, b - PB, b, lambda s: PB <= s < nblk - PB, KEEP)
    for side in range(2):
        for d in far:
            b = nblk - 1 - d if side else d
            known = [nblk - 1 - e if side else e for e in deep]
            modes(m2, PB, rp, b - PB, b, lambda s, known=known: s in known, None)

    near = near_ref[...].astype(jnp.float32)
    first_tiles, _ = halo_layout(own_pad)

    def pack(out, high):
        near_at = nblk - PB if high else 0
        far_at = nblk - 2 * PB if high else PB
        edge_at = PB if high else 0
        all_at = nblk - 2 * PB if high else 0
        for i in range(PB):
            for g in groups:
                out[first_tiles[0] + g * PB + i] = init_ref[rows8(g), lanes(near_at + i)]
                out[first_tiles[1] + g * PB + i] = edge_ref[rows8(g), lanes(edge_at + i)]
            for g in MODE_GROUPS:
                t = g * PB + i
                out[first_tiles[2] + t] = mode_ref[rows8(g), lanes(near_at + i)]
                out[first_tiles[3] + t] = m1[rows8(g), lanes(far_at + i - PB)]
                out[first_tiles[4] + t] = m2[rows8(g), lanes(far_at + i - PB)]
                out[first_tiles[5] + t] = rp[rows8(g), lanes(far_at + i - PB)]
        for i in range(2 * PB):
            out[first_tiles[6] + i, 0:NEIGH, :] = coef_ref[0:NEIGH, lanes(all_at + i)]
            out[first_tiles[6] + i, NEIGH : 2 * NEIGH, :] = near[:, lanes(all_at + i)]
            out[first_tiles[7], i : i + 1, :] = coef_ref[NEIGH : NEIGH + 1, lanes(all_at + i)]

    odd = lax.axis_index("cell") & 1

    @pl.when(odd == 0)
    def _():
        pack(a_ref, True)
        pack(b_ref, False)

    @pl.when(odd == 1)
    def _():
        pack(a_ref, False)
        pack(b_ref, True)

    copies[8].wait()


def cross_kernel(own_pad, rows, starts, init_ref, scaled_ref, idx_ref, wt_ref, lead_ref, matrix_ref,
                 cross_ref, first, deriv, push, ut):
    cells = init_ref.shape[1]
    nblk = cells // LANES
    own_groups = list(range(own_pad // 8))
    cross_groups = list(range(own_pad // 8, rows // 8))

    def table(b):
        return idx_ref, wt_ref, b

    derive = matrix_of(lead_ref, starts[0], rows, own_pad)
    for d in range(0, nblk, 2):
        deriv[:, lanes(d, 2)] = dot(derive, init_ref[:, lanes(d, 2)])

    def read_init(g, b):
        return init_ref[rows8(g), lanes(b)]

    def read_first(g, b):
        return first[rows8(g), lanes(b)]

    inside = range(PB, nblk - PB)

    def coefs(s):
        return wt_ref[s, NEIGH * (PB + 1) : NEIGH * (PB + 1) + 1, :]

    for b in range(nblk):
        bf = coefficient(table(b))
        for g in cross_groups:
            first[rows8(g), lanes(b)] = -bf * deriv[rows8(g), lanes(b)]
        if b in inside:
            build_product(ut, b - PB, table(b), b, coefs)
            sums, pushes = stencil(read_init, b, table(b), own_groups, None, (ut, b - PB))
            for g in own_groups:
                push[rows8(g), lanes(b - PB)] = pushes[g]
                first[rows8(g), lanes(b)] = (
                    KEEP * init_ref[rows8(g), lanes(b)]
                    + scaled_ref[rows8(g), lanes(b)]
                    - bf * deriv[rows8(g), lanes(b)]
                    + sums[g]
                )
    derive = matrix_of(matrix_ref, starts[1], rows, rows)
    couple = matrix_of(lead_ref, starts[0] + own_pad, rows - own_pad, own_pad)
    for d in range(PB, nblk - PB, 2):
        deriv[:, lanes(d, 2)] = dot(derive, first[:, lanes(d, 2)])
        turn = dot(couple, push[:, lanes(d - PB, 2)])
        for b in range(d, d + 2):
            bf = coefficient(table(b))
            for g in cross_groups:
                part = rows8(g - len(own_groups))
                cross_ref[part, lanes(b - PB)] = (
                    KEEP * read_first(g, b) - bf * deriv[rows8(g), lanes(b)] - turn[part, lanes(b - d)]
                )


def inner_kernel(smode_ref, m1_ref, m2_ref, idx_ref, wt_ref, mpart_ref, m2_out, rp_ref):
    cells = smode_ref.shape[1]
    nblk = cells // LANES
    inside = range(PB, nblk - PB)
    middle = range(2 * PB, nblk - 2 * PB)
    ends = list(range(PB)) + list(range(nblk - PB, nblk))

    def table(b):
        return idx_ref, wt_ref, b

    def read_m1(g, b):
        return m1_ref[rows8(g), lanes(b - PB)]

    def read_m2(g, b):
        return m2_out[rows8(g), lanes(b - PB)]

    m2_out[...] = m2_ref[...]
    for b in range(3 * PB, nblk - 3 * PB):
        sums = stencil(read_m1, b, table(b), MODE_GROUPS)
        parts = turned([read_m1(g, b) for g in MODE_GROUPS], table(b), KEEP)
        for g in MODE_GROUPS:
            m2_out[rows8(g), lanes(b - PB)] = parts[g] + sums[g] + smode_ref[rows8(g), lanes(b)]
    for i, b in enumerate(ends):
        sums = stencil(read_m1, b, table(b), MODE_GROUPS, lambda s: s in inside)
        for g in MODE_GROUPS:
            mpart_ref[rows8(g), lanes(i)] = sums[g] + smode_ref[rows8(g), lanes(b)]
    for b in range(nblk):
        sums = stencil(read_m2, b, table(b), MODE_GROUPS, lambda s: s in middle)
        if b in middle:
            parts = turned([read_m2(g, b) for g in MODE_GROUPS], table(b), -RELAX)
            sums = [total + part for total, part in zip(sums, parts)]
        for g in MODE_GROUPS:
            rp_ref[rows8(g), lanes(b)] = sums[g] + smode_ref[rows8(g), lanes(b)]


def outer_kernel(own_pad, rows, starts, a_ref, b_ref, init_ref, smode_ref, edge_ref,
                 push_ref, mpart_ref, first_ref, m1i_ref, m2i_ref, rp_ref, idx_in, wt_in,
                 lead_ref, matrix_ref, send_ref, v1, deriv, c2x,
                 halo, v2, push, m1x, m2x, rx, c1x, idx, wt, ut):
    cells = init_ref.shape[1]
    nblk = cells // LANES
    lead = own_pad // 8
    own_groups = list(range(lead))
    cross_groups = list(range(lead, rows // 8))
    tiles, _ = halo_layout(own_pad)
    odd = lax.axis_index("cell") & 1

    @pl.when(odd == 0)
    def _():
        halo[1] = a_ref[...]
        halo[0] = b_ref[...]

    @pl.when(odd == 1)
    def _():
        halo[0] = a_ref[...]
        halo[1] = b_ref[...]

    def side_of(b):
        return (0, b + 2 * PB) if b < 0 else (1, b - nblk)

    for side in range(2):
        for i in range(2 * PB):
            tile = tiles[6] + i
            build_table(idx, wt, side * 2 * PB + i, halo[side, tile, NEIGH : 2 * NEIGH, :].astype(jnp.int32),
                        halo[side, tile, 0:NEIGH, :], halo[side, tiles[7], i : i + 1, :])

    def table(b):
        if 0 <= b < nblk:
            return idx_in, wt_in, b
        side, i = side_of(b)
        return idx, wt, side * 2 * PB + i

    def section(number, g, b, far=False):
        side, i = side_of(b)
        if (side == 1) == far:
            i -= PB
        return halo[side, tiles[number] + g * PB + i]

    def own(b):
        return 0 <= b < nblk

    def read_init(g, b):
        return init_ref[rows8(g), lanes(b)] if own(b) else section(0, g, b)

    ring = list(range(-PB, PB)) + list(range(nblk - PB, nblk + PB))
    place = {b: i for i, b in enumerate(ring)}

    def read_v1(g, b):
        return v1[rows8(g), lanes(place[b])]

    def coefs(b):
        if own(b):
            return jnp.zeros((1, LANES), jnp.float32)
        side, i = side_of(b)
        return halo[side, tiles[7], i : i + 1, :]

    derive_cross = matrix_of(lead_ref, starts[0], rows, own_pad)
    for side in range(2):
        first = nblk if side else -PB
        values = jnp.concatenate(
            [
                jnp.concatenate([section(0, g, first + i) for i in range(PB)], axis=1)
                for g in own_groups
            ],
            axis=0,
        )
        turn = dot(derive_cross, values)
        for i in range(PB):
            b = first + i
            bf = coefficient(table(b))
            for g in cross_groups:
                v1[rows8(g), lanes(place[b])] = -bf * turn[rows8(g), lanes(i)]
            sums = stencil(read_init, b, table(b), own_groups, own)
            for g in own_groups:
                v1[rows8(g), lanes(place[b])] = section(1, g, b) + sums[g]
        for i in range(PB):
            b = nblk - PB + i if side else i
            at = lanes(side * PB + i)
            build_product(ut, side * PB + i, table(b), b, coefs)
            sums, pushes = stencil(
                read_init, b, table(b), own_groups, lambda s: not own(s), (ut, side * PB + i)
            )
            for g in own_groups:
                push[rows8(g), at] = push_ref[rows8(g), at] + pushes[g]
                v1[rows8(g), lanes(place[b])] = edge_ref[rows8(g), at] + sums[g]
            for g in cross_groups:
                v1[rows8(g), lanes(place[b])] = first_ref[rows8(g), lanes(b)]
    both = matrix_of(matrix_ref, starts[1], rows + MODES, rows)
    restrict = matrix_of(matrix_ref, starts[1] + rows, MODES, rows)
    low = -2 * PB
    for side in range(2):
        b = nblk if side else -PB
        m1x[:, lanes(b - low, PB)] = dot(restrict, v1[:, lanes(place[b], PB)])
        b = nblk - PB if side else 0
        mixed = dot(both, v1[:, lanes(place[b], PB)])
        deriv[:, lanes(side * PB, PB)] = mixed[0:rows]
        m1x[:, lanes(b - low, PB)] = mixed[rows:]
    m1x[:, lanes(PB - low, nblk - 2 * PB)] = m1i_ref[...]
    for b in list(range(-2 * PB, -PB)) + list(range(nblk + PB, nblk + 2 * PB)):
        for g in MODE_GROUPS:
            m1x[rows8(g), lanes(b - low)] = section(3, g, b, True)

    ends = list(range(PB)) + list(range(nblk - PB, nblk))
    couple = matrix_of(lead_ref, starts[0] + own_pad, rows - own_pad, own_pad)
    for side in range(2):
        turn = dot(couple, push[:, lanes(side * PB, PB)])
        for i in range(PB):
            b, at = ends[side * PB + i], lanes(side * PB + i)
            bf = coefficient(table(b))
            for g in cross_groups:
                part = rows8(g - lead)
                v2[part, at] = KEEP * read_v1(g, b) - bf * deriv[rows8(g), at] - turn[part, lanes(i)]

    def reader(ref, first):
        return lambda g, b: ref[rows8(g), lanes(b - first)]

    def modes(src, first, b, keep, known=None):
        read = reader(src, first)
        sums = stencil(read, b, table(b), MODE_GROUPS, known)
        if keep is None:
            return sums
        parts = turned([read(g, b) for g in MODE_GROUPS], table(b), keep)
        return [total + part for total, part in zip(sums, parts)]

    near = list(range(-PB, 0)) + list(range(nblk, nblk + PB))
    far = list(range(-2 * PB, -PB)) + list(range(nblk + PB, nblk + 2 * PB))
    for b in far:
        sums = modes(m1x, low, b, None, lambda s: s in place)
        for g in MODE_GROUPS:
            m2x[rows8(g), lanes(b - low)] = section(4, g, b, True) + sums[g]
    for b in near:
        sums = modes(m1x, low, b, KEEP)
        for g in MODE_GROUPS:
            m2x[rows8(g), lanes(b - low)] = section(2, g, b) + sums[g]
    for i, b in enumerate(ends):
        sums = modes(m1x, low, b, KEEP, lambda s: s in place)
        for g in MODE_GROUPS:
            m2x[rows8(g), lanes(b - low)] = mpart_ref[rows8(g), lanes(i)] + sums[g]
    m2x[:, lanes(2 * PB - low, nblk - 4 * PB)] = m2i_ref[:, lanes(PB, nblk - 4 * PB)]
    for b in list(range(PB, 2 * PB)) + list(range(nblk - 2 * PB, nblk - PB)):
        sums = modes(m1x, low, b, None, lambda s: s in place)
        for g in MODE_GROUPS:
            m2x[rows8(g), lanes(b - low)] = m2i_ref[rows8(g), lanes(b - PB)] + sums[g]

    middle = range(2 * PB, nblk - 2 * PB)
    for b in range(-2 * PB, nblk + 2 * PB):
        if b in middle:
            sums = modes(m2x, low, b, None, lambda s: s not in middle)
        elif own(b):
            sums = modes(m2x, low, b, -RELAX, lambda s: s not in middle)
        else:
            sums = modes(m2x, low, b, -RELAX, lambda s: -2 * PB <= s < nblk + 2 * PB)
        for g in MODE_GROUPS:
            if own(b):
                ready = rp_ref[rows8(g), lanes(b)]
            else:
                ready = section(5, g, b, True) if b in far else section(2, g, b)
            rx[rows8(g), lanes(b - low)] = ready + sums[g]
    for b in range(-PB, nblk + PB):
        sums = modes(rx, low, b, KEEP)
        for g in MODE_GROUPS:
            c1x[rows8(g), lanes(b + PB)] = sums[g] + rx[rows8(g), lanes(b - low)]
    for b in range(nblk):
        sums = modes(c1x, -PB, b, KEEP)
        for g in MODE_GROUPS:
            c2x[rows8(g), lanes(b)] = sums[g] + rx[rows8(g), lanes(b - low)]

    cross = rows - own_pad
    prolong = matrix_of(matrix_ref, starts[3] + own_pad, cross, MODES)
    for b in range(0, nblk, 2):
        values = c2x[:, lanes(b, 2)]
        if b in ends:
            at = lanes(ends.index(b), 2)
            send_ref[0:cross, at] = v2[:, at] + dot(prolong, values)
        else:
            fold, at = divmod(b - PB, 2 * PB)
            send_ref[cross + fold * MODES : cross + (fold + 1) * MODES, lanes(at, 2)] = values


def own_kernel(own_pad, starts, first, deriv, v1_ref, ends_ref, scaled_ref, c2_ref, idx_ref, wt_ref,
               matrix_ref, base_ref):
    cells = scaled_ref.shape[1]
    nblk = cells // LANES
    groups = list(range(own_pad // 8))
    ring = list(range(-PB, PB)) + list(range(nblk - PB, nblk + PB))
    ends = list(range(PB)) + list(range(nblk - PB, nblk))
    prolong = matrix_of(matrix_ref, starts[3], own_pad, MODES)

    def read(g, b):
        if b in ring:
            return v1_ref[rows8(g), lanes(ring.index(b))]
        return first[rows8(g), lanes(b)]

    for d in range(0, nblk, 2):
        lifted = dot(prolong, c2_ref[:, lanes(d, 2)])
        for b in range(d, d + 2):
            table = (idx_ref, wt_ref, b)
            bf = coefficient(table)
            sums = stencil(read, b, table, groups)
            for g in groups:
                if b in ends:
                    turn = ends_ref[rows8(g), lanes(ends.index(b))]
                else:
                    turn = deriv[rows8(g), lanes(b)]
                base_ref[rows8(g), lanes(b)] = (
                    KEEP * read(g, b)
                    + scaled_ref[rows8(g), lanes(b)]
                    - bf * turn
                    + sums[g]
                    + lifted[rows8(g), lanes(b - d)]
                )


def final_kernel(count, starts, base_ref, matrix_ref, *refs):
    out_hbm, out_ref, sems = refs[2 * count :]
    own_pad = base_ref.shape[0]
    nblk = out_ref.shape[1] // LANES
    early, late = refs[0 : 2 * count : 2], refs[1 : 2 * count : 2]
    copies = []
    ends = list(range(PB)) + list(range(nblk - PB, nblk))
    for b in range(0, nblk, 2):
        total = base_ref[:, lanes(b, 2)]
        for k in range(count):
            if b in ends:
                total = total + late[k][0:own_pad, lanes(ends.index(b), 2)]
            else:
                fold, at = divmod(b - PB, 2 * PB)
                lift = matrix_of(matrix_ref, starts[4 + k], own_pad, MODES)
                first = own_pad + fold * MODES
                total = (
                    total
                    + early[k][:, lanes(b - PB, 2)]
                    + dot(lift, late[k][first : first + MODES, lanes(at, 2)])
                )
        out_ref[:, lanes(b, 2)] = total
        if b % 4 == 2:
            piece = (slice(None), lanes(b - 2, 4))
            copies.append(pltpu.make_async_copy(out_ref.at[piece], out_hbm.at[piece], sems.at[b // 4]))
            copies[-1].start()
    for copy in copies:
        copy.wait()


def vm(*shape):
    return pltpu.VMEM(shape, jnp.float32)


def f32(*shape):
    return jax.ShapeDtypeStruct(shape, jnp.float32)


def call(kernel, out_shape, scratch, cost_us, *args, fetch=False, store=False):
    whole = pl.BlockSpec(memory_space=pltpu.VMEM)
    single = not isinstance(out_shape, (tuple, list))
    return pl.pallas_call(
        kernel,
        out_shape=out_shape,
        in_specs=[pl.BlockSpec(memory_space=pltpu.HBM) if fetch else whole] * len(args),
        out_specs=(pl.BlockSpec(memory_space=pltpu.HBM) if store else whole) if single else [whole] * len(out_shape),
        scratch_shapes=scratch,
        compiler_params=pltpu.CompilerParams(vmem_limit_bytes=16 * 1024 * 1024),
        cost_estimate=pl.CostEstimate(
            flops=int(cost_us * 1e8), bytes_accessed=int(cost_us * 3e6), transcendentals=0
        ),
    )(*args)


def per_device(initial, source, neighbors, face_weights, damping):
    own, cells = initial.shape
    nblk = cells // LANES
    inst_count = lax.axis_size("inst")
    cell_count = lax.axis_size("cell")
    own_pad = up8(own)
    lead, matrices, starts, rows = constants(own, inst_count)
    lead, matrices = jnp.asarray(lead), jnp.asarray(matrices)
    cross = rows - own_pad
    if own_pad != own:
        initial = jnp.pad(initial, ((0, own_pad - own), (0, 0)))
        source = jnp.pad(source, ((0, own_pad - own), (0, 0)))
    _, tiles = halo_layout(own_pad)
    assert nblk >= 8 * PB and nblk % 4 == 0
    slots = NEIGH * (PB + 1) + 4
    folds = -(-(nblk - 2 * PB) // (2 * PB))

    def wide(height, blocks):
        return f32(height, blocks * LANES)

    def scratch(height, blocks):
        return vm(height, blocks * LANES)

    def int32(*shape):
        return jax.ShapeDtypeStruct(shape, jnp.int32)

    pack_a, pack_b, initial, scaled, smode, ends, push, m1, m2, idx, wt, lead, matrices = call(
        functools.partial(pack_kernel, own_pad, starts),
        [f32(tiles, 8, LANES), f32(tiles, 8, LANES), wide(own_pad, nblk), wide(own_pad, nblk),
         wide(MODES, nblk), wide(own_pad, 2 * PB), wide(own_pad, 2 * PB), wide(MODES, nblk - 2 * PB),
         wide(MODES, nblk - 2 * PB),
         int32(nblk, 8, LANES), f32(nblk, slots, LANES),
         jax.ShapeDtypeStruct(lead.shape, lead.dtype),
         jax.ShapeDtypeStruct(matrices.shape, matrices.dtype)],
        [scratch(own_pad, nblk), pltpu.VMEM((NEIGH, cells), jnp.int32), vm(NEIGH, cells), vm(1, cells),
         vm(8, cells), scratch(MODES, nblk), scratch(MODES, nblk - 2 * PB), vm(2 * PB, slots, LANES),
         pltpu.SemaphoreType.DMA((9,))],
        2,
        *[
            pltpu.with_memory_space_constraint(x, pltpu.HBM)
            for x in (initial, source, neighbors, face_weights, damping.reshape(1, cells), lead, matrices)
        ],
        fetch=True,
    )
    near_pairs = [(i, i ^ 1) for i in range(cell_count) if i ^ 1 < cell_count]
    far_pairs = []
    for i in range(1, cell_count - 1, 2):
        far_pairs += [(i, i + 1), (i + 1, i)]
    halo_b = lax.ppermute(pack_b, "cell", far_pairs)
    halo_a = lax.ppermute(pack_a, "cell", near_pairs)

    cross_mid, first, deriv = call(
        functools.partial(cross_kernel, own_pad, rows, starts),
        [wide(cross, nblk - 2 * PB), wide(rows, nblk), wide(rows, nblk)],
        [scratch(own_pad, nblk - 2 * PB), vm(nblk - 2 * PB, slots, LANES)], 3,
        initial, scaled, idx, wt, lead, matrices,
    )

    def share(array, k):
        if cross == own_pad:
            return array
        part = lax.slice_in_dim(array, (k - 1) * own, k * own, axis=0)
        return jnp.pad(part, ((0, own_pad - own), (0, 0)))

    def shift(k):
        return [(i, (i + k) % inst_count) for i in range(inst_count)]

    early = [lax.ppermute(share(cross_mid, k), "inst", shift(k)) for k in range(1, inst_count)]

    mpart, m2, rp = call(
        inner_kernel,
        [wide(MODES, 2 * PB), wide(MODES, nblk - 2 * PB), wide(MODES, nblk)], [], 3,
        smode, m1, m2, idx, wt,
    )
    send, v1, dends, c2 = call(
        functools.partial(outer_kernel, own_pad, rows, starts),
        [wide(cross + folds * MODES, 2 * PB), wide(rows, 4 * PB), wide(rows, 2 * PB), wide(MODES, nblk)],
        [pltpu.VMEM((2, tiles, 8, LANES), jnp.float32), scratch(cross, 2 * PB),
         scratch(own_pad, 2 * PB), scratch(MODES, nblk + 4 * PB), scratch(MODES, nblk + 4 * PB),
         scratch(MODES, nblk + 4 * PB), scratch(MODES, nblk + 2 * PB),
         pltpu.VMEM((4 * PB, 8, LANES), jnp.int32), vm(4 * PB, slots, LANES), vm(2 * PB, slots, LANES)],
        8, halo_a, halo_b, initial, smode, ends, push, mpart, first, m1, m2, rp, idx, wt, lead, matrices,
    )

    def share_late(k):
        if cross == own_pad:
            return send
        return jnp.concatenate([share(send[:cross], k), send[cross:]], axis=0)

    late = [lax.ppermute(share_late(k), "inst", shift(k)) for k in range(1, inst_count)]
    base = call(
        functools.partial(own_kernel, own_pad, starts), wide(own_pad, nblk), [], 2,
        first, deriv, v1, dends, scaled, c2, idx, wt, matrices,
    )
    received = [r for pair in zip(early, late) for r in pair]
    out = call(
        functools.partial(final_kernel, inst_count - 1, starts), f32(own_pad, cells),
        [vm(own_pad, cells), pltpu.SemaphoreType.DMA((nblk // 4,))], 1,
        base, matrices, *received, store=True,
    )
    return out[:own] if own_pad != own else out


def solution(mesh):
    return jax.shard_map(
        per_device,
        mesh=mesh,
        in_specs=(
            P("inst", "cell"),
            P("inst", "cell"),
            P(None, "cell"),
            P(None, "cell"),
            P("cell"),
        ),
        out_specs=P("inst", "cell"),
        check_vma=False,
    )
```

```python
import functools

import jax
import jax.numpy as jnp
import numpy as np
from jax import lax
from jax.experimental import pallas as pl
from jax.experimental.pallas import tpu as pltpu
from jax.sharding import PartitionSpec as P


NI = 16
COMP = 5
NEIGH = 4
PLANE = 256
FREQ = 0.15
RELAX = 0.6
KEEP = 1.0 - RELAX

LANES = 128
PB = PLANE // LANES
MODES = 16


def up8(count):
    return -(-count // 8) * 8


def row_map(own):
    rows = [divmod(r, COMP) for r in range(own)]
    rows += [None] * (up8(own) - own)
    other = NI * COMP - own
    rows += [divmod(own + r, COMP) for r in range(other)]
    rows += [None] * (up8(other) - other)
    return rows


def mode_row(h, c):
    if h:
        return 8 * (h - 1) + 3 + c
    return c if c < 3 else 5 + c


def split_matrix(matrix):
    high = matrix.astype(jnp.bfloat16)
    low = (matrix - high.astype(np.float64)).astype(jnp.bfloat16)
    return np.concatenate([high, low, high], axis=1)


def constants(own, inst_count):
    rows = row_map(own)
    own_pad = up8(own)
    count = len(rows)
    derive = np.zeros((count, count))
    restrict = np.zeros((MODES, count))
    prolong = np.zeros((count, MODES))
    for i, left in enumerate(rows):
        if left is None:
            continue
        n, c = left
        phase = 2.0 * np.pi * n / NI
        shape = (1.0, np.cos(phase), np.sin(phase))
        for h in range(3):
            restrict[mode_row(h, c), i] = shape[h] * (1.0 if h == 0 else 2.0) / NI
            prolong[i, mode_row(h, c)] = shape[h]
        for j, right in enumerate(rows):
            if right is not None and right[1] == c and right[0] != n:
                gap = n - right[0]
                derive[i, j] = 0.5 * (-1.0) ** gap / np.tan(np.pi * gap / NI)
    other = prolong[own_pad:]
    lifts = []
    for k in range(1, inst_count):
        lift = np.zeros((own_pad, MODES))
        lift[:own] = other[(k - 1) * own : k * own]
        lifts.append(lift)
    early = [derive[:, :own_pad], restrict[:, :own_pad]]
    late = [np.concatenate([derive, restrict]), prolong] + lifts
    (lead, lead_starts), (rest, rest_starts) = stack(early), stack(late)
    starts = [lead_starts[0], rest_starts[0], lead_starts[1]] + rest_starts[1:]
    return lead, rest, starts, count


def stack(parts):
    wides = [split_matrix(part) for part in parts]
    width = -(-max(wide.shape[1] for wide in wides) // LANES) * LANES
    blocks, starts, at = [], [], 0
    for wide in wides:
        height = -(-wide.shape[0] // 16) * 16
        blocks.append(np.pad(wide, ((0, height - wide.shape[0]), (0, width - wide.shape[1]))))
        starts.append(at)
        at += height
    return np.concatenate(blocks), starts


def split3(values):
    high = values.astype(jnp.bfloat16).astype(jnp.float32)
    return jnp.concatenate([values, values, values - high], axis=0).astype(jnp.bfloat16)


def dot(matrix, values):
    return jnp.dot(matrix, split3(values), preferred_element_type=jnp.float32)


def matrix_of(ref, start, height, depth):
    return ref[start : start + height, 0 : 3 * depth]


def lanes(start, count=1):
    return slice(start * LANES, (start + count) * LANES)


def build_table(idx_ref, wt_ref, at, near, bw, bf):
    target = near + lax.broadcasted_iota(jnp.int32, near.shape, 1)
    slot = lax.broadcasted_iota(jnp.int32, near.shape, 0)
    base = (target >> 7) + jnp.where((slot & 1) == 0, PB, 0)
    idx_ref[at, 0:NEIGH, :] = target & (LANES - 1)
    idx_ref[at, NEIGH : 2 * NEIGH, :] = target & (LANES - 1)
    for j in range(PB + 1):
        wt_ref[at, NEIGH * j : NEIGH * (j + 1), :] = jnp.where(base == j, bw, 0.0)
    wt_ref[at, NEIGH * (PB + 1) : NEIGH * (PB + 1) + 1, :] = bf


def build_product(ut_ref, at, table, block, coefs):
    idx_ref, wt_ref, to = table
    even = (lax.broadcasted_iota(jnp.int32, (8, LANES), 0) & 1) == 0
    for j in range(PB + 1):
        low = jnp.broadcast_to(coefs(block + j - PB), (8, LANES))
        high = jnp.broadcast_to(coefs(block + j), (8, LANES))
        taken = jnp.take_along_axis(jnp.where(even, low, high), idx_ref[to], axis=1)
        part = slice(NEIGH * j, NEIGH * (j + 1))
        ut_ref[at, part, :] = wt_ref[to, part, :] * taken[0:NEIGH]


def coefficient(table):
    _, wt_ref, at = table
    return wt_ref[at, pl.ds(NEIGH * (PB + 1), 8, stride=0), :]


def stencil(read, block, table, groups, known=None, product=None):
    idx_ref, wt_ref, at = table
    sums, others, cache = [0.0] * len(groups), [0.0] * len(groups), {}

    def source(g, b):
        if (g, b) not in cache:
            cache[g, b] = read(g, b)
        return cache[g, b]

    for k in range(NEIGH):
        index = None
        for j in range(PB + 1):
            b = block + j - (0 if k % 2 else PB)
            if known is not None and not known(b):
                continue
            if index is None:
                index = idx_ref[at, pl.ds(k, 8, stride=0), :]
            row = pl.ds(NEIGH * j + k, 8, stride=0)
            weight = wt_ref[at, row, :]
            if product is not None:
                other = product[0][product[1], row, :]
            for i, g in enumerate(groups):
                taken = jnp.take_along_axis(source(g, b), index, axis=1)
                sums[i] = sums[i] + weight * taken
                if product is not None:
                    others[i] = others[i] + other * taken
    return sums if product is None else (sums, others)


def turned(values, table, keep):
    top = lax.broadcasted_iota(jnp.int32, (8, LANES), 0) >= 3
    bf = jnp.where(top, coefficient(table), 0.0)
    low, high = values
    return keep * low - bf * high, keep * high + bf * low


def rows8(g):
    return slice(8 * g, 8 * g + 8)


MODE_GROUPS = list(range(MODES // 8))


def halo_layout(own_pad):
    fine, mode = own_pad // 8 * PB, MODES // 8 * PB
    sizes = [fine, fine, mode, mode, mode, mode, 2 * PB]
    starts = [sum(sizes[:i]) for i in range(len(sizes))]
    return starts, sum(sizes)


SPARE = 2


def spare_tile(tiles, near_last, i):
    return tiles[2 if (i >= PB) == bool(near_last) else 3] + PB + i % PB


def pack_kernel(own_pad, starts, init_hbm, src_hbm, near_hbm, face_hbm, damp_hbm, lead_hbm, matrix_hbm,
                a_ref, b_ref, init_ref, scaled_ref, mode_ref, edge_ref, push_ref, m1, m2, idx_ref, wt_ref,
                lead_ref, matrix_ref,
                src_ref, near_ref, face_ref, damp_ref, coef_ref, m0, rp, ut, sems):
    cells = init_ref.shape[1]
    nblk = cells // LANES
    half = own_pad // 16 * 8
    copies = [
        pltpu.make_async_copy(face_hbm, face_ref, sems.at[0]),
        pltpu.make_async_copy(damp_hbm, damp_ref, sems.at[1]),
        pltpu.make_async_copy(near_hbm, near_ref, sems.at[2]),
        pltpu.make_async_copy(lead_hbm, lead_ref, sems.at[3]),
        pltpu.make_async_copy(init_hbm.at[0:half], init_ref.at[0:half], sems.at[4]),
        pltpu.make_async_copy(init_hbm.at[half:own_pad], init_ref.at[half:own_pad], sems.at[5]),
        pltpu.make_async_copy(src_hbm.at[0:half], src_ref.at[0:half], sems.at[6]),
        pltpu.make_async_copy(src_hbm.at[half:own_pad], src_ref.at[half:own_pad], sems.at[7]),
        pltpu.make_async_copy(matrix_hbm, matrix_ref, sems.at[8]),
    ]
    for copy in copies:
        copy.start()
    for copy in copies[0:3]:
        copy.wait()
    face = face_ref[...]
    inverse = RELAX / (damp_ref[...] + jnp.sum(face, axis=0, keepdims=True))
    coef_ref[0:NEIGH, :] = inverse * face
    coef_ref[NEIGH : NEIGH + 1, :] = FREQ * inverse
    for b in range(nblk):
        build_table(idx_ref, wt_ref, b, near_ref[:, lanes(b)],
                    coef_ref[0:NEIGH, lanes(b)], coef_ref[NEIGH : NEIGH + 1, lanes(b)])

    def table(b):
        return idx_ref, wt_ref, b

    def reader(ref, first=0):
        return lambda g, b: ref[rows8(g), lanes(b - first)]

    def coefs(s):
        if not 0 <= s < nblk:
            return jnp.zeros((1, LANES), jnp.float32)
        return coef_ref[NEIGH : NEIGH + 1, lanes(s)]

    ends = list(range(PB)) + list(range(nblk - PB, nblk))
    for i, b in enumerate(ends):
        build_product(ut, i, table(b), b, coefs)
    for copy in copies[3:6]:
        copy.wait()
    groups = list(range(own_pad // 8))
    restrict = matrix_of(lead_ref, starts[2], MODES, own_pad)
    derive = matrix_of(lead_ref, starts[0], own_pad, own_pad)
    for d in range(0, nblk, 2):
        m0[:, lanes(d, 2)] = dot(restrict, init_ref[:, lanes(d, 2)])

    for side in range(2):
        at = side * (nblk - PB)
        deriv = dot(derive, init_ref[:, lanes(at, PB)])
        for i in range(PB):
            b, here = at + i, lanes(side * PB + i)
            sums, pushes = stencil(
                reader(init_ref), b, table(b), groups, lambda s: 0 <= s < nblk, (ut, side * PB + i)
            )
            bf = coefficient(table(b))
            for g in groups:
                push_ref[rows8(g), here] = pushes[g]
                edge_ref[rows8(g), here] = (
                    KEEP * init_ref[rows8(g), lanes(b)] - bf * deriv[rows8(g), lanes(i)] + sums[g]
                )
    for copy in copies[6:8]:
        copy.wait()
    for g in groups:
        scaled_ref[rows8(g), :] = src_ref[rows8(g), :] * inverse
    for i, b in enumerate(ends):
        for g in groups:
            edge_ref[rows8(g), lanes(i)] = edge_ref[rows8(g), lanes(i)] + scaled_ref[rows8(g), lanes(b)]
    for d in range(0, nblk, 2):
        mode_ref[:, lanes(d, 2)] = dot(restrict, scaled_ref[:, lanes(d, 2)])

    def modes(src, first, out, to, b, known, keep):
        sums = stencil(reader(src, first), b, table(b), MODE_GROUPS, known)
        parts = (0.0, 0.0)
        if keep is not None:
            parts = turned([src[rows8(g), lanes(b - first)] for g in MODE_GROUPS], table(b), keep)
        for g in MODE_GROUPS:
            out[rows8(g), lanes(to)] = parts[g] + sums[g] + mode_ref[rows8(g), lanes(b)]

    near, far, deep = range(PB), range(PB, 2 * PB), range(2 * PB, 3 * PB)
    for b in range(PB, nblk - PB):
        modes(m0, 0, m1, b - PB, b, None, KEEP)
    for side in range(2):
        for d in list(far) + list(deep):
            b = nblk - 1 - d if side else d
            modes(m1, PB, m2, b - PB, b, lambda s: PB <= s < nblk - PB, KEEP)
    for side in range(2):
        for d in far:
            b = nblk - 1 - d if side else d
            known = [nblk - 1 - e if side else e for e in deep]
            modes(m2, PB, rp, b - PB, b, lambda s, known=known: s in known, None)

    near = near_ref[...].astype(jnp.float32)
    first_tiles, _ = halo_layout(own_pad)

    def pack(out, high):
        near_at = nblk - PB if high else 0
        far_at = nblk - 2 * PB if high else PB
        edge_at = PB if high else 0
        all_at = nblk - 2 * PB if high else 0
        for i in range(PB):
            for g in groups:
                out[first_tiles[0] + g * PB + i] = init_ref[rows8(g), lanes(near_at + i)]
                out[first_tiles[1] + g * PB + i] = edge_ref[rows8(g), lanes(edge_at + i)]
            for g in MODE_GROUPS:
                t = g * PB + i
                out[first_tiles[2] + t] = mode_ref[rows8(g), lanes(near_at + i)]
                out[first_tiles[3] + t] = m1[rows8(g), lanes(far_at + i - PB)]
                out[first_tiles[4] + t] = m2[rows8(g), lanes(far_at + i - PB)]
                out[first_tiles[5] + t] = rp[rows8(g), lanes(far_at + i - PB)]
        for i in range(2 * PB):
            out[first_tiles[6] + i, 0:NEIGH, :] = coef_ref[0:NEIGH, lanes(all_at + i)]
            out[first_tiles[6] + i, NEIGH : 2 * NEIGH, :] = near[:, lanes(all_at + i)]
            out[spare_tile(first_tiles, high, i), SPARE : SPARE + 1, :] = coef_ref[NEIGH : NEIGH + 1, lanes(all_at + i)]

    odd = lax.axis_index("cell") & 1

    @pl.when(odd == 0)
    def _():
        pack(a_ref, True)
        pack(b_ref, False)

    @pl.when(odd == 1)
    def _():
        pack(a_ref, False)
        pack(b_ref, True)

    copies[8].wait()


def cross_kernel(own_pad, rows, starts, init_ref, scaled_ref, idx_ref, wt_ref, lead_ref, matrix_ref,
                 cross_ref, first, deriv, push, ut):
    cells = init_ref.shape[1]
    nblk = cells // LANES
    own_groups = list(range(own_pad // 8))
    cross_groups = list(range(own_pad // 8, rows // 8))

    def table(b):
        return idx_ref, wt_ref, b

    derive = matrix_of(lead_ref, starts[0], rows, own_pad)
    for d in range(0, nblk, 2):
        deriv[:, lanes(d, 2)] = dot(derive, init_ref[:, lanes(d, 2)])

    def read_init(g, b):
        return init_ref[rows8(g), lanes(b)]

    def read_first(g, b):
        return first[rows8(g), lanes(b)]

    inside = range(PB, nblk - PB)

    def coefs(s):
        return wt_ref[s, NEIGH * (PB + 1) : NEIGH * (PB + 1) + 1, :]

    for b in range(nblk):
        bf = coefficient(table(b))
        for g in cross_groups:
            first[rows8(g), lanes(b)] = -bf * deriv[rows8(g), lanes(b)]
        if b in inside:
            build_product(ut, b - PB, table(b), b, coefs)
            sums, pushes = stencil(read_init, b, table(b), own_groups, None, (ut, b - PB))
            for g in own_groups:
                push[rows8(g), lanes(b - PB)] = pushes[g]
                first[rows8(g), lanes(b)] = (
                    KEEP * init_ref[rows8(g), lanes(b)]
                    + scaled_ref[rows8(g), lanes(b)]
                    - bf * deriv[rows8(g), lanes(b)]
                    + sums[g]
                )
    derive = matrix_of(matrix_ref, starts[1], rows, rows)
    couple = matrix_of(lead_ref, starts[0] + own_pad, rows - own_pad, own_pad)
    for d in range(PB, nblk - PB, 2):
        deriv[:, lanes(d, 2)] = dot(derive, first[:, lanes(d, 2)])
        turn = dot(couple, push[:, lanes(d - PB, 2)])
        for b in range(d, d + 2):
            bf = coefficient(table(b))
            for g in cross_groups:
                part = rows8(g - len(own_groups))
                cross_ref[part, lanes(b - PB)] = (
                    KEEP * read_first(g, b) - bf * deriv[rows8(g), lanes(b)] - turn[part, lanes(b - d)]
                )


def inner_kernel(smode_ref, m1_ref, m2_ref, idx_ref, wt_ref, mpart_ref, m2_out, rp_ref):
    cells = smode_ref.shape[1]
    nblk = cells // LANES
    inside = range(PB, nblk - PB)
    middle = range(2 * PB, nblk - 2 * PB)
    ends = list(range(PB)) + list(range(nblk - PB, nblk))

    def table(b):
        return idx_ref, wt_ref, b

    def read_m1(g, b):
        return m1_ref[rows8(g), lanes(b - PB)]

    def read_m2(g, b):
        return m2_out[rows8(g), lanes(b - PB)]

    m2_out[...] = m2_ref[...]
    for b in range(3 * PB, nblk - 3 * PB):
        sums = stencil(read_m1, b, table(b), MODE_GROUPS)
        parts = turned([read_m1(g, b) for g in MODE_GROUPS], table(b), KEEP)
        for g in MODE_GROUPS:
            m2_out[rows8(g), lanes(b - PB)] = parts[g] + sums[g] + smode_ref[rows8(g), lanes(b)]
    for i, b in enumerate(ends):
        sums = stencil(read_m1, b, table(b), MODE_GROUPS, lambda s: s in inside)
        for g in MODE_GROUPS:
            mpart_ref[rows8(g), lanes(i)] = sums[g] + smode_ref[rows8(g), lanes(b)]
    for b in range(nblk):
        sums = stencil(read_m2, b, table(b), MODE_GROUPS, lambda s: s in middle)
        if b in middle:
            parts = turned([read_m2(g, b) for g in MODE_GROUPS], table(b), -RELAX)
            sums = [total + part for total, part in zip(sums, parts)]
        for g in MODE_GROUPS:
            rp_ref[rows8(g), lanes(b)] = sums[g] + smode_ref[rows8(g), lanes(b)]


def outer_kernel(own_pad, rows, starts, a_ref, b_ref, init_ref, smode_ref, edge_ref,
                 push_ref, mpart_ref, first_ref, m1i_ref, m2i_ref, rp_ref, idx_in, wt_in,
                 lead_ref, matrix_ref, send_ref, v1, deriv, c2x,
                 halo, v2, push, m1x, m2x, rx, c1x, idx, wt, ut):
    cells = init_ref.shape[1]
    nblk = cells // LANES
    lead = own_pad // 8
    own_groups = list(range(lead))
    cross_groups = list(range(lead, rows // 8))
    tiles, _ = halo_layout(own_pad)
    odd = lax.axis_index("cell") & 1

    @pl.when(odd == 0)
    def _():
        halo[1] = a_ref[...]
        halo[0] = b_ref[...]

    @pl.when(odd == 1)
    def _():
        halo[0] = a_ref[...]
        halo[1] = b_ref[...]

    def side_of(b):
        return (0, b + 2 * PB) if b < 0 else (1, b - nblk)

    for side in range(2):
        for i in range(2 * PB):
            tile = tiles[6] + i
            build_table(idx, wt, side * 2 * PB + i, halo[side, tile, NEIGH : 2 * NEIGH, :].astype(jnp.int32),
                        halo[side, tile, 0:NEIGH, :],
                        halo[side, spare_tile(tiles, side == 0, i), SPARE : SPARE + 1, :])

    def table(b):
        if 0 <= b < nblk:
            return idx_in, wt_in, b
        side, i = side_of(b)
        return idx, wt, side * 2 * PB + i

    def section(number, g, b, far=False):
        side, i = side_of(b)
        if (side == 1) == far:
            i -= PB
        return halo[side, tiles[number] + g * PB + i]

    def own(b):
        return 0 <= b < nblk

    def read_init(g, b):
        return init_ref[rows8(g), lanes(b)] if own(b) else section(0, g, b)

    ring = list(range(-PB, PB)) + list(range(nblk - PB, nblk + PB))
    place = {b: i for i, b in enumerate(ring)}

    def read_v1(g, b):
        return v1[rows8(g), lanes(place[b])]

    def coefs(b):
        if own(b):
            return jnp.zeros((1, LANES), jnp.float32)
        side, i = side_of(b)
        return halo[side, spare_tile(tiles, side == 0, i), SPARE : SPARE + 1, :]

    derive_cross = matrix_of(lead_ref, starts[0], rows, own_pad)
    for side in range(2):
        first = nblk if side else -PB
        values = jnp.concatenate(
            [
                jnp.concatenate([section(0, g, first + i) for i in range(PB)], axis=1)
                for g in own_groups
            ],
            axis=0,
        )
        turn = dot(derive_cross, values)
        for i in range(PB):
            b = first + i
            bf = coefficient(table(b))
            for g in cross_groups:
                v1[rows8(g), lanes(place[b])] = -bf * turn[rows8(g), lanes(i)]
            sums = stencil(read_init, b, table(b), own_groups, own)
            for g in own_groups:
                v1[rows8(g), lanes(place[b])] = section(1, g, b) + sums[g]
        for i in range(PB):
            b = nblk - PB + i if side else i
            at = lanes(side * PB + i)
            build_product(ut, side * PB + i, table(b), b, coefs)
            sums, pushes = stencil(
                read_init, b, table(b), own_groups, lambda s: not own(s), (ut, side * PB + i)
            )
            for g in own_groups:
                push[rows8(g), at] = push_ref[rows8(g), at] + pushes[g]
                v1[rows8(g), lanes(place[b])] = edge_ref[rows8(g), at] + sums[g]
            for g in cross_groups:
                v1[rows8(g), lanes(place[b])] = first_ref[rows8(g), lanes(b)]
    both = matrix_of(matrix_ref, starts[1], rows + MODES, rows)
    restrict = matrix_of(matrix_ref, starts[1] + rows, MODES, rows)
    low = -2 * PB
    for side in range(2):
        b = nblk if side else -PB
        m1x[:, lanes(b - low, PB)] = dot(restrict, v1[:, lanes(place[b], PB)])
        b = nblk - PB if side else 0
        mixed = dot(both, v1[:, lanes(place[b], PB)])
        deriv[:, lanes(side * PB, PB)] = mixed[0:rows]
        m1x[:, lanes(b - low, PB)] = mixed[rows:]
    m1x[:, lanes(PB - low, nblk - 2 * PB)] = m1i_ref[...]
    for b in list(range(-2 * PB, -PB)) + list(range(nblk + PB, nblk + 2 * PB)):
        for g in MODE_GROUPS:
            m1x[rows8(g), lanes(b - low)] = section(3, g, b, True)

    ends = list(range(PB)) + list(range(nblk - PB, nblk))
    couple = matrix_of(lead_ref, starts[0] + own_pad, rows - own_pad, own_pad)
    for side in range(2):
        turn = dot(couple, push[:, lanes(side * PB, PB)])
        for i in range(PB):
            b, at = ends[side * PB + i], lanes(side * PB + i)
            bf = coefficient(table(b))
            for g in cross_groups:
                part = rows8(g - lead)
                v2[part, at] = KEEP * read_v1(g, b) - bf * deriv[rows8(g), at] - turn[part, lanes(i)]

    def reader(ref, first):
        return lambda g, b: ref[rows8(g), lanes(b - first)]

    def modes(src, first, b, keep, known=None):
        read = reader(src, first)
        sums = stencil(read, b, table(b), MODE_GROUPS, known)
        if keep is None:
            return sums
        parts = turned([read(g, b) for g in MODE_GROUPS], table(b), keep)
        return [total + part for total, part in zip(sums, parts)]

    near = list(range(-PB, 0)) + list(range(nblk, nblk + PB))
    far = list(range(-2 * PB, -PB)) + list(range(nblk + PB, nblk + 2 * PB))
    for b in far:
        sums = modes(m1x, low, b, None, lambda s: s in place)
        for g in MODE_GROUPS:
            m2x[rows8(g), lanes(b - low)] = section(4, g, b, True) + sums[g]
    for b in near:
        sums = modes(m1x, low, b, KEEP)
        for g in MODE_GROUPS:
            m2x[rows8(g), lanes(b - low)] = section(2, g, b) + sums[g]
    for i, b in enumerate(ends):
        sums = modes(m1x, low, b, KEEP, lambda s: s in place)
        for g in MODE_GROUPS:
            m2x[rows8(g), lanes(b - low)] = mpart_ref[rows8(g), lanes(i)] + sums[g]
    m2x[:, lanes(2 * PB - low, nblk - 4 * PB)] = m2i_ref[:, lanes(PB, nblk - 4 * PB)]
    for b in list(range(PB, 2 * PB)) + list(range(nblk - 2 * PB, nblk - PB)):
        sums = modes(m1x, low, b, None, lambda s: s in place)
        for g in MODE_GROUPS:
            m2x[rows8(g), lanes(b - low)] = m2i_ref[rows8(g), lanes(b - PB)] + sums[g]

    middle = range(2 * PB, nblk - 2 * PB)
    for b in range(-2 * PB, nblk + 2 * PB):
        if b in middle:
            sums = modes(m2x, low, b, None, lambda s: s not in middle)
        elif own(b):
            sums = modes(m2x, low, b, -RELAX, lambda s: s not in middle)
        else:
            sums = modes(m2x, low, b, -RELAX, lambda s: -2 * PB <= s < nblk + 2 * PB)
        for g in MODE_GROUPS:
            if own(b):
                ready = rp_ref[rows8(g), lanes(b)]
            else:
                ready = section(5, g, b, True) if b in far else section(2, g, b)
            rx[rows8(g), lanes(b - low)] = ready + sums[g]
    for b in range(-PB, nblk + PB):
        sums = modes(rx, low, b, KEEP)
        for g in MODE_GROUPS:
            c1x[rows8(g), lanes(b + PB)] = sums[g] + rx[rows8(g), lanes(b - low)]
    for b in range(nblk):
        sums = modes(c1x, -PB, b, KEEP)
        for g in MODE_GROUPS:
            c2x[rows8(g), lanes(b)] = sums[g] + rx[rows8(g), lanes(b - low)]

    cross = rows - own_pad
    prolong = matrix_of(matrix_ref, starts[3] + own_pad, cross, MODES)
    for b in range(0, nblk, 2):
        values = c2x[:, lanes(b, 2)]
        if b in ends:
            at = lanes(ends.index(b), 2)
            send_ref[0:cross, at] = v2[:, at] + dot(prolong, values)
        else:
            fold, at = divmod(b - PB, 2 * PB)
            send_ref[cross + fold * MODES : cross + (fold + 1) * MODES, lanes(at, 2)] = values


def own_kernel(own_pad, starts, first, deriv, v1_ref, ends_ref, scaled_ref, c2_ref, idx_ref, wt_ref,
               matrix_ref, base_ref):
    cells = scaled_ref.shape[1]
    nblk = cells // LANES
    groups = list(range(own_pad // 8))
    ring = list(range(-PB, PB)) + list(range(nblk - PB, nblk + PB))
    ends = list(range(PB)) + list(range(nblk - PB, nblk))
    prolong = matrix_of(matrix_ref, starts[3], own_pad, MODES)

    def read(g, b):
        if b in ring:
            return v1_ref[rows8(g), lanes(ring.index(b))]
        return first[rows8(g), lanes(b)]

    for d in range(0, nblk, 2):
        lifted = dot(prolong, c2_ref[:, lanes(d, 2)])
        for b in range(d, d + 2):
            table = (idx_ref, wt_ref, b)
            bf = coefficient(table)
            sums = stencil(read, b, table, groups)
            for g in groups:
                if b in ends:
                    turn = ends_ref[rows8(g), lanes(ends.index(b))]
                else:
                    turn = deriv[rows8(g), lanes(b)]
                base_ref[rows8(g), lanes(b)] = (
                    KEEP * read(g, b)
                    + scaled_ref[rows8(g), lanes(b)]
                    - bf * turn
                    + sums[g]
                    + lifted[rows8(g), lanes(b - d)]
                )


def final_kernel(count, starts, base_ref, matrix_ref, *refs):
    out_hbm, out_ref, sems = refs[2 * count :]
    own_pad = base_ref.shape[0]
    nblk = out_ref.shape[1] // LANES
    early, late = refs[0 : 2 * count : 2], refs[1 : 2 * count : 2]
    copies = []
    ends = list(range(PB)) + list(range(nblk - PB, nblk))
    for b in range(0, nblk, 2):
        total = base_ref[:, lanes(b, 2)]
        for k in range(count):
            if b in ends:
                total = total + late[k][0:own_pad, lanes(ends.index(b), 2)]
            else:
                fold, at = divmod(b - PB, 2 * PB)
                lift = matrix_of(matrix_ref, starts[4 + k], own_pad, MODES)
                first = own_pad + fold * MODES
                total = (
                    total
                    + early[k][:, lanes(b - PB, 2)]
                    + dot(lift, late[k][first : first + MODES, lanes(at, 2)])
                )
        out_ref[:, lanes(b, 2)] = total
        if b % 4 == 2:
            piece = (slice(None), lanes(b - 2, 4))
            copies.append(pltpu.make_async_copy(out_ref.at[piece], out_hbm.at[piece], sems.at[b // 4]))
            copies[-1].start()
    for copy in copies:
        copy.wait()


def vm(*shape):
    return pltpu.VMEM(shape, jnp.float32)


def f32(*shape):
    return jax.ShapeDtypeStruct(shape, jnp.float32)


def call(kernel, out_shape, scratch, cost_us, *args, fetch=False, store=False):
    whole = pl.BlockSpec(memory_space=pltpu.VMEM)
    single = not isinstance(out_shape, (tuple, list))
    return pl.pallas_call(
        kernel,
        out_shape=out_shape,
        in_specs=[pl.BlockSpec(memory_space=pltpu.HBM) if fetch else whole] * len(args),
        out_specs=(pl.BlockSpec(memory_space=pltpu.HBM) if store else whole) if single else [whole] * len(out_shape),
        scratch_shapes=scratch,
        compiler_params=pltpu.CompilerParams(vmem_limit_bytes=16 * 1024 * 1024),
        cost_estimate=pl.CostEstimate(
            flops=int(cost_us * 1e8), bytes_accessed=int(cost_us * 3e6), transcendentals=0
        ),
    )(*args)


def per_device(initial, source, neighbors, face_weights, damping):
    own, cells = initial.shape
    nblk = cells // LANES
    inst_count = lax.axis_size("inst")
    cell_count = lax.axis_size("cell")
    own_pad = up8(own)
    lead, matrices, starts, rows = constants(own, inst_count)
    lead, matrices = jnp.asarray(lead), jnp.asarray(matrices)
    cross = rows - own_pad
    if own_pad != own:
        initial = jnp.pad(initial, ((0, own_pad - own), (0, 0)))
        source = jnp.pad(source, ((0, own_pad - own), (0, 0)))
    _, tiles = halo_layout(own_pad)
    assert nblk >= 8 * PB and nblk % 4 == 0
    slots = NEIGH * (PB + 1) + 4
    folds = -(-(nblk - 2 * PB) // (2 * PB))

    def wide(height, blocks):
        return f32(height, blocks * LANES)

    def scratch(height, blocks):
        return vm(height, blocks * LANES)

    def int32(*shape):
        return jax.ShapeDtypeStruct(shape, jnp.int32)

    pack_a, pack_b, initial, scaled, smode, ends, push, m1, m2, idx, wt, lead, matrices = call(
        functools.partial(pack_kernel, own_pad, starts),
        [f32(tiles, 8, LANES), f32(tiles, 8, LANES), wide(own_pad, nblk), wide(own_pad, nblk),
         wide(MODES, nblk), wide(own_pad, 2 * PB), wide(own_pad, 2 * PB), wide(MODES, nblk - 2 * PB),
         wide(MODES, nblk - 2 * PB),
         int32(nblk, 8, LANES), f32(nblk, slots, LANES),
         jax.ShapeDtypeStruct(lead.shape, lead.dtype),
         jax.ShapeDtypeStruct(matrices.shape, matrices.dtype)],
        [scratch(own_pad, nblk), pltpu.VMEM((NEIGH, cells), jnp.int32), vm(NEIGH, cells), vm(1, cells),
         vm(8, cells), scratch(MODES, nblk), scratch(MODES, nblk - 2 * PB), vm(2 * PB, slots, LANES),
         pltpu.SemaphoreType.DMA((9,))],
        2,
        *[
            pltpu.with_memory_space_constraint(x, pltpu.HBM)
            for x in (initial, source, neighbors, face_weights, damping.reshape(1, cells), lead, matrices)
        ],
        fetch=True,
    )
    near_pairs = [(i, i ^ 1) for i in range(cell_count) if i ^ 1 < cell_count]
    far_pairs = []
    for i in range(1, cell_count - 1, 2):
        far_pairs += [(i, i + 1), (i + 1, i)]
    halo_b = lax.ppermute(pack_b, "cell", far_pairs)
    halo_a = lax.ppermute(pack_a, "cell", near_pairs)

    cross_mid, first, deriv = call(
        functools.partial(cross_kernel, own_pad, rows, starts),
        [wide(cross, nblk - 2 * PB), wide(rows, nblk), wide(rows, nblk)],
        [scratch(own_pad, nblk - 2 * PB), vm(nblk - 2 * PB, slots, LANES)], 3,
        initial, scaled, idx, wt, lead, matrices,
    )

    def share(array, k):
        if cross == own_pad:
            return array
        part = lax.slice_in_dim(array, (k - 1) * own, k * own, axis=0)
        return jnp.pad(part, ((0, own_pad - own), (0, 0)))

    def shift(k):
        return [(i, (i + k) % inst_count) for i in range(inst_count)]

    early = [lax.ppermute(share(cross_mid, k), "inst", shift(k)) for k in range(1, inst_count)]

    mpart, m2, rp = call(
        inner_kernel,
        [wide(MODES, 2 * PB), wide(MODES, nblk - 2 * PB), wide(MODES, nblk)], [], 3,
        smode, m1, m2, idx, wt,
    )
    send, v1, dends, c2 = call(
        functools.partial(outer_kernel, own_pad, rows, starts),
        [wide(cross + folds * MODES, 2 * PB), wide(rows, 4 * PB), wide(rows, 2 * PB), wide(MODES, nblk)],
        [pltpu.VMEM((2, tiles, 8, LANES), jnp.float32), scratch(cross, 2 * PB),
         scratch(own_pad, 2 * PB), scratch(MODES, nblk + 4 * PB), scratch(MODES, nblk + 4 * PB),
         scratch(MODES, nblk + 4 * PB), scratch(MODES, nblk + 2 * PB),
         pltpu.VMEM((4 * PB, 8, LANES), jnp.int32), vm(4 * PB, slots, LANES), vm(2 * PB, slots, LANES)],
        8, halo_a, halo_b, initial, smode, ends, push, mpart, first, m1, m2, rp, idx, wt, lead, matrices,
    )

    def share_late(k):
        if cross == own_pad:
            return send
        return jnp.concatenate([share(send[:cross], k), send[cross:]], axis=0)

    late = [lax.ppermute(share_late(k), "inst", shift(k)) for k in range(1, inst_count)]
    base = call(
        functools.partial(own_kernel, own_pad, starts), wide(own_pad, nblk), [], 2,
        first, deriv, v1, dends, scaled, c2, idx, wt, matrices,
    )
    received = [r for pair in zip(early, late) for r in pair]
    out = call(
        functools.partial(final_kernel, inst_count - 1, starts), f32(own_pad, cells),
        [vm(own_pad, cells), pltpu.SemaphoreType.DMA((nblk // 4,))], 1,
        base, matrices, *received, store=True,
    )
    return out[:own] if own_pad != own else out


def solution(mesh):
    return jax.shard_map(
        per_device,
        mesh=mesh,
        in_specs=(
            P("inst", "cell"),
            P("inst", "cell"),
            P(None, "cell"),
            P(None, "cell"),
            P("cell"),
        ),
        out_specs=P("inst", "cell"),
        check_vma=False,
    )
```

```python
import functools

import jax
import jax.numpy as jnp
import numpy as np
from jax import lax
from jax.experimental import pallas as pl
from jax.experimental.pallas import tpu as pltpu
from jax.sharding import PartitionSpec as P


NI = 16
COMP = 5
NEIGH = 4
PLANE = 256
FREQ = 0.15
RELAX = 0.6
KEEP = 1.0 - RELAX

LANES = 128
PB = PLANE // LANES
MODES = 16


def up8(count):
    return -(-count // 8) * 8


def row_map(own):
    rows = [divmod(r, COMP) for r in range(own)]
    rows += [None] * (up8(own) - own)
    other = NI * COMP - own
    rows += [divmod(own + r, COMP) for r in range(other)]
    rows += [None] * (up8(other) - other)
    return rows


def mode_row(h, c):
    if h:
        return 8 * (h - 1) + 3 + c
    return c if c < 3 else 5 + c


def split_matrix(matrix):
    high = matrix.astype(jnp.bfloat16)
    low = (matrix - high.astype(np.float64)).astype(jnp.bfloat16)
    return np.concatenate([high, low, high], axis=1)


def constants(own, inst_count):
    rows = row_map(own)
    own_pad = up8(own)
    count = len(rows)
    derive = np.zeros((count, count))
    restrict = np.zeros((MODES, count))
    prolong = np.zeros((count, MODES))
    for i, left in enumerate(rows):
        if left is None:
            continue
        n, c = left
        phase = 2.0 * np.pi * n / NI
        shape = (1.0, np.cos(phase), np.sin(phase))
        for h in range(3):
            restrict[mode_row(h, c), i] = shape[h] * (1.0 if h == 0 else 2.0) / NI
            prolong[i, mode_row(h, c)] = shape[h]
        for j, right in enumerate(rows):
            if right is not None and right[1] == c and right[0] != n:
                gap = n - right[0]
                derive[i, j] = 0.5 * (-1.0) ** gap / np.tan(np.pi * gap / NI)
    other = prolong[own_pad:]
    lifts = []
    for k in range(1, inst_count):
        lift = np.zeros((own_pad, MODES))
        lift[:own] = other[(k - 1) * own : k * own]
        lifts.append(lift)
    early = [derive[:, :own_pad], restrict[:, :own_pad]]
    late = [np.concatenate([derive, restrict]), prolong] + lifts
    (lead, lead_starts), (rest, rest_starts) = stack(early), stack(late)
    starts = [lead_starts[0], rest_starts[0], lead_starts[1]] + rest_starts[1:]
    return lead, rest, starts, count


def stack(parts):
    wides = [split_matrix(part) for part in parts]
    width = -(-max(wide.shape[1] for wide in wides) // LANES) * LANES
    blocks, starts, at = [], [], 0
    for wide in wides:
        height = -(-wide.shape[0] // 16) * 16
        blocks.append(np.pad(wide, ((0, height - wide.shape[0]), (0, width - wide.shape[1]))))
        starts.append(at)
        at += height
    return np.concatenate(blocks), starts


def split3(values):
    high = values.astype(jnp.bfloat16).astype(jnp.float32)
    return jnp.concatenate([values, values, values - high], axis=0).astype(jnp.bfloat16)


def dot(matrix, values):
    return jnp.dot(matrix, split3(values), preferred_element_type=jnp.float32)


def matrix_of(ref, start, height, depth):
    return ref[start : start + height, 0 : 3 * depth]


def lanes(start, count=1):
    return slice(start * LANES, (start + count) * LANES)


def build_table(idx_ref, wt_ref, at, near, bw, bf):
    target = near + lax.broadcasted_iota(jnp.int32, near.shape, 1)
    slot = lax.broadcasted_iota(jnp.int32, near.shape, 0)
    base = (target >> 7) + jnp.where((slot & 1) == 0, PB, 0)
    idx_ref[at, 0:NEIGH, :] = target & (LANES - 1)
    idx_ref[at, NEIGH : 2 * NEIGH, :] = target & (LANES - 1)
    for j in range(PB + 1):
        wt_ref[at, NEIGH * j : NEIGH * (j + 1), :] = jnp.where(base == j, bw, 0.0)
    wt_ref[at, NEIGH * (PB + 1) : NEIGH * (PB + 1) + 1, :] = bf


def build_product(ut_ref, at, table, block, coefs):
    idx_ref, wt_ref, to = table
    even = (lax.broadcasted_iota(jnp.int32, (8, LANES), 0) & 1) == 0
    for j in range(PB + 1):
        low = jnp.broadcast_to(coefs(block + j - PB), (8, LANES))
        high = jnp.broadcast_to(coefs(block + j), (8, LANES))
        taken = jnp.take_along_axis(jnp.where(even, low, high), idx_ref[to], axis=1)
        part = slice(NEIGH * j, NEIGH * (j + 1))
        ut_ref[at, part, :] = wt_ref[to, part, :] * taken[0:NEIGH]


def coefficient(table):
    _, wt_ref, at = table
    return wt_ref[at, pl.ds(NEIGH * (PB + 1), 8, stride=0), :]


def stencil(read, block, table, groups, known=None, product=None):
    idx_ref, wt_ref, at = table
    sums, others, cache = [0.0] * len(groups), [0.0] * len(groups), {}

    def source(g, b):
        if (g, b) not in cache:
            cache[g, b] = read(g, b)
        return cache[g, b]

    for k in range(NEIGH):
        index = None
        for j in range(PB + 1):
            b = block + j - (0 if k % 2 else PB)
            if known is not None and not known(b):
                continue
            if index is None:
                index = idx_ref[at, pl.ds(k, 8, stride=0), :]
            row = pl.ds(NEIGH * j + k, 8, stride=0)
            weight = wt_ref[at, row, :]
            if product is not None:
                other = product[0][product[1], row, :]
            for i, g in enumerate(groups):
                taken = jnp.take_along_axis(source(g, b), index, axis=1)
                sums[i] = sums[i] + weight * taken
                if product is not None:
                    others[i] = others[i] + other * taken
    return sums if product is None else (sums, others)


def turned(values, table, keep):
    top = lax.broadcasted_iota(jnp.int32, (8, LANES), 0) >= 3
    bf = jnp.where(top, coefficient(table), 0.0)
    low, high = values
    return keep * low - bf * high, keep * high + bf * low


def rows8(g):
    return slice(8 * g, 8 * g + 8)


MODE_GROUPS = list(range(MODES // 8))


def halo_layout(own_pad):
    fine, mode = own_pad // 8 * PB, MODES // 8 * PB
    sizes = [fine, fine, mode, mode, mode, mode, 2 * PB]
    starts = [sum(sizes[:i]) for i in range(len(sizes))]
    return starts, sum(sizes)


SPARE = 2


def spare_tile(tiles, near_last, i):
    return tiles[2 if (i >= PB) == bool(near_last) else 3] + PB + i % PB


def pack_kernel(own_pad, starts, init_hbm, src_hbm, near_hbm, face_hbm, damp_hbm, lead_hbm, matrix_hbm,
                a_ref, b_ref, init_ref, scaled_ref, mode_ref, edge_ref, push_ref, m1, m2, idx_ref, wt_ref,
                lead_ref, matrix_ref,
                src_ref, near_ref, face_ref, damp_ref, coef_ref, m0, rp, ut, sems):
    cells = init_ref.shape[1]
    nblk = cells // LANES
    half = own_pad // 16 * 8
    copies = [
        pltpu.make_async_copy(face_hbm, face_ref, sems.at[0]),
        pltpu.make_async_copy(damp_hbm, damp_ref, sems.at[1]),
        pltpu.make_async_copy(near_hbm, near_ref, sems.at[2]),
        pltpu.make_async_copy(lead_hbm, lead_ref, sems.at[3]),
        pltpu.make_async_copy(init_hbm.at[0:half], init_ref.at[0:half], sems.at[4]),
        pltpu.make_async_copy(init_hbm.at[half:own_pad], init_ref.at[half:own_pad], sems.at[5]),
        pltpu.make_async_copy(src_hbm.at[0:half], src_ref.at[0:half], sems.at[6]),
        pltpu.make_async_copy(src_hbm.at[half:own_pad], src_ref.at[half:own_pad], sems.at[7]),
        pltpu.make_async_copy(matrix_hbm, matrix_ref, sems.at[8]),
    ]
    for copy in copies:
        copy.start()
    for copy in copies[0:3]:
        copy.wait()
    face = face_ref[...]
    inverse = RELAX / (damp_ref[...] + jnp.sum(face, axis=0, keepdims=True))
    coef_ref[0:NEIGH, :] = inverse * face
    coef_ref[NEIGH : NEIGH + 1, :] = FREQ * inverse
    for b in range(nblk):
        build_table(idx_ref, wt_ref, b, near_ref[:, lanes(b)],
                    coef_ref[0:NEIGH, lanes(b)], coef_ref[NEIGH : NEIGH + 1, lanes(b)])

    def table(b):
        return idx_ref, wt_ref, b

    def reader(ref, first=0):
        return lambda g, b: ref[rows8(g), lanes(b - first)]

    def coefs(s):
        if not 0 <= s < nblk:
            return jnp.zeros((1, LANES), jnp.float32)
        return coef_ref[NEIGH : NEIGH + 1, lanes(s)]

    ends = list(range(PB)) + list(range(nblk - PB, nblk))
    for i, b in enumerate(ends):
        build_product(ut, i, table(b), b, coefs)
    for copy in copies[3:6]:
        copy.wait()
    groups = list(range(own_pad // 8))
    restrict = matrix_of(lead_ref, starts[2], MODES, own_pad)
    derive = matrix_of(lead_ref, starts[0], own_pad, own_pad)
    for d in range(0, nblk, 2):
        m0[:, lanes(d, 2)] = dot(restrict, init_ref[:, lanes(d, 2)])

    for side in range(2):
        at = side * (nblk - PB)
        deriv = dot(derive, init_ref[:, lanes(at, PB)])
        for i in range(PB):
            b, here = at + i, lanes(side * PB + i)
            sums, pushes = stencil(
                reader(init_ref), b, table(b), groups, lambda s: 0 <= s < nblk, (ut, side * PB + i)
            )
            bf = coefficient(table(b))
            for g in groups:
                push_ref[rows8(g), here] = pushes[g]
                edge_ref[rows8(g), here] = (
                    KEEP * init_ref[rows8(g), lanes(b)] - bf * deriv[rows8(g), lanes(i)] + sums[g]
                )
    for copy in copies[6:8]:
        copy.wait()
    for g in groups:
        scaled_ref[rows8(g), :] = src_ref[rows8(g), :] * inverse
    for i, b in enumerate(ends):
        for g in groups:
            edge_ref[rows8(g), lanes(i)] = edge_ref[rows8(g), lanes(i)] + scaled_ref[rows8(g), lanes(b)]
    for d in range(0, nblk, 2):
        mode_ref[:, lanes(d, 2)] = dot(restrict, scaled_ref[:, lanes(d, 2)])

    def modes(src, first, out, to, b, known, keep):
        sums = stencil(reader(src, first), b, table(b), MODE_GROUPS, known)
        parts = (0.0, 0.0)
        if keep is not None:
            parts = turned([src[rows8(g), lanes(b - first)] for g in MODE_GROUPS], table(b), keep)
        for g in MODE_GROUPS:
            out[rows8(g), lanes(to)] = parts[g] + sums[g] + mode_ref[rows8(g), lanes(b)]

    near, far, deep = range(PB), range(PB, 2 * PB), range(2 * PB, 3 * PB)
    for b in range(PB, nblk - PB):
        modes(m0, 0, m1, b - PB, b, None, KEEP)
    for side in range(2):
        for d in list(far) + list(deep):
            b = nblk - 1 - d if side else d
            modes(m1, PB, m2, b - PB, b, lambda s: PB <= s < nblk - PB, KEEP)
    for side in range(2):
        for d in far:
            b = nblk - 1 - d if side else d
            known = [nblk - 1 - e if side else e for e in deep]
            modes(m2, PB, rp, b - PB, b, lambda s, known=known: s in known, None)

    near = near_ref[...].astype(jnp.float32)
    first_tiles, _ = halo_layout(own_pad)

    def pack(out, high):
        near_at = nblk - PB if high else 0
        far_at = nblk - 2 * PB if high else PB
        edge_at = PB if high else 0
        all_at = nblk - 2 * PB if high else 0
        for i in range(PB):
            for g in groups:
                out[first_tiles[0] + g * PB + i] = init_ref[rows8(g), lanes(near_at + i)]
                out[first_tiles[1] + g * PB + i] = edge_ref[rows8(g), lanes(edge_at + i)]
            for g in MODE_GROUPS:
                t = g * PB + i
                out[first_tiles[2] + t] = mode_ref[rows8(g), lanes(near_at + i)]
                out[first_tiles[3] + t] = m1[rows8(g), lanes(far_at + i - PB)]
                out[first_tiles[4] + t] = m2[rows8(g), lanes(far_at + i - PB)]
                out[first_tiles[5] + t] = rp[rows8(g), lanes(far_at + i - PB)]
        for i in range(2 * PB):
            out[first_tiles[6] + i, 0:NEIGH, :] = coef_ref[0:NEIGH, lanes(all_at + i)]
            out[first_tiles[6] + i, NEIGH : 2 * NEIGH, :] = near[:, lanes(all_at + i)]
            out[spare_tile(first_tiles, high, i), SPARE : SPARE + 1, :] = coef_ref[NEIGH : NEIGH + 1, lanes(all_at + i)]

    odd = lax.axis_index("cell") & 1

    @pl.when(odd == 0)
    def _():
        pack(a_ref, True)
        pack(b_ref, False)

    @pl.when(odd == 1)
    def _():
        pack(a_ref, False)
        pack(b_ref, True)

    copies[8].wait()


def cross_kernel(own_pad, rows, starts, init_ref, scaled_ref, idx_ref, wt_ref, lead_ref, matrix_ref,
                 cross_ref, first, deriv, push, ut):
    cells = init_ref.shape[1]
    nblk = cells // LANES
    own_groups = list(range(own_pad // 8))
    cross_groups = list(range(own_pad // 8, rows // 8))

    def table(b):
        return idx_ref, wt_ref, b

    derive = matrix_of(lead_ref, starts[0], rows, own_pad)
    for d in range(0, nblk, 2):
        deriv[:, lanes(d, 2)] = dot(derive, init_ref[:, lanes(d, 2)])

    def read_init(g, b):
        return init_ref[rows8(g), lanes(b)]

    def read_first(g, b):
        return first[rows8(g), lanes(b)]

    inside = range(PB, nblk - PB)

    def coefs(s):
        return wt_ref[s, NEIGH * (PB + 1) : NEIGH * (PB + 1) + 1, :]

    for b in range(nblk):
        bf = coefficient(table(b))
        for g in cross_groups:
            first[rows8(g), lanes(b)] = -bf * deriv[rows8(g), lanes(b)]
        if b in inside:
            build_product(ut, b - PB, table(b), b, coefs)
            sums, pushes = stencil(read_init, b, table(b), own_groups, None, (ut, b - PB))
            for g in own_groups:
                push[rows8(g), lanes(b - PB)] = pushes[g]
                first[rows8(g), lanes(b)] = (
                    KEEP * init_ref[rows8(g), lanes(b)]
                    + scaled_ref[rows8(g), lanes(b)]
                    - bf * deriv[rows8(g), lanes(b)]
                    + sums[g]
                )
    derive = matrix_of(matrix_ref, starts[1], rows, rows)
    couple = matrix_of(lead_ref, starts[0] + own_pad, rows - own_pad, own_pad)
    for d in range(PB, nblk - PB, 2):
        deriv[:, lanes(d, 2)] = dot(derive, first[:, lanes(d, 2)])
        turn = dot(couple, push[:, lanes(d - PB, 2)])
        for b in range(d, d + 2):
            bf = coefficient(table(b))
            for g in cross_groups:
                part = rows8(g - len(own_groups))
                cross_ref[part, lanes(b - PB)] = (
                    KEEP * read_first(g, b) - bf * deriv[rows8(g), lanes(b)] - turn[part, lanes(b - d)]
                )


def inner_kernel(smode_ref, m1_ref, m2_ref, idx_ref, wt_ref, mpart_ref, m2_out, rp_ref):
    cells = smode_ref.shape[1]
    nblk = cells // LANES
    inside = range(PB, nblk - PB)
    middle = range(2 * PB, nblk - 2 * PB)
    ends = list(range(PB)) + list(range(nblk - PB, nblk))

    def table(b):
        return idx_ref, wt_ref, b

    def read_m1(g, b):
        return m1_ref[rows8(g), lanes(b - PB)]

    def read_m2(g, b):
        return m2_out[rows8(g), lanes(b - PB)]

    m2_out[...] = m2_ref[...]
    for b in range(3 * PB, nblk - 3 * PB):
        sums = stencil(read_m1, b, table(b), MODE_GROUPS)
        parts = turned([read_m1(g, b) for g in MODE_GROUPS], table(b), KEEP)
        for g in MODE_GROUPS:
            m2_out[rows8(g), lanes(b - PB)] = parts[g] + sums[g] + smode_ref[rows8(g), lanes(b)]
    for i, b in enumerate(ends):
        sums = stencil(read_m1, b, table(b), MODE_GROUPS, lambda s: s in inside)
        for g in MODE_GROUPS:
            mpart_ref[rows8(g), lanes(i)] = sums[g] + smode_ref[rows8(g), lanes(b)]
    for b in range(nblk):
        sums = stencil(read_m2, b, table(b), MODE_GROUPS, lambda s: s in middle)
        if b in middle:
            parts = turned([read_m2(g, b) for g in MODE_GROUPS], table(b), -RELAX)
            sums = [total + part for total, part in zip(sums, parts)]
        for g in MODE_GROUPS:
            rp_ref[rows8(g), lanes(b)] = sums[g] + smode_ref[rows8(g), lanes(b)]


def outer_kernel(own_pad, rows, starts, a_ref, b_ref, init_ref, smode_ref, edge_ref,
                 push_ref, mpart_ref, first_ref, m1i_ref, m2i_ref, rp_ref, idx_in, wt_in,
                 lead_ref, matrix_ref, send_ref, v1, deriv, c2x,
                 halo, v2, push, m1x, m2x, rx, c1x, idx, wt, ut):
    cells = init_ref.shape[1]
    nblk = cells // LANES
    lead = own_pad // 8
    own_groups = list(range(lead))
    cross_groups = list(range(lead, rows // 8))
    tiles, _ = halo_layout(own_pad)
    odd = lax.axis_index("cell") & 1

    @pl.when(odd == 0)
    def _():
        halo[1] = a_ref[...]
        halo[0] = b_ref[...]

    @pl.when(odd == 1)
    def _():
        halo[0] = a_ref[...]
        halo[1] = b_ref[...]

    def side_of(b):
        return (0, b + 2 * PB) if b < 0 else (1, b - nblk)

    for side in range(2):
        for i in range(2 * PB):
            tile = tiles[6] + i
            build_table(idx, wt, side * 2 * PB + i, halo[side, tile, NEIGH : 2 * NEIGH, :].astype(jnp.int32),
                        halo[side, tile, 0:NEIGH, :],
                        halo[side, spare_tile(tiles, side == 0, i), SPARE : SPARE + 1, :])

    def table(b):
        if 0 <= b < nblk:
            return idx_in, wt_in, b
        side, i = side_of(b)
        return idx, wt, side * 2 * PB + i

    def section(number, g, b, far=False):
        side, i = side_of(b)
        if (side == 1) == far:
            i -= PB
        return halo[side, tiles[number] + g * PB + i]

    def own(b):
        return 0 <= b < nblk

    def read_init(g, b):
        return init_ref[rows8(g), lanes(b)] if own(b) else section(0, g, b)

    ring = list(range(-PB, PB)) + list(range(nblk - PB, nblk + PB))
    place = {b: i for i, b in enumerate(ring)}

    def read_v1(g, b):
        return v1[rows8(g), lanes(place[b])]

    def coefs(b):
        if own(b):
            return jnp.zeros((1, LANES), jnp.float32)
        side, i = side_of(b)
        return halo[side, spare_tile(tiles, side == 0, i), SPARE : SPARE + 1, :]

    derive_cross = matrix_of(lead_ref, starts[0], rows, own_pad)
    for side in range(2):
        first = nblk if side else -PB
        values = jnp.concatenate(
            [
                jnp.concatenate([section(0, g, first + i) for i in range(PB)], axis=1)
                for g in own_groups
            ],
            axis=0,
        )
        turn = dot(derive_cross, values)
        for i in range(PB):
            b = first + i
            bf = coefficient(table(b))
            for g in cross_groups:
                v1[rows8(g), lanes(place[b])] = -bf * turn[rows8(g), lanes(i)]
            sums = stencil(read_init, b, table(b), own_groups, own)
            for g in own_groups:
                v1[rows8(g), lanes(place[b])] = section(1, g, b) + sums[g]
        for i in range(PB):
            b = nblk - PB + i if side else i
            at = lanes(side * PB + i)
            build_product(ut, side * PB + i, table(b), b, coefs)
            sums, pushes = stencil(
                read_init, b, table(b), own_groups, lambda s: not own(s), (ut, side * PB + i)
            )
            for g in own_groups:
                push[rows8(g), at] = push_ref[rows8(g), at] + pushes[g]
                v1[rows8(g), lanes(place[b])] = edge_ref[rows8(g), at] + sums[g]
            for g in cross_groups:
                v1[rows8(g), lanes(place[b])] = first_ref[rows8(g), lanes(b)]
    both = matrix_of(matrix_ref, starts[1], rows + MODES, rows)
    restrict = matrix_of(matrix_ref, starts[1] + rows, MODES, rows)
    low = -2 * PB
    for side in range(2):
        b = nblk if side else -PB
        m1x[:, lanes(b - low, PB)] = dot(restrict, v1[:, lanes(place[b], PB)])
        b = nblk - PB if side else 0
        mixed = dot(both, v1[:, lanes(place[b], PB)])
        deriv[:, lanes(side * PB, PB)] = mixed[0:rows]
        m1x[:, lanes(b - low, PB)] = mixed[rows:]
    m1x[:, lanes(PB - low, nblk - 2 * PB)] = m1i_ref[...]
    for b in list(range(-2 * PB, -PB)) + list(range(nblk + PB, nblk + 2 * PB)):
        for g in MODE_GROUPS:
            m1x[rows8(g), lanes(b - low)] = section(3, g, b, True)

    ends = list(range(PB)) + list(range(nblk - PB, nblk))
    couple = matrix_of(lead_ref, starts[0] + own_pad, rows - own_pad, own_pad)
    for side in range(2):
        turn = dot(couple, push[:, lanes(side * PB, PB)])
        for i in range(PB):
            b, at = ends[side * PB + i], lanes(side * PB + i)
            bf = coefficient(table(b))
            for g in cross_groups:
                part = rows8(g - lead)
                v2[part, at] = KEEP * read_v1(g, b) - bf * deriv[rows8(g), at] - turn[part, lanes(i)]

    def reader(ref, first):
        return lambda g, b: ref[rows8(g), lanes(b - first)]

    def modes(src, first, b, keep, known=None):
        read = reader(src, first)
        sums = stencil(read, b, table(b), MODE_GROUPS, known)
        if keep is None:
            return sums
        parts = turned([read(g, b) for g in MODE_GROUPS], table(b), keep)
        return [total + part for total, part in zip(sums, parts)]

    near = list(range(-PB, 0)) + list(range(nblk, nblk + PB))
    far = list(range(-2 * PB, -PB)) + list(range(nblk + PB, nblk + 2 * PB))
    for b in far:
        sums = modes(m1x, low, b, None, lambda s: s in place)
        for g in MODE_GROUPS:
            m2x[rows8(g), lanes(b - low)] = section(4, g, b, True) + sums[g]
    for b in near:
        sums = modes(m1x, low, b, KEEP)
        for g in MODE_GROUPS:
            m2x[rows8(g), lanes(b - low)] = section(2, g, b) + sums[g]
    for i, b in enumerate(ends):
        sums = modes(m1x, low, b, KEEP, lambda s: s in place)
        for g in MODE_GROUPS:
            m2x[rows8(g), lanes(b - low)] = mpart_ref[rows8(g), lanes(i)] + sums[g]
    m2x[:, lanes(2 * PB - low, nblk - 4 * PB)] = m2i_ref[:, lanes(PB, nblk - 4 * PB)]
    for b in list(range(PB, 2 * PB)) + list(range(nblk - 2 * PB, nblk - PB)):
        sums = modes(m1x, low, b, None, lambda s: s in place)
        for g in MODE_GROUPS:
            m2x[rows8(g), lanes(b - low)] = m2i_ref[rows8(g), lanes(b - PB)] + sums[g]

    middle = range(2 * PB, nblk - 2 * PB)
    for b in range(-2 * PB, nblk + 2 * PB):
        if b in middle:
            sums = modes(m2x, low, b, None, lambda s: s not in middle)
        elif own(b):
            sums = modes(m2x, low, b, -RELAX, lambda s: s not in middle)
        else:
            sums = modes(m2x, low, b, -RELAX, lambda s: -2 * PB <= s < nblk + 2 * PB)
        for g in MODE_GROUPS:
            if own(b):
                ready = rp_ref[rows8(g), lanes(b)]
            else:
                ready = section(5, g, b, True) if b in far else section(2, g, b)
            rx[rows8(g), lanes(b - low)] = ready + sums[g]
    for b in range(-PB, nblk + PB):
        sums = modes(rx, low, b, KEEP)
        for g in MODE_GROUPS:
            c1x[rows8(g), lanes(b + PB)] = sums[g] + rx[rows8(g), lanes(b - low)]
    for b in range(nblk):
        sums = modes(c1x, -PB, b, KEEP)
        for g in MODE_GROUPS:
            c2x[rows8(g), lanes(b)] = sums[g] + rx[rows8(g), lanes(b - low)]

    cross = rows - own_pad
    prolong = matrix_of(matrix_ref, starts[3] + own_pad, cross, MODES)
    for b in range(0, nblk, 2):
        values = c2x[:, lanes(b, 2)]
        if b in ends:
            at = lanes(ends.index(b), 2)
            send_ref[0:cross, at] = v2[:, at] + dot(prolong, values)
        else:
            fold, at = divmod(b - PB, 2 * PB)
            send_ref[cross + fold * MODES : cross + (fold + 1) * MODES, lanes(at, 2)] = values


def own_kernel(own_pad, starts, first, deriv, v1_ref, ends_ref, scaled_ref, c2_ref, idx_ref, wt_ref,
               matrix_ref, base_ref):
    cells = scaled_ref.shape[1]
    nblk = cells // LANES
    groups = list(range(own_pad // 8))
    ring = list(range(-PB, PB)) + list(range(nblk - PB, nblk + PB))
    ends = list(range(PB)) + list(range(nblk - PB, nblk))
    prolong = matrix_of(matrix_ref, starts[3], own_pad, MODES)

    def read(g, b):
        if b in ring:
            return v1_ref[rows8(g), lanes(ring.index(b))]
        return first[rows8(g), lanes(b)]

    for d in range(0, nblk, 2):
        lifted = dot(prolong, c2_ref[:, lanes(d, 2)])
        for b in range(d, d + 2):
            table = (idx_ref, wt_ref, b)
            bf = coefficient(table)
            sums = stencil(read, b, table, groups)
            for g in groups:
                if b in ends:
                    turn = ends_ref[rows8(g), lanes(ends.index(b))]
                else:
                    turn = deriv[rows8(g), lanes(b)]
                base_ref[rows8(g), lanes(b)] = (
                    KEEP * read(g, b)
                    + scaled_ref[rows8(g), lanes(b)]
                    - bf * turn
                    + sums[g]
                    + lifted[rows8(g), lanes(b - d)]
                )


def final_kernel(count, starts, base_ref, matrix_ref, *refs):
    out_hbm, out_ref, sems = refs[2 * count :]
    own_pad = base_ref.shape[0]
    nblk = out_ref.shape[1] // LANES
    early, late = refs[0 : 2 * count : 2], refs[1 : 2 * count : 2]
    copies = []
    ends = list(range(PB)) + list(range(nblk - PB, nblk))
    for b in range(0, nblk, 2):
        total = base_ref[:, lanes(b, 2)]
        for k in range(count):
            if b in ends:
                total = total + late[k][0:own_pad, lanes(ends.index(b), 2)]
            else:
                fold, at = divmod(b - PB, 2 * PB)
                lift = matrix_of(matrix_ref, starts[4 + k], own_pad, MODES)
                first = own_pad + fold * MODES
                total = (
                    total
                    + early[k][:, lanes(b - PB, 2)]
                    + dot(lift, late[k][first : first + MODES, lanes(at, 2)])
                )
        out_ref[:, lanes(b, 2)] = total
        piece = (slice(None), lanes(b, 2))
        copies.append(pltpu.make_async_copy(out_ref.at[piece], out_hbm.at[piece], sems.at[b // 2]))
        copies[-1].start()
    for copy in copies:
        copy.wait()


def vm(*shape):
    return pltpu.VMEM(shape, jnp.float32)


def f32(*shape):
    return jax.ShapeDtypeStruct(shape, jnp.float32)


def call(kernel, out_shape, scratch, cost_us, *args, fetch=False, store=False):
    whole = pl.BlockSpec(memory_space=pltpu.VMEM)
    single = not isinstance(out_shape, (tuple, list))
    return pl.pallas_call(
        kernel,
        out_shape=out_shape,
        in_specs=[pl.BlockSpec(memory_space=pltpu.HBM) if fetch else whole] * len(args),
        out_specs=(pl.BlockSpec(memory_space=pltpu.HBM) if store else whole) if single else [whole] * len(out_shape),
        scratch_shapes=scratch,
        compiler_params=pltpu.CompilerParams(vmem_limit_bytes=16 * 1024 * 1024),
        cost_estimate=pl.CostEstimate(
            flops=int(cost_us * 1e8), bytes_accessed=int(cost_us * 3e6), transcendentals=0
        ),
    )(*args)


def per_device(initial, source, neighbors, face_weights, damping):
    own, cells = initial.shape
    nblk = cells // LANES
    inst_count = lax.axis_size("inst")
    cell_count = lax.axis_size("cell")
    own_pad = up8(own)
    lead, matrices, starts, rows = constants(own, inst_count)
    lead, matrices = jnp.asarray(lead), jnp.asarray(matrices)
    cross = rows - own_pad
    if own_pad != own:
        initial = jnp.pad(initial, ((0, own_pad - own), (0, 0)))
        source = jnp.pad(source, ((0, own_pad - own), (0, 0)))
    _, tiles = halo_layout(own_pad)
    assert nblk >= 8 * PB and nblk % 4 == 0
    slots = NEIGH * (PB + 1) + 4
    folds = -(-(nblk - 2 * PB) // (2 * PB))

    def wide(height, blocks):
        return f32(height, blocks * LANES)

    def scratch(height, blocks):
        return vm(height, blocks * LANES)

    def int32(*shape):
        return jax.ShapeDtypeStruct(shape, jnp.int32)

    pack_a, pack_b, initial, scaled, smode, ends, push, m1, m2, idx, wt, lead, matrices = call(
        functools.partial(pack_kernel, own_pad, starts),
        [f32(tiles, 8, LANES), f32(tiles, 8, LANES), wide(own_pad, nblk), wide(own_pad, nblk),
         wide(MODES, nblk), wide(own_pad, 2 * PB), wide(own_pad, 2 * PB), wide(MODES, nblk - 2 * PB),
         wide(MODES, nblk - 2 * PB),
         int32(nblk, 8, LANES), f32(nblk, slots, LANES),
         jax.ShapeDtypeStruct(lead.shape, lead.dtype),
         jax.ShapeDtypeStruct(matrices.shape, matrices.dtype)],
        [scratch(own_pad, nblk), pltpu.VMEM((NEIGH, cells), jnp.int32), vm(NEIGH, cells), vm(1, cells),
         vm(8, cells), scratch(MODES, nblk), scratch(MODES, nblk - 2 * PB), vm(2 * PB, slots, LANES),
         pltpu.SemaphoreType.DMA((9,))],
        2,
        *[
            pltpu.with_memory_space_constraint(x, pltpu.HBM)
            for x in (initial, source, neighbors, face_weights, damping.reshape(1, cells), lead, matrices)
        ],
        fetch=True,
    )
    near_pairs = [(i, i ^ 1) for i in range(cell_count) if i ^ 1 < cell_count]
    far_pairs = []
    for i in range(1, cell_count - 1, 2):
        far_pairs += [(i, i + 1), (i + 1, i)]
    halo_b = lax.ppermute(pack_b, "cell", far_pairs)
    halo_a = lax.ppermute(pack_a, "cell", near_pairs)

    cross_mid, first, deriv = call(
        functools.partial(cross_kernel, own_pad, rows, starts),
        [wide(cross, nblk - 2 * PB), wide(rows, nblk), wide(rows, nblk)],
        [scratch(own_pad, nblk - 2 * PB), vm(nblk - 2 * PB, slots, LANES)], 3,
        initial, scaled, idx, wt, lead, matrices,
    )

    def share(array, k):
        if cross == own_pad:
            return array
        part = lax.slice_in_dim(array, (k - 1) * own, k * own, axis=0)
        return jnp.pad(part, ((0, own_pad - own), (0, 0)))

    def shift(k):
        return [(i, (i + k) % inst_count) for i in range(inst_count)]

    early = [lax.ppermute(share(cross_mid, k), "inst", shift(k)) for k in range(1, inst_count)]

    mpart, m2, rp = call(
        inner_kernel,
        [wide(MODES, 2 * PB), wide(MODES, nblk - 2 * PB), wide(MODES, nblk)], [], 3,
        smode, m1, m2, idx, wt,
    )
    send, v1, dends, c2 = call(
        functools.partial(outer_kernel, own_pad, rows, starts),
        [wide(cross + folds * MODES, 2 * PB), wide(rows, 4 * PB), wide(rows, 2 * PB), wide(MODES, nblk)],
        [pltpu.VMEM((2, tiles, 8, LANES), jnp.float32), scratch(cross, 2 * PB),
         scratch(own_pad, 2 * PB), scratch(MODES, nblk + 4 * PB), scratch(MODES, nblk + 4 * PB),
         scratch(MODES, nblk + 4 * PB), scratch(MODES, nblk + 2 * PB),
         pltpu.VMEM((4 * PB, 8, LANES), jnp.int32), vm(4 * PB, slots, LANES), vm(2 * PB, slots, LANES)],
        8, halo_a, halo_b, initial, smode, ends, push, mpart, first, m1, m2, rp, idx, wt, lead, matrices,
    )

    def share_late(k):
        if cross == own_pad:
            return send
        return jnp.concatenate([share(send[:cross], k), send[cross:]], axis=0)

    late = [lax.ppermute(share_late(k), "inst", shift(k)) for k in range(1, inst_count)]
    base = call(
        functools.partial(own_kernel, own_pad, starts), wide(own_pad, nblk), [], 2,
        first, deriv, v1, dends, scaled, c2, idx, wt, matrices,
    )
    received = [r for pair in zip(early, late) for r in pair]
    out = call(
        functools.partial(final_kernel, inst_count - 1, starts), f32(own_pad, cells),
        [vm(own_pad, cells), pltpu.SemaphoreType.DMA((nblk // 2,))], 1,
        base, matrices, *received, store=True,
    )
    return out[:own] if own_pad != own else out


def solution(mesh):
    return jax.shard_map(
        per_device,
        mesh=mesh,
        in_specs=(
            P("inst", "cell"),
            P("inst", "cell"),
            P(None, "cell"),
            P(None, "cell"),
            P("cell"),
        ),
        out_specs=P("inst", "cell"),
        check_vma=False,
    )
```
